128 devices in a mesh: ctx: 16 (over y_hi, x, core), ch: 8 (over y_lo, z).
Axes of the slice: x: 4, y: 4 (y_hi: 2, y_lo: 2; y = y_hi * 2 + y_lo), z: 4, core: 2. Of those that a mesh axis runs over, the one named last changes fastest.
Arguments:
- query_act: bfloat16 [512, 65536], P('ch', 'ctx'), may hold values from -64 to 64
- key_act: bfloat16 [512, 65536], P('ch', 'ctx'), may hold values from -6 to 6
- value_act: bfloat16 [512, 65536], P('ch', 'ctx'), may hold values from -6 to 6
- short_taps: float32 [3, 512, 3], P(None, 'ch'), may hold values from -3.5 to 3.5
- pos_proj: float32 [33, 64], replicated, may hold values from -2 to 2
- pos_phase: float32 [64], replicated, may hold values from -3.140625 to 3.140625
- mix_proj: float32 [64, 64], replicated, may hold values from -1.5 to 1.5
- mix_phase: float32 [64], replicated, may hold values from -3.140625 to 3.140625
- filter_out: float32 [64, 512], P(None, 'ch'), may hold values from -0.75 to 0.75
- decay_len: float32 [512], P('ch'), may hold values from 16 to 65536
- skip_gain: float32 [512], P('ch'), may hold values from -3 to 3
- out_gain: float32 [512], P('ch'), may hold values from 0.1 to 1.9
Outputs:
- output: bfloat16 [512, 65536], P('ch', 'ctx')
The draws below stay inside these ranges and needn't reach their ends.
All inputs are finite; a program needn't handle non-finite values.
Results may differ from the reference program's by a relative error of at most 0.014.
Values may be sent and summed in bfloat16 or wider, within the bound.
No kernel may reach another device: no remote copies, remote signals or barrier semaphores. Data moves between devices by JAX's collectives and lax.ppermute only.
A program may use at most 192 MiB of HBM per device.

```python
import math
import jax
import jax.numpy as jnp
from jax import lax

C_DEV = 64
E = 33
H = 64
C = 512
TOKENS = 65536
N_CH = 8


def draw_query_act(key, part):
    first_key, second_key = jax.random.split(jax.random.fold_in(key, 11))
    channel_pos = jnp.arange(C, dtype=jnp.int32).astype(jnp.float32) / max(C - 1, 1)
    base = jnp.clip(jax.random.normal(first_key, (C, TOKENS), jnp.float32), -6.0, 6.0)
    channel_scale = jnp.exp(0.5 * math.log(10.0) * channel_pos)
    token_scale = jnp.exp(jax.random.uniform(second_key, (TOKENS,), jnp.float32, 0.0, math.log(3.0)))
    return (base * channel_scale[:, None] * token_scale[None, :]).astype(jnp.bfloat16)


def block_levels(own_key, shape, cuts, low, top_value):
    level = 1.0
    for axis_at, blocks in cuts:
        draws = jax.random.uniform(jax.random.fold_in(jax.random.fold_in(own_key, 6), axis_at), (blocks,), jnp.float32, low / len(cuts), top_value / len(cuts))
        level = level * jnp.repeat(jnp.exp(draws), shape[axis_at] // blocks).reshape((-1,) + (1,) * (len(shape) - 1 - axis_at))
    return level


def scatter_about(key, shape, spread, limit, shards=(), kind=jnp.bfloat16):
    result = jax.random.normal(key, shape, jnp.float32) * spread
    if len(shards) > 0:
        result = block_levels(key, shape, shards, -0.22, 0.18) * result
    return jnp.clip(result, min=-limit, max=limit).astype(kind)


def setup_inputs(seed: int = 0) -> dict:
    keys = jax.random.split(jax.random.key(seed), 13)
    return {
        "query_act": draw_query_act(jax.random.fold_in(keys[12], 71), 0),
        "key_act": scatter_about(keys[1], (C, TOKENS), 1.0, 6.0, ((0, 8), (1, 16))),
        "value_act": scatter_about(keys[2], (C, TOKENS), 1.0, 6.0, ((0, 8), (1, 16))),
        "short_taps": scatter_about(keys[3], (3, C, 3), 3 ** -0.5, 3.5, ((1, 8),), jnp.float32),
        "pos_proj": scatter_about(keys[4], (E, H), (E // 4) ** -0.5, 2.0, (), jnp.float32),
        "pos_phase": jnp.clip(jax.random.uniform(keys[5], (H,), jnp.float32, -3.140625, 3.140625), -3.140625, 3.140625),
        "mix_proj": scatter_about(keys[6], (H, H), (H // 4) ** -0.5, 1.5, (), jnp.float32),
        "mix_phase": jnp.clip(jax.random.uniform(keys[7], (H,), jnp.float32, -3.140625, 3.140625), -3.140625, 3.140625),
        "filter_out": scatter_about(keys[8], (H, C), H ** -0.5, 0.75, ((1, 8),), jnp.float32),
        "decay_len": jnp.clip(jnp.exp(math.log(65536.0) - 8.317766 * jax.random.uniform(keys[9], (C,), jnp.float32) ** block_levels(keys[9], (C,), ((0, 8),), -0.2, 0.2)), 16.0, 65536.0),
        "skip_gain": scatter_about(keys[10], (C,), 0.5, 3.0, ((0, 8),), jnp.float32),
        "out_gain": jnp.clip(1.0 + 0.18 * jax.random.normal(keys[11], (C,), jnp.float32), 0.1, 1.9),
    }


HIGHEST = lax.Precision.HIGHEST
TWO_PI = 2.0 * math.pi
EPSILON = 1e-06

def short_conv(current, tail, taps):
    extended = jnp.concatenate([tail, current.astype(jnp.float32)], axis=1)
    return taps[:, 0:1] * extended[:, :-2] + taps[:, 1:2] * extended[:, 1:-1] + taps[:, 2:3] * extended[:, 2:]

def filter_taps(times, total, pos_proj, pos_phase, mix_proj, mix_phase, out_cols, decay_cols):
    bands = (pos_proj.shape[0] - 1) // 2
    freqs = 2 ** jnp.arange(bands, dtype=jnp.int32)
    phase = (freqs[:, None] * (times[None, :] // 64) % total * 64 + freqs[:, None] * (times[None, :] % 64)) % total
    angle = phase.astype(jnp.float32) * (TWO_PI / total)
    frac = times.astype(jnp.float32) / total
    features = jnp.concatenate([frac[None, :], jnp.cos(angle), jnp.sin(angle)], axis=0)
    hidden = jnp.sin(jnp.einsum('eh,em->hm', pos_proj, features, precision=HIGHEST) + pos_phase[:, None])
    hidden = jnp.sin(jnp.einsum('gh,gm->hm', mix_proj, hidden, precision=HIGHEST) + mix_phase[:, None])
    raw = jnp.einsum('hc,hm->cm', out_cols, hidden, precision=HIGHEST)
    window = jnp.exp(-times.astype(jnp.float32)[None, :] / decay_cols[:, None]) + 0.1
    return raw * window

def reference(query_act, key_act, value_act, short_taps, pos_proj, pos_phase, mix_proj, mix_phase, filter_out, decay_len, skip_gain, out_gain):
    zero_tail = jnp.zeros((C, 2), jnp.float32)
    query_short = short_conv(query_act, zero_tail, short_taps[0])
    key_short = short_conv(key_act, zero_tail, short_taps[1])
    value_short = short_conv(value_act, zero_tail, short_taps[2])
    gated = key_short * value_short
    times = jnp.arange(TOKENS, dtype=jnp.int32)
    raw = filter_taps(times, TOKENS, pos_proj, pos_phase, mix_proj, mix_phase, filter_out, decay_len)
    unit_filter = raw * lax.rsqrt(lax.optimization_barrier(jnp.sum(raw * raw, axis=1)) + EPSILON)[:, None]

    def convolve(pieces):
        data, taps = pieces
        spectrum = jnp.fft.rfft(data, n=2 * TOKENS, axis=1) * jnp.fft.rfft(taps, n=2 * TOKENS, axis=1)
        return jnp.fft.irfft(spectrum, n=2 * TOKENS, axis=1)[:, :TOKENS].astype(jnp.float32)
    mixed = lax.map(convolve, (gated.reshape(N_CH, C_DEV, TOKENS), unit_filter.reshape(N_CH, C_DEV, TOKENS)))
    mixed = mixed.reshape(C, TOKENS)
    gated_out = query_short * (mixed + skip_gain[:, None] * gated)
    scale = lax.rsqrt(lax.optimization_barrier(jnp.mean(gated_out * gated_out, axis=0)) + EPSILON)
    return (gated_out * out_gain[:, None] * scale[None, :]).astype(jnp.bfloat16)
```

```python
import math

import ml_dtypes
import numpy as np

import jax
import jax.numpy as jnp
from jax import lax
from jax.experimental import pallas as pl
from jax.experimental.pallas import tpu as pltpu
from jax.sharding import PartitionSpec as P

EPSILON = 1e-06
F32 = jnp.float32
BF16 = jnp.bfloat16
HIGHEST = lax.Precision.HIGHEST
SIDE = 256
SIN_COEFS = (
    6.2831852727319815,
    -41.34169706978675,
    81.60502464546778,
    -76.70155145963659,
    42.01616757273089,
    -14.86861627497293,
    3.1996998510441665,
)


def sin_turns(turns):
    rest = turns - jnp.floor(turns + 0.5)
    square = rest * rest
    acc = jnp.full_like(rest, SIN_COEFS[-1])
    for coef in SIN_COEFS[-2::-1]:
        acc = acc * square + coef
    return acc * rest


def split(array):
    high = array.astype(BF16)
    low = (array - high.astype(F32)).astype(BF16)
    return high, low


def dot(lhs, rhs):
    return lax.dot_general(lhs, rhs, (((1,), (0,)), ((), ())), preferred_element_type=F32)


def dot_t(lhs, rhs):
    return lax.dot_general(
        lhs, rhs, (((0,), (0,)), ((), ())), precision=HIGHEST, preferred_element_type=F32
    )


def column(row):
    size = row.shape[1]
    eye = lax.broadcasted_iota(jnp.int32, (size, size), 0) == lax.broadcasted_iota(
        jnp.int32, (size, size), 1
    )
    return jnp.sum(jnp.where(eye, jnp.broadcast_to(row, (size, size)), 0.0), axis=1, keepdims=True)


def np_split(array):
    high = array.astype(np.float32).astype(ml_dtypes.bfloat16)
    low = (array - high.astype(np.float64)).astype(np.float32).astype(ml_dtypes.bfloat16)
    return high, low


def transform_tables(side):
    total = side * side
    ids = np.arange(side)
    first = np.exp(-2j * np.pi * np.outer(ids - 0.25, ids) / side)
    twist = np.exp(-2j * np.pi * np.outer(ids - 0.25, ids) / total)
    second = np.exp(-2j * np.pi * (np.outer(ids, ids) % side) / side)
    left = np.concatenate([first.real, first.imag], axis=0)
    right = np.block([[second.real, second.imag], [-second.imag, second.real]])
    return (
        *np_split(left),
        *np_split(np.ascontiguousarray(left.T)),
        *np_split(right),
        *np_split(np.ascontiguousarray(right.T)),
        twist.real.astype(np.float32),
        twist.imag.astype(np.float32),
    )


def filter_kernel(place, pos, phase, mix, mix_phase, out_cols, decay, raw, w_one, w_two, hid, spread):
    bands = (pos.shape[0] - 1) // 2
    units = pos.shape[1]
    chans = out_cols.shape[1]
    rows = raw.shape[2]
    inv_turn = 1.0 / (2.0 * math.pi)
    w_one[...] = jnp.zeros_like(w_one)
    w_one[0 : 2 * bands, :] = pos[1 : 2 * bands + 1, :] * inv_turn
    w_one[2 * bands : 2 * bands + 1, :] = pos[0:1, :] * inv_turn
    w_one[2 * bands + 1 : 2 * bands + 2, :] = phase[...] * inv_turn
    w_two[...] = jnp.zeros_like(w_two)
    w_two[0:units, :] = mix[...] * inv_turn
    w_two[units : units + 1, :] = mix_phase[...] * inv_turn
    decay_col = column(decay[...])
    step = 1024
    total = raw.shape[0] * rows * SIDE
    for at in range(0, rows * SIDE, step):
        base = place[0] * (rows * SIDE) + at
        times = base + lax.broadcasted_iota(jnp.int32, (bands, step), 1)
        freqs = jnp.left_shift(
            jnp.ones((bands, step), jnp.int32), lax.broadcasted_iota(jnp.int32, (bands, step), 0)
        )
        turns = ((freqs * times) & (total - 1)).astype(F32) * (1.0 / total)
        time8 = (base + lax.broadcasted_iota(jnp.int32, (8, step), 1)).astype(F32)
        row8 = lax.broadcasted_iota(jnp.int32, (8, step), 0)
        extra = jnp.where(row8 == 0, time8 * (1.0 / total), jnp.where(row8 == 1, 1.0, 0.0))
        feats = jnp.concatenate([sin_turns(turns + 0.25), sin_turns(turns), extra], axis=0)
        hid[0:units, :] = sin_turns(dot_t(w_one[...], feats))
        hid[units:, :] = jnp.where(row8 == 0, 1.0, 0.0)
        hidden = sin_turns(dot_t(w_two[...], hid[...]))
        taps = dot_t(out_cols[...], hidden)
        times_c = (base + lax.broadcasted_iota(jnp.int32, (chans, step), 1)).astype(F32)
        taps = taps * (jnp.exp(-times_c / decay_col) + 0.1)
        for sub in range(0, step, 128):
            row, half = divmod((at + sub) // 128, 2)
            spread[half, pl.ds(row, chans, stride=rows), :] = taps[:, sub : sub + 128]
    for half in range(2):
        raw[:, :, :, half * 128 : half * 128 + 128] = (
            spread[half].reshape(raw.shape[:3] + (128,)).astype(BF16)
        )


def short(current, tail, taps):
    lane = lax.broadcasted_iota(jnp.int32, current.shape, 1)
    one = jnp.where(lane == 0, tail[:, 1:2], pltpu.roll(current, 1, 1))
    two = jnp.where(
        lane == 0, tail[:, 0:1], jnp.where(lane == 1, tail[:, 1:2], pltpu.roll(current, 2, 1))
    )
    return taps[:, 0:1] * two + taps[:, 1:2] * one + taps[:, 2:3] * current


def gate_kernel(key, value, key_tail, value_tail, taps, _, sent, spread):
    chans = key.shape[0]
    rows = sent.shape[2]
    gated = short(key[...].astype(F32), key_tail[...].astype(F32), taps[1]) * short(
        value[...].astype(F32), value_tail[...].astype(F32), taps[2]
    )
    for row in range(rows):
        for half in range(2):
            at = row * SIDE + half * 128
            spread[half, pl.ds(row, chans, stride=rows), :] = gated[:, at : at + 128]
    for half in range(2):
        sent[:, :, :, half * 128 : half * 128 + 128] = (
            spread[half].reshape(sent.shape[:3] + (128,)).astype(BF16)
        )


def conv_kernel(
    place, skip, data, taps, left_hi, left_lo, back_hi, back_lo, right_hi, right_lo,
    inv_hi, inv_lo, twist_re, twist_im, mixed,
):
    side = SIDE
    chan = place[0] * pl.num_programs(0) + pl.program_id(0)
    data_in = data[...].reshape(side, side)
    taps_in = taps[...].reshape(side, side)
    both = jnp.concatenate([data_in, taps_in], axis=1)
    first = dot(left_hi[...], both) + dot(left_lo[...], both)
    t_re = twist_re[...]
    t_im = twist_im[...]

    def turned(re, im):
        return jnp.concatenate([re * t_re - im * t_im, re * t_im + im * t_re], axis=1)

    stacked = jnp.concatenate(
        [turned(first[:side, :side], first[side:, :side]), turned(first[:side, side:], first[side:, side:])],
        axis=0,
    )
    hi, lo = split(stacked)
    spec = dot(hi, right_hi[...]) + dot(hi, right_lo[...]) + dot(lo, right_hi[...])
    d_re, d_im = spec[:side, :side], spec[:side, side:]
    f_re, f_im = spec[side:, :side], spec[side:, side:]
    hi, lo = split(jnp.concatenate([d_re * f_re - d_im * f_im, d_re * f_im + d_im * f_re], axis=1))
    inner = dot(hi, inv_hi[...]) + dot(hi, inv_lo[...]) + dot(lo, inv_hi[...])
    g_re, g_im = inner[:, :side], inner[:, side:]
    hi, lo = split(
        jnp.concatenate([g_re * t_re + g_im * t_im, g_im * t_re - g_re * t_im], axis=0)
    )
    values = dot(back_hi[...], hi) + dot(back_lo[...], hi) + dot(back_hi[...], lo)
    wide = taps_in.astype(F32)
    energy = jnp.sum(jnp.sum(wide * wide, axis=1, keepdims=True), axis=0, keepdims=True)
    unit = lax.rsqrt(energy + EPSILON) * (1.0 / (side * side))
    values = values * unit + skip[chan] * data_in.astype(F32)
    mixed[...] = values.astype(BF16).reshape(mixed.shape)


def out_kernel(query, query_tail, taps, mixed, gated_out, sums, spread):
    chans = query.shape[0]
    rows = mixed.shape[2]
    step = pl.program_id(0)
    for half in range(2):
        spread[half] = (
            mixed[:, :, :, half * 128 : half * 128 + 128].astype(F32).reshape(chans * rows, 128)
        )
    q_short = short(query[...].astype(F32), query_tail[...].astype(F32), taps[0])
    width = sums.shape[2]
    parts = width // SIDE

    @pl.when(step == 0)
    def _():
        sums[...] = jnp.zeros_like(sums)

    for row in range(rows):
        for half in range(2):
            at = row * SIDE + half * 128
            piece = q_short[:, at : at + 128] * spread[half, pl.ds(row, chans, stride=rows), :]
            gated_out[:, at : at + 128] = piece
            where = (row % parts) * SIDE + half * 128
            part = jnp.sum(piece * piece, axis=0, keepdims=True)
            for peer in range(sums.shape[0]):
                sums[peer, row // parts : row // parts + 1, where : where + 128] += part


def scale_kernel(gated_out, sums, gain, result):
    row = pl.program_id(0)
    energy = jnp.sum(sums[:, pl.ds(row, 1), :], axis=0)
    channels = gain.shape[1] * sums.shape[0]
    scale = lax.rsqrt(energy / channels + EPSILON)
    result[...] = (gated_out[...] * column(gain[...]) * scale).astype(BF16)


def whole(shape, memory_space=None):
    return pl.BlockSpec(shape, lambda *_: (0,) * len(shape), memory_space=memory_space)


SCALAR = pl.BlockSpec(memory_space=pltpu.SMEM)


def params(**more):
    return pltpu.CompilerParams(vmem_limit_bytes=48 * 1024 * 1024, **more)


def shards(
    query_act,
    key_act,
    value_act,
    short_taps,
    pos_proj,
    pos_phase,
    mix_proj,
    mix_phase,
    filter_out,
    decay_len,
    skip_gain,
    out_gain,
):
    chans, tokens = query_act.shape
    peers = lax.axis_size("ctx")
    groups = lax.axis_size("ch")
    place = lax.axis_index("ctx").astype(jnp.int32).reshape(1)
    own = chans // peers
    rows = tokens // SIDE
    units = pos_proj.shape[1]
    feats = (pos_proj.shape[0] - 1) // 2 * 2 + 8
    tails = lax.ppermute(
        jnp.concatenate([a[:, -2:] for a in (query_act, key_act, value_act)], axis=1),
        "ctx",
        [(i, i + 1) for i in range(peers - 1)],
    )
    q_tail, k_tail, v_tail = tails[:, 0:2], tails[:, 2:4], tails[:, 4:6]
    sent_shape = jax.ShapeDtypeStruct((peers, 2 * own, rows, SIDE), BF16)
    sent = pl.pallas_call(
        filter_kernel,
        out_shape=sent_shape,
        grid=(1,),
        in_specs=[
            SCALAR,
            whole(pos_proj.shape),
            whole((1, units)),
            whole(mix_proj.shape),
            whole((1, units)),
            whole(filter_out.shape),
            whole((1, chans)),
        ],
        out_specs=pl.BlockSpec((peers, own, rows, SIDE), lambda i: (0, 1, 0, 0)),
        scratch_shapes=[
            pltpu.VMEM((feats, units), F32),
            pltpu.VMEM((units + 8, units), F32),
            pltpu.VMEM((units + 8, 1024), F32),
            pltpu.VMEM((2, chans * rows, 128), F32),
        ],
        compiler_params=params(),
        name="filter_taps",
    )(
        place, pos_proj, pos_phase[None], mix_proj, mix_phase[None], filter_out, decay_len[None]
    )
    group = 16
    steps = chans // group
    wide = pl.BlockSpec((group, tokens), lambda i: (i, 0))
    tail_spec = pl.BlockSpec((group, 2), lambda i: (i, 0))
    taps_spec = pl.BlockSpec((3, group, 3), lambda i: (0, i, 0))
    sent = pl.pallas_call(
        gate_kernel,
        out_shape=sent_shape,
        grid=(steps,),
        in_specs=[wide, wide, tail_spec, tail_spec, taps_spec, pl.BlockSpec(memory_space=pl.ANY)],
        out_specs=pl.BlockSpec((group // own, own, rows, SIDE), lambda i: (i, 0, 0, 0)),
        scratch_shapes=[pltpu.VMEM((2, group * rows, 128), F32)],
        input_output_aliases={5: 0},
        compiler_params=params(),
        name="gate",
    )(key_act, value_act, k_tail, v_tail, short_taps, sent)
    got = lax.all_to_all(sent, "ctx", split_axis=0, concat_axis=0, tiled=True)
    tables = [jnp.asarray(t) for t in transform_tables(SIDE)]
    mixed = pl.pallas_call(
        conv_kernel,
        out_shape=jax.ShapeDtypeStruct((peers, own, rows, SIDE), BF16),
        grid=(own,),
        in_specs=[
            SCALAR,
            SCALAR,
            pl.BlockSpec((peers, 1, rows, SIDE), lambda i: (0, i, 0, 0)),
            pl.BlockSpec((peers, 1, rows, SIDE), lambda i: (0, i + own, 0, 0)),
        ]
        + [whole(t.shape) for t in tables],
        out_specs=pl.BlockSpec((peers, 1, rows, SIDE), lambda i: (0, i, 0, 0)),
        compiler_params=params(),
        name="long_conv",
    )(place, skip_gain, got, got, *tables)
    mixed = lax.all_to_all(mixed, "ctx", split_axis=0, concat_axis=0, tiled=True)
    width = tokens // 8
    gated_out, sums = pl.pallas_call(
        out_kernel,
        out_shape=(
            jax.ShapeDtypeStruct((chans, tokens), F32),
            jax.ShapeDtypeStruct((groups, 8, width), F32),
        ),
        grid=(steps,),
        in_specs=[
            wide,
            tail_spec,
            taps_spec,
            pl.BlockSpec((group // own, own, rows, SIDE), lambda i: (i, 0, 0, 0)),
        ],
        out_specs=(wide, whole((groups, 8, width))),
        scratch_shapes=[pltpu.VMEM((2, group * rows, 128), F32)],
        compiler_params=params(),
        name="gate_out",
    )(query_act, q_tail, short_taps, mixed)
    sums = lax.all_to_all(sums, "ch", split_axis=0, concat_axis=0, tiled=True)
    return pl.pallas_call(
        scale_kernel,
        out_shape=jax.ShapeDtypeStruct((chans, tokens), BF16),
        grid=(8,),
        in_specs=[
            pl.BlockSpec((chans, width), lambda i: (0, i)),
            whole((groups, 8, width)),
            whole((1, chans)),
        ],
        out_specs=pl.BlockSpec((chans, width), lambda i: (0, i)),
        compiler_params=params(),
        name="norm_out",
    )(gated_out, sums, out_gain[None])


def solution(mesh):
    return jax.shard_map(
        shards,
        mesh=mesh,
        in_specs=(
            P("ch", "ctx"),
            P("ch", "ctx"),
            P("ch", "ctx"),
            P(None, "ch", None),
            P(),
            P(),
            P(),
            P(),
            P(None, "ch"),
            P("ch"),
            P("ch"),
            P("ch"),
        ),
        out_specs=P("ch", "ctx"),
        check_vma=False,
    )
```

```python
import math

import ml_dtypes
import numpy as np

import jax
import jax.numpy as jnp
from jax import lax
from jax.experimental import pallas as pl
from jax.experimental.pallas import tpu as pltpu
from jax.sharding import PartitionSpec as P

EPSILON = 1e-06
F32 = jnp.float32
BF16 = jnp.bfloat16
SIDE = 256
GROUP = 2
SIN_COEFS = (
    6.2831852727319815,
    -41.34169706978675,
    81.60502464546778,
    -76.70155145963659,
    42.01616757273089,
    -14.86861627497293,
    3.1996998510441665,
)


def sin_turns(turns):
    rest = turns - jnp.floor(turns + 0.5)
    square = rest * rest
    acc = jnp.full_like(rest, SIN_COEFS[-1])
    for coef in SIN_COEFS[-2::-1]:
        acc = acc * square + coef
    return acc * rest


def split(array):
    high = array.astype(BF16)
    low = (array - high.astype(F32)).astype(BF16)
    return high, low


def dot(lhs, rhs):
    return lax.dot_general(lhs, rhs, (((1,), (0,)), ((), ())), preferred_element_type=F32)


def dot_t(lhs, rhs):
    return lax.dot_general(lhs, rhs, (((0,), (0,)), ((), ())), preferred_element_type=F32)


def weight_stack(weights):
    high, low = split(weights)
    return jnp.concatenate([high, high, low], axis=0)


def value_stack(values):
    high, low = split(values)
    return jnp.concatenate([high, low, high], axis=0)


def column(row):
    size = row.shape[1]
    eye = lax.broadcasted_iota(jnp.int32, (size, size), 0) == lax.broadcasted_iota(
        jnp.int32, (size, size), 1
    )
    return jnp.sum(jnp.where(eye, jnp.broadcast_to(row, (size, size)), 0.0), axis=1, keepdims=True)


def np_split(array):
    high = array.astype(np.float32).astype(ml_dtypes.bfloat16)
    low = (array - high.astype(np.float64)).astype(np.float32).astype(ml_dtypes.bfloat16)
    return high, low


def transform_tables(side):
    total = side * side
    ids = np.arange(side)
    first = np.exp(-2j * np.pi * np.outer(ids - 0.25, ids) / side)
    twist = np.exp(-2j * np.pi * np.outer(ids - 0.25, ids) / total)
    second = np.exp(-2j * np.pi * (np.outer(ids, ids) % side) / side)
    left = np.concatenate([first.real, first.imag], axis=0)
    right = np.block([[second.real, second.imag], [-second.imag, second.real]])
    return (
        *np_split(left),
        *np_split(np.ascontiguousarray(left.T)),
        np_split(right)[0],
        np_split(np.ascontiguousarray(right.T))[0],
        twist.real.astype(np.float32),
        twist.imag.astype(np.float32),
    )


def short(current, taps):
    return (
        taps[:, 0:1] * pltpu.roll(current, 2, 1)
        + taps[:, 1:2] * pltpu.roll(current, 1, 1)
        + taps[:, 2:3] * current
    )


def send_kernel(
    place, pos, phase, mix, mix_phase, out_cols, decay, taps, query_end, key_hbm, value_hbm,
    sent, key, value, w_one, spread, gate_spread, sems,
):
    bands = (pos.shape[0] - 1) // 2
    peers, slots, rows, half_side = sent.shape
    own = (slots - 1) // 4
    chans, tokens = key.shape
    total = peers * tokens
    copies = [
        pltpu.make_async_copy(key_hbm, key, sems.at[0]),
        pltpu.make_async_copy(value_hbm, value, sems.at[1]),
    ]
    for copy in copies:
        copy.start()
    inv_turn = 1.0 / (2.0 * math.pi)
    w_one[...] = jnp.zeros_like(w_one)
    w_one[0 : 2 * bands, :] = pos[1 : 2 * bands + 1, :] * inv_turn
    w_one[2 * bands : 2 * bands + 1, :] = pos[0:1, :] * inv_turn
    w_one[2 * bands + 1 : 2 * bands + 2, :] = phase[...] * inv_turn
    one_w = weight_stack(w_one[...])
    two_w = weight_stack(mix[...] * inv_turn)
    out_w = weight_stack(out_cols[...])
    two_bias = column(mix_phase[...] * inv_turn)
    decay_rate = -1.0 / column(decay[...])
    step = 1024
    for at in range(0, tokens, step):
        base = place[0] * tokens + at
        times = base + lax.broadcasted_iota(jnp.int32, (bands, step), 1)
        freqs = jnp.left_shift(
            jnp.ones((bands, step), jnp.int32), lax.broadcasted_iota(jnp.int32, (bands, step), 0)
        )
        turns = ((freqs * times) & (total - 1)).astype(F32) * (1.0 / total)
        row = lax.broadcasted_iota(jnp.int32, (bands, step), 0)
        extra = jnp.where(
            row == 0, times.astype(F32) * (1.0 / total), jnp.where(row == 1, 1.0, 0.0)
        )
        feats = jnp.concatenate([sin_turns(turns + 0.25), sin_turns(turns), extra], axis=0)
        hidden = sin_turns(dot_t(one_w, value_stack(feats)))
        hidden = sin_turns(dot_t(two_w, value_stack(hidden)) + two_bias)
        window = jnp.exp(times[0:1, :].astype(F32) * decay_rate) + 0.1
        raw = dot_t(out_w, value_stack(hidden)) * window
        for sub in range(0, step, half_side):
            row_at, half = divmod((at + sub) // half_side, 2)
            spread[half, pl.ds(row_at, chans, stride=rows), :] = raw[:, sub : sub + half_side]
    for half in range(2):
        sent[:, (2 + half) * own : (3 + half) * own] = (
            spread[half].reshape(peers, own, rows, half_side).astype(BF16)
        )
    for copy in copies:
        copy.wait()
    group = 16
    for at in range(0, chans, group):
        pick = slice(at, at + group)
        gated = short(key[pick, :].astype(F32), taps[1, pick, :]) * short(
            value[pick, :].astype(F32), taps[2, pick, :]
        )
        for sub in range(0, tokens, half_side):
            row_at, half = divmod(sub // half_side, 2)
            gate_spread[half, pl.ds(at * rows + row_at, group, stride=rows), :] = gated[
                :, sub : sub + half_side
            ]
    for half in range(2):
        sent[:, half * own : (half + 1) * own] = (
            gate_spread[half].reshape(peers, own, rows, half_side).astype(BF16)
        )
    lane = lax.broadcasted_iota(jnp.int32, (group, half_side), 1)
    ends = jnp.zeros((group, half_side), F32)
    for part in range(chans // group):
        moved = pltpu.roll(
            query_end[part * group : (part + 1) * group, :].astype(F32), 10 + 2 * part, 1
        )
        ends = jnp.where(lane // 2 == 4 + part, moved, ends)
    for part in range(chans // group):
        pick = slice(part * group, (part + 1) * group)
        key_head = key[pick, 0:half_side].astype(F32)
        value_head = pltpu.roll(value[pick, 0:half_side].astype(F32), 2, 1)
        key_end = pltpu.roll(key[pick, tokens - half_side : tokens].astype(F32), 6, 1)
        value_end = pltpu.roll(value[pick, tokens - half_side : tokens].astype(F32), 8, 1)
        edge = jnp.where(
            lane < 2,
            key_head,
            jnp.where(lane < 4, value_head, jnp.where(lane < 6, key_end, jnp.where(lane < 8, value_end, ends))),
        ).astype(BF16)
        for peer in range(part * group // own, (part + 1) * group // own):
            sent[peer, slots - 1] = edge


def terms(lhs, rhs, pairs):
    total = None
    for left, right in pairs:
        part = dot(lhs[left], rhs[right])
        total = part if total is None else total + part
    return total


def first_gated(edges, taps, chan, row):
    picked = lax.broadcasted_iota(jnp.int32, edges.shape, 1) == row
    here = jnp.sum(jnp.where(picked, edges, 0.0), axis=1, keepdims=True)
    before = jnp.concatenate([jnp.zeros_like(here[:1]), here[:-1]], axis=0)
    shorts = []
    for which in range(2):
        tap = taps[which + 1, pl.ds(chan, 1), :]
        seen = [before[:, :, 4 + 2 * which + i : 5 + 2 * which + i] for i in range(2)]
        seen += [here[:, :, 2 * which + i : 2 * which + i + 1] for i in range(2)]
        shorts.append(
            [sum(tap[:, i : i + 1] * seen[at + i] for i in range(3)) for at in range(2)]
        )
    return shorts[0][0] * shorts[1][0], shorts[0][1] * shorts[1][1]


def conv_kernel(
    place, skip, got, taps, left_hi, left_lo, back_hi, back_lo, right_hi, inv_hi,
    twist_re, twist_im, mixed,
):
    side = SIDE
    peers, slots, rows, half_side = got.shape
    own = (slots - 1) // 4
    edges = got[:, slots - 1].astype(F32)
    t_re = twist_re[...]
    t_im = twist_im[...]
    left = (left_hi[...], left_lo[...])
    back = (back_hi[...], back_lo[...])
    spot_row = lax.broadcasted_iota(jnp.int32, (peers, rows, half_side), 1)
    spot_lane = lax.broadcasted_iota(jnp.int32, (peers, rows, half_side), 2)
    group = GROUP
    for at in range(0, own, group):
        data, filt = [], []
        for slot in range(at, at + group):
            chan = place[0] * own + slot
            zero, one = first_gated(edges, taps, chan, lax.rem(chan, rows))
            head = got[:, slot].astype(F32)
            head = jnp.where((spot_row == 0) & (spot_lane == 0), zero, head)
            head = jnp.where((spot_row == 0) & (spot_lane == 1), one, head).astype(BF16)
            data.append(
                jnp.concatenate(
                    [head.reshape(side, half_side), got[:, own + slot].reshape(side, half_side)],
                    axis=1,
                )
            )
            filt.append(
                jnp.concatenate(
                    [got[:, (2 + half) * own + slot].reshape(side, half_side) for half in range(2)],
                    axis=1,
                )
            )
        first = terms(left, (jnp.concatenate(data + filt, axis=1),), ((0, 0), (1, 0)))
        turned = []
        for at_col in range(0, 2 * group * side, side):
            re, im = first[:side, at_col : at_col + side], first[side:, at_col : at_col + side]
            turned.append(
                jnp.concatenate([re * t_re - im * t_im, re * t_im + im * t_re], axis=1).astype(BF16)
            )
        spec = dot(jnp.concatenate(turned, axis=0), right_hi[...])
        edge_row = group * side
        d_re, d_im = spec[:edge_row, :side], spec[:edge_row, side:]
        f_re, f_im = spec[edge_row:, :side], spec[edge_row:, side:]
        product = jnp.concatenate([d_re * f_re - d_im * f_im, d_re * f_im + d_im * f_re], axis=1)
        inner = dot(product.astype(BF16), inv_hi[...])
        turned = []
        for at_row in range(0, group * side, side):
            re, im = inner[at_row : at_row + side, :side], inner[at_row : at_row + side, side:]
            turned.append(jnp.concatenate([re * t_re + im * t_im, im * t_re - re * t_im], axis=0))
        values = terms(back, split(jnp.concatenate(turned, axis=1)), ((0, 0), (1, 0), (0, 1)))
        for index in range(group):
            wide = filt[index].astype(F32)
            energy = jnp.sum(jnp.sum(wide * wide, axis=1, keepdims=True), axis=0, keepdims=True)
            unit = lax.rsqrt(energy + EPSILON) * (1.0 / (side * side))
            skipped = skip[place[0] * own + at + index] * data[index].astype(F32)
            result = values[:, index * side : (index + 1) * side] * unit + skipped
            mixed[:, at + index] = result.astype(BF16).reshape(peers, rows, side)


def query_kernel(place, query, taps, got, q_short):
    slots = got.shape[1]
    before = jnp.maximum(place[0] - 1, 0)
    tails = got[before, slots - 1].astype(F32)
    tails = jnp.where(jnp.broadcast_to(place[0], tails.shape) > 0, tails, 0.0)
    group = tails.shape[0]
    for part in range(query.shape[0] // group):
        pick = slice(part * group, (part + 1) * group)
        tap = taps[0, pick, :]
        current = query[pick, :].astype(F32)
        q_short[pick, :] = short(current, tap)
        two, one = tails[:, 8 + 2 * part : 9 + 2 * part], tails[:, 9 + 2 * part : 10 + 2 * part]
        q_short[pick, 0:1] = tap[:, 0:1] * two + tap[:, 1:2] * one + tap[:, 2:3] * current[:, 0:1]
        q_short[pick, 1:2] = (
            tap[:, 0:1] * one + tap[:, 1:2] * current[:, 0:1] + tap[:, 2:3] * current[:, 1:2]
        )


def out_kernel(q_short, mixed, gain, gated_out, sums, spread, total):
    peers, own, rows, side = mixed.shape
    chans = peers * own
    half_side = side // 2
    gains = column(gain[...])
    for half in range(2):
        spread[half] = (
            mixed[:, :, :, half * half_side : (half + 1) * half_side]
            .astype(F32)
            .reshape(chans * rows, half_side)
        )
    for at in range(0, q_short.shape[1], half_side):
        row, half = divmod(at // half_side, 2)
        piece = q_short[:, at : at + half_side] * spread[half, pl.ds(row, chans, stride=rows), :]
        gated_out[:, at : at + half_side] = piece * gains
        sum_row, lane = divmod(at, sums.shape[2])
        total[sum_row : sum_row + 1, lane : lane + half_side] = jnp.sum(
            piece * piece, axis=0, keepdims=True
        )
    for peer in range(sums.shape[0]):
        sums[peer] = total[...]


def scale_kernel(gated_out, sums, result):
    width = sums.shape[2]
    energy = jnp.sum(sums[...], axis=0)
    channels = gated_out.shape[0] * pl.num_programs(0) * sums.shape[0]
    scale = lax.rsqrt(energy / channels + EPSILON)
    for row in range(sums.shape[1]):
        at = row * width
        result[:, at : at + width] = (
            gated_out[:, at : at + width] * scale[row : row + 1, :]
        ).astype(BF16)


def whole(shape, memory_space=None):
    return pl.BlockSpec(shape, lambda *_: (0,) * len(shape), memory_space=memory_space)


SCALAR = pl.BlockSpec(memory_space=pltpu.SMEM)
VECTOR = pl.BlockSpec(memory_space=pltpu.VMEM)
OUTSIDE = pl.BlockSpec(memory_space=pl.ANY)


def params(**more):
    return pltpu.CompilerParams(vmem_limit_bytes=32 * 1024 * 1024, **more)


def shards(
    query_act,
    key_act,
    value_act,
    short_taps,
    pos_proj,
    pos_phase,
    mix_proj,
    mix_phase,
    filter_out,
    decay_len,
    skip_gain,
    out_gain,
):
    chans, tokens = query_act.shape
    peers = lax.axis_size("ctx")
    groups = lax.axis_size("ch")
    place = lax.axis_index("ctx").astype(jnp.int32).reshape(1)
    own = chans // peers
    rows = tokens // SIDE
    units = pos_proj.shape[1]
    half_side = SIDE // 2
    spread = pltpu.VMEM((2, chans * rows, half_side), F32)
    sent = pl.pallas_call(
        send_kernel,
        out_shape=jax.ShapeDtypeStruct((peers, 4 * own + 1, rows, half_side), BF16),
        in_specs=[SCALAR] + [VECTOR] * 8 + [OUTSIDE] * 2,
        out_specs=VECTOR,
        scratch_shapes=[
            pltpu.VMEM((chans, tokens), BF16),
            pltpu.VMEM((chans, tokens), BF16),
            pltpu.VMEM(((pos_proj.shape[0] - 1) // 2 * 3, units), F32),
            spread,
            spread,
            pltpu.SemaphoreType.DMA((2,)),
        ],
        compiler_params=params(),
        name="send",
    )(
        place,
        pos_proj,
        pos_phase[None],
        mix_proj,
        mix_phase[None],
        filter_out,
        decay_len[None],
        short_taps,
        query_act[:, -half_side:],
        key_act,
        value_act,
    )
    got = lax.all_to_all(sent, "ctx", split_axis=0, concat_axis=0, tiled=True)
    tables = [jnp.asarray(t) for t in transform_tables(SIDE)]
    mixed = pl.pallas_call(
        conv_kernel,
        out_shape=jax.ShapeDtypeStruct((peers, own, rows, SIDE), BF16),
        in_specs=[SCALAR, SCALAR] + [VECTOR] * (2 + len(tables)),
        out_specs=VECTOR,
        compiler_params=params(),
        name="long_conv",
    )(place, skip_gain, got, short_taps, *tables)
    mixed = lax.all_to_all(mixed, "ctx", split_axis=0, concat_axis=0, tiled=True)
    q_short = pl.pallas_call(
        query_kernel,
        out_shape=jax.ShapeDtypeStruct((chans, tokens), F32),
        in_specs=[SCALAR] + [VECTOR] * 3,
        out_specs=VECTOR,
        compiler_params=params(),
        name="query_short",
    )(place, query_act, short_taps, got)
    width = tokens // 8
    gated_out, sums = pl.pallas_call(
        out_kernel,
        out_shape=(
            jax.ShapeDtypeStruct((chans, tokens), F32),
            jax.ShapeDtypeStruct((groups, 8, width), F32),
        ),
        in_specs=[VECTOR] * 3,
        out_specs=(VECTOR, VECTOR),
        scratch_shapes=[spread, pltpu.VMEM((8, width), F32)],
        compiler_params=params(),
        name="gate_out",
    )(q_short, mixed, out_gain[None])
    sums = lax.all_to_all(sums, "ch", split_axis=0, concat_axis=0, tiled=True)
    group = 16
    wide = pl.BlockSpec((group, tokens), lambda i: (i, 0))
    return pl.pallas_call(
        scale_kernel,
        out_shape=jax.ShapeDtypeStruct((chans, tokens), BF16),
        grid=(chans // group,),
        in_specs=[wide, whole((groups, 8, width))],
        out_specs=wide,
        compiler_params=params(),
        name="norm_out",
    )(gated_out, sums)


def solution(mesh):
    return jax.shard_map(
        shards,
        mesh=mesh,
        in_specs=(
            P("ch", "ctx"),
            P("ch", "ctx"),
            P("ch", "ctx"),
            P(None, "ch", None),
            P(),
            P(),
            P(),
            P(),
            P(None, "ch"),
            P("ch"),
            P("ch"),
            P("ch"),
        ),
        out_specs=P("ch", "ctx"),
        check_vma=False,
    )
```

```python
import math

import ml_dtypes
import numpy as np

import jax
import jax.numpy as jnp
from jax import lax
from jax.experimental import pallas as pl
from jax.experimental.pallas import tpu as pltpu
from jax.sharding import PartitionSpec as P

EPSILON = 1e-06
F32 = jnp.float32
BF16 = jnp.bfloat16
SIDE = 256
GROUP = 2
SIN_COEFS = (
    6.283182819148623,
    -41.341421436010776,
    81.59618459694858,
    -76.58010652932292,
    41.205417211473964,
    -12.271293082622988,
)


def sin_turns(turns):
    rest = turns - jnp.floor(turns + 0.5)
    square = rest * rest
    acc = jnp.full_like(rest, SIN_COEFS[-1])
    for coef in SIN_COEFS[-2::-1]:
        acc = acc * square + coef
    return acc * rest


def split(array):
    high = array.astype(BF16)
    low = (array - high.astype(F32)).astype(BF16)
    return high, low


def dot(lhs, rhs):
    return lax.dot_general(lhs, rhs, (((1,), (0,)), ((), ())), preferred_element_type=F32)


def dot_t(lhs, rhs):
    return lax.dot_general(lhs, rhs, (((0,), (0,)), ((), ())), preferred_element_type=F32)


def weight_stack(weights):
    high, low = split(weights)
    return jnp.concatenate([high, high, low], axis=0)


def value_stack(values):
    high, low = split(values)
    return jnp.concatenate([high, low, high], axis=0)


def column(row):
    size = row.shape[1]
    eye = lax.broadcasted_iota(jnp.int32, (size, size), 0) == lax.broadcasted_iota(
        jnp.int32, (size, size), 1
    )
    return jnp.sum(jnp.where(eye, jnp.broadcast_to(row, (size, size)), 0.0), axis=1, keepdims=True)


def np_split(array):
    high = array.astype(np.float32).astype(ml_dtypes.bfloat16)
    low = (array - high.astype(np.float64)).astype(np.float32).astype(ml_dtypes.bfloat16)
    return high, low


def stacked(array):
    high, low = np_split(array)
    return np.concatenate([high, low], axis=1)


def transform_tables(side):
    total = side * side
    ids = np.arange(side)
    first = np.exp(-2j * np.pi * np.outer(ids - 0.25, ids) / side)
    twist = np.exp(-2j * np.pi * np.outer(ids - 0.25, ids) / total)
    second = np.exp(-2j * np.pi * (np.outer(ids, ids) % side) / side)
    left = np.concatenate([first.real, first.imag], axis=0)
    right = np.block([[second.real, second.imag], [-second.imag, second.real]])
    return (
        stacked(left),
        np.concatenate([stacked(left.T), np_split(left.T)[0]], axis=1),
        np_split(right)[0],
        np_split(np.ascontiguousarray(right.T))[0],
        twist.real.astype(np.float32),
        twist.imag.astype(np.float32),
    )


def short(current, taps):
    return (
        taps[0] * pltpu.roll(current, 2, 1)
        + taps[1] * pltpu.roll(current, 1, 1)
        + taps[2] * current
    )


def send_kernel(
    place, pos_hbm, phase_hbm, mix_hbm, mix_phase_hbm, out_hbm, decay_hbm, taps_hbm, query_hbm,
    key_hbm, value_hbm, sent, pos, phase, mix, mix_phase, out_cols, decay, taps, query_end, key,
    value, w_one, spread, gate_spread, sems,
):
    bands = (pos.shape[0] - 1) // 2
    peers, slots, rows, half_side = sent.shape
    own = (slots - 1) // 4
    chans, tokens = key.shape
    total = peers * tokens
    pairs = [
        (pos_hbm, pos),
        (phase_hbm, phase),
        (mix_hbm, mix),
        (mix_phase_hbm, mix_phase),
        (out_hbm, out_cols),
        (decay_hbm, decay),
        (taps_hbm, taps),
        (query_hbm.at[:, tokens - half_side : tokens], query_end),
        (key_hbm, key),
        (value_hbm, value),
    ]
    copies = [
        pltpu.make_async_copy(source, target, sems.at[at])
        for at, (source, target) in enumerate(pairs)
    ]
    for copy in copies:
        copy.start()
    for copy in copies[:6]:
        copy.wait()
    inv_turn = 1.0 / (2.0 * math.pi)
    w_one[...] = jnp.zeros_like(w_one)
    w_one[0 : 2 * bands, :] = pos[1 : 2 * bands + 1, :] * inv_turn
    w_one[2 * bands : 2 * bands + 1, :] = pos[0:1, :] * inv_turn
    w_one[2 * bands + 1 : 2 * bands + 2, :] = phase[...] * inv_turn
    one_w = weight_stack(w_one[...])
    two_w = weight_stack(mix[...] * inv_turn)
    out_w = weight_stack(out_cols[...])
    two_bias = column(mix_phase[...] * inv_turn)
    decay_rate = -1.0 / column(decay[...])
    fine = jnp.exp(
        lax.broadcasted_iota(jnp.int32, (1, half_side), 1).astype(F32) * decay_rate
    )
    step = 1024
    for at in range(0, tokens, step):
        base = place[0] * tokens + at
        times = base + lax.broadcasted_iota(jnp.int32, (bands, step), 1)
        freqs = jnp.left_shift(
            jnp.ones((bands, step), jnp.int32), lax.broadcasted_iota(jnp.int32, (bands, step), 0)
        )
        turns = ((freqs * times) & (total - 1)).astype(F32) * (1.0 / total)
        row = lax.broadcasted_iota(jnp.int32, (bands, step), 0)
        extra = jnp.where(
            row == 0, times.astype(F32) * (1.0 / total), jnp.where(row == 1, 1.0, 0.0)
        )
        feats = jnp.concatenate([sin_turns(turns + 0.25), sin_turns(turns), extra], axis=0)
        hidden = sin_turns(dot_t(one_w, value_stack(feats)))
        hidden = sin_turns(dot_t(two_w, value_stack(hidden)) + two_bias)
        raw = dot_t(out_w, value_stack(hidden))
        for sub in range(0, step, half_side):
            row_at, half = divmod((at + sub) // half_side, 2)
            coarse = jnp.exp((base + sub).astype(F32) * decay_rate)
            spread[half, pl.ds(row_at, chans, stride=rows), :] = raw[
                :, sub : sub + half_side
            ] * (coarse * fine + 0.1)
    for half in range(2):
        sent[:, (2 + half) * own : (3 + half) * own] = (
            spread[half].reshape(peers, own, rows, half_side).astype(BF16)
        )
    for copy in copies[6:]:
        copy.wait()
    columns = [[column(taps[which, i : i + 1, :]) for i in range(3)] for which in (1, 2)]
    group = 16
    for at in range(0, chans, group):
        pick = slice(at, at + group)
        gated = short(key[pick, :].astype(F32), [tap[pick, :] for tap in columns[0]]) * short(
            value[pick, :].astype(F32), [tap[pick, :] for tap in columns[1]]
        )
        for sub in range(0, tokens, half_side):
            row_at, half = divmod(sub // half_side, 2)
            gate_spread[half, pl.ds(at * rows + row_at, group, stride=rows), :] = gated[
                :, sub : sub + half_side
            ]
    for half in range(2):
        sent[:, half * own : (half + 1) * own] = (
            gate_spread[half].reshape(peers, own, rows, half_side).astype(BF16)
        )
    lane = lax.broadcasted_iota(jnp.int32, (group, half_side), 1)
    ends = jnp.zeros((group, half_side), F32)
    for part in range(chans // group):
        moved = pltpu.roll(
            query_end[part * group : (part + 1) * group, :].astype(F32), 10 + 2 * part, 1
        )
        ends = jnp.where(lane // 2 == 4 + part, moved, ends)
    for part in range(chans // group):
        pick = slice(part * group, (part + 1) * group)
        key_head = key[pick, 0:half_side].astype(F32)
        value_head = pltpu.roll(value[pick, 0:half_side].astype(F32), 2, 1)
        key_end = pltpu.roll(key[pick, tokens - half_side : tokens].astype(F32), 6, 1)
        value_end = pltpu.roll(value[pick, tokens - half_side : tokens].astype(F32), 8, 1)
        edge = jnp.where(
            lane < 2,
            key_head,
            jnp.where(lane < 4, value_head, jnp.where(lane < 6, key_end, jnp.where(lane < 8, value_end, ends))),
        ).astype(BF16)
        for peer in range(part * group // own, (part + 1) * group // own):
            sent[peer, slots - 1] = edge


def first_gated(edges, taps, local):
    row = lax.rem(local, edges.shape[1])
    picked = lax.broadcasted_iota(jnp.int32, edges.shape, 1) == row
    here = jnp.sum(jnp.where(picked, edges, 0.0), axis=1, keepdims=True)
    before = jnp.concatenate([jnp.zeros_like(here[:1]), here[:-1]], axis=0)
    shorts = []
    for which in range(2):
        row = taps[which + 1]
        lane = lax.broadcasted_iota(jnp.int32, row.shape, 1)
        tap = jnp.sum(jnp.where(lane == local, row, 0.0), axis=1, keepdims=True)
        seen = [before[:, :, 4 + 2 * which + i : 5 + 2 * which + i] for i in range(2)]
        seen += [here[:, :, 2 * which + i : 2 * which + i + 1] for i in range(2)]
        shorts.append(
            [sum(tap[i : i + 1, :] * seen[at + i] for i in range(3)) for at in range(2)]
        )
    return shorts[0][0] * shorts[1][0], shorts[0][1] * shorts[1][1]


def conv_kernel(
    place, skip, got, taps, left, back, right_hi, inv_hi,
    twist_re, twist_im, mixed,
):
    side = SIDE
    peers, slots, rows, half_side = got.shape
    own = (slots - 1) // 4
    edges = got[:, slots - 1].astype(F32)
    t_re = twist_re[...]
    t_im = twist_im[...]
    spot_row = lax.broadcasted_iota(jnp.int32, (peers, rows, half_side), 1)
    spot_lane = lax.broadcasted_iota(jnp.int32, (peers, rows, half_side), 2)
    group = GROUP
    for at in range(0, own, group):
        data, filt = [], []
        for slot in range(at, at + group):
            chan = place[0] * own + slot
            zero, one = first_gated(edges, taps, chan)
            head = got[:, slot].astype(F32)
            head = jnp.where((spot_row == 0) & (spot_lane == 0), zero, head)
            head = jnp.where((spot_row == 0) & (spot_lane == 1), one, head).astype(BF16)
            data.append(
                jnp.concatenate(
                    [head.reshape(side, half_side), got[:, own + slot].reshape(side, half_side)],
                    axis=1,
                )
            )
            filt.append(
                jnp.concatenate(
                    [got[:, (2 + half) * own + slot].reshape(side, half_side) for half in range(2)],
                    axis=1,
                )
            )
        both = jnp.concatenate(data + filt, axis=1)
        first = dot(left[...], jnp.concatenate([both, both], axis=0))
        turned = []
        for at_col in range(0, 2 * group * side, side):
            re, im = first[:side, at_col : at_col + side], first[side:, at_col : at_col + side]
            turned.append(
                jnp.concatenate([re * t_re - im * t_im, re * t_im + im * t_re], axis=1).astype(BF16)
            )
        spec = dot(jnp.concatenate(turned, axis=0), right_hi[...])
        edge_row = group * side
        d_re, d_im = spec[:edge_row, :side], spec[:edge_row, side:]
        f_re, f_im = spec[edge_row:, :side], spec[edge_row:, side:]
        product = jnp.concatenate([d_re * f_re - d_im * f_im, d_re * f_im + d_im * f_re], axis=1)
        inner = dot(product.astype(BF16), inv_hi[...])
        turned = []
        for at_row in range(0, group * side, side):
            re, im = inner[at_row : at_row + side, :side], inner[at_row : at_row + side, side:]
            turned.append(jnp.concatenate([re * t_re + im * t_im, im * t_re - re * t_im], axis=0))
        high, low = split(jnp.concatenate(turned, axis=1))
        values = dot(back[...], jnp.concatenate([high, high, low], axis=0))
        for index in range(group):
            wide = filt[index].astype(F32)
            energy = jnp.sum(jnp.sum(wide * wide, axis=1, keepdims=True), axis=0, keepdims=True)
            unit = lax.rsqrt(energy + EPSILON) * (1.0 / (side * side))
            skipped = skip[place[0] * own + at + index] * data[index].astype(F32)
            result = values[:, index * side : (index + 1) * side] * unit + skipped
            mixed[:, at + index] = result.astype(BF16).reshape(peers, rows, side)


def query_kernel(place, query, taps, got, q_short):
    slots = got.shape[1]
    before = jnp.maximum(place[0] - 1, 0)
    tails = got[before, slots - 1].astype(F32)
    tails = jnp.where(jnp.broadcast_to(place[0], tails.shape) > 0, tails, 0.0)
    group = tails.shape[0]
    columns = [column(taps[0, i : i + 1, :]) for i in range(3)]
    for part in range(query.shape[0] // group):
        pick = slice(part * group, (part + 1) * group)
        tap = [each[pick, :] for each in columns]
        current = query[pick, :].astype(F32)
        q_short[pick, :] = short(current, tap)
        two, one = tails[:, 8 + 2 * part : 9 + 2 * part], tails[:, 9 + 2 * part : 10 + 2 * part]
        q_short[pick, 0:1] = tap[0] * two + tap[1] * one + tap[2] * current[:, 0:1]
        q_short[pick, 1:2] = (
            tap[0] * one + tap[1] * current[:, 0:1] + tap[2] * current[:, 1:2]
        )


def out_kernel(q_short, mixed, gain, gated_out, sums, spread, total):
    peers, own, rows, side = mixed.shape
    chans = peers * own
    half_side = side // 2
    gains = column(gain[...])
    for half in range(2):
        spread[half] = (
            mixed[:, :, :, half * half_side : (half + 1) * half_side]
            .astype(F32)
            .reshape(chans * rows, half_side)
        )
    for at in range(0, q_short.shape[1], half_side):
        row, half = divmod(at // half_side, 2)
        piece = q_short[:, at : at + half_side] * spread[half, pl.ds(row, chans, stride=rows), :]
        gated_out[:, at : at + half_side] = piece * gains
        sum_row, lane = divmod(at, sums.shape[2])
        total[sum_row : sum_row + 1, lane : lane + half_side] = jnp.sum(
            piece * piece, axis=0, keepdims=True
        )
    for peer in range(sums.shape[0]):
        sums[peer] = total[...]


def scale_kernel(gated_out, sums, result):
    width = sums.shape[2]
    energy = jnp.sum(sums[...], axis=0)
    channels = gated_out.shape[0] * pl.num_programs(0) * sums.shape[0]
    scale = lax.rsqrt(energy / channels + EPSILON)
    for row in range(sums.shape[1]):
        at = row * width
        result[:, at : at + width] = (
            gated_out[:, at : at + width] * scale[row : row + 1, :]
        ).astype(BF16)


def whole(shape, memory_space=None):
    return pl.BlockSpec(shape, lambda *_: (0,) * len(shape), memory_space=memory_space)


SCALAR = pl.BlockSpec(memory_space=pltpu.SMEM)
VECTOR = pl.BlockSpec(memory_space=pltpu.VMEM)
OUTSIDE = pl.BlockSpec(memory_space=pltpu.HBM)


def in_hbm(array):
    return pltpu.with_memory_space_constraint(array, pltpu.HBM)


def params(**more):
    return pltpu.CompilerParams(vmem_limit_bytes=32 * 1024 * 1024, **more)


def shards(
    query_act,
    key_act,
    value_act,
    short_taps,
    pos_proj,
    pos_phase,
    mix_proj,
    mix_phase,
    filter_out,
    decay_len,
    skip_gain,
    out_gain,
):
    chans, tokens = query_act.shape
    peers = lax.axis_size("ctx")
    groups = lax.axis_size("ch")
    place = lax.axis_index("ctx").astype(jnp.int32).reshape(1)
    own = chans // peers
    rows = tokens // SIDE
    units = pos_proj.shape[1]
    half_side = SIDE // 2
    taps = jnp.transpose(short_taps, (0, 2, 1))
    spread = pltpu.VMEM((2, chans * rows, half_side), F32)
    sent = pl.pallas_call(
        send_kernel,
        out_shape=jax.ShapeDtypeStruct((peers, 4 * own + 1, rows, half_side), BF16),
        in_specs=[SCALAR] + [OUTSIDE] * 10,
        out_specs=VECTOR,
        scratch_shapes=[
            pltpu.VMEM(pos_proj.shape, F32),
            pltpu.VMEM((1, units), F32),
            pltpu.VMEM(mix_proj.shape, F32),
            pltpu.VMEM((1, units), F32),
            pltpu.VMEM(filter_out.shape, F32),
            pltpu.VMEM((1, chans), F32),
            pltpu.VMEM(taps.shape, F32),
            pltpu.VMEM((chans, half_side), BF16),
            pltpu.VMEM((chans, tokens), BF16),
            pltpu.VMEM((chans, tokens), BF16),
            pltpu.VMEM(((pos_proj.shape[0] - 1) // 2 * 3, units), F32),
            spread,
            spread,
            pltpu.SemaphoreType.DMA((10,)),
        ],
        compiler_params=params(),
        name="send",
    )(
        place,
        *map(
            in_hbm,
            (
                pos_proj,
                pos_phase[None],
                mix_proj,
                mix_phase[None],
                filter_out,
                decay_len[None],
                taps,
                query_act,
                key_act,
                value_act,
            ),
        ),
    )
    got = lax.all_to_all(sent, "ctx", split_axis=0, concat_axis=0, tiled=True)
    tables = [jnp.asarray(t) for t in transform_tables(SIDE)]
    mixed = pl.pallas_call(
        conv_kernel,
        out_shape=jax.ShapeDtypeStruct((peers, own, rows, SIDE), BF16),
        in_specs=[SCALAR, SCALAR] + [VECTOR] * (2 + len(tables)),
        out_specs=VECTOR,
        compiler_params=params(),
        name="long_conv",
    )(place, skip_gain, got, taps, *tables)
    mixed = lax.all_to_all(mixed, "ctx", split_axis=0, concat_axis=0, tiled=True)
    q_short = pl.pallas_call(
        query_kernel,
        out_shape=jax.ShapeDtypeStruct((chans, tokens), F32),
        in_specs=[SCALAR] + [VECTOR] * 3,
        out_specs=VECTOR,
        compiler_params=params(),
        name="query_short",
    )(place, query_act, taps, got)
    width = tokens // 8
    gated_out, sums = pl.pallas_call(
        out_kernel,
        out_shape=(
            jax.ShapeDtypeStruct((chans, tokens), F32),
            jax.ShapeDtypeStruct((groups, 8, width), F32),
        ),
        in_specs=[VECTOR] * 3,
        out_specs=(VECTOR, VECTOR),
        scratch_shapes=[spread, pltpu.VMEM((8, width), F32)],
        compiler_params=params(),
        name="gate_out",
    )(q_short, mixed, out_gain[None])
    sums = lax.all_to_all(sums, "ch", split_axis=0, concat_axis=0, tiled=True)
    group = 16
    wide = pl.BlockSpec((group, tokens), lambda i: (i, 0))
    return pl.pallas_call(
        scale_kernel,
        out_shape=jax.ShapeDtypeStruct((chans, tokens), BF16),
        grid=(chans // group,),
        in_specs=[wide, whole((groups, 8, width))],
        out_specs=wide,
        compiler_params=params(),
        name="norm_out",
    )(gated_out, sums)


def solution(mesh):
    return jax.shard_map(
        shards,
        mesh=mesh,
        in_specs=(
            P("ch", "ctx"),
            P("ch", "ctx"),
            P("ch", "ctx"),
            P(None, "ch", None),
            P(),
            P(),
            P(),
            P(),
            P(None, "ch"),
            P("ch"),
            P("ch"),
            P("ch"),
        ),
        out_specs=P("ch", "ctx"),
        check_vma=False,
    )
```

```python
import math

import ml_dtypes
import numpy as np

import jax
import jax.numpy as jnp
from jax import lax
from jax.experimental import pallas as pl
from jax.experimental.pallas import tpu as pltpu
from jax.sharding import PartitionSpec as P

EPSILON = 1e-06
F32 = jnp.float32
BF16 = jnp.bfloat16
SIDE = 256
GROUP = 2
SIN_COEFS = (
    6.283182819148623,
    -41.341421436010776,
    81.59618459694858,
    -76.58010652932292,
    41.205417211473964,
    -12.271293082622988,
)


def sin_turns(turns):
    rest = turns - jnp.floor(turns + 0.5)
    square = rest * rest
    acc = jnp.full_like(rest, SIN_COEFS[-1])
    for coef in SIN_COEFS[-2::-1]:
        acc = acc * square + coef
    return acc * rest


def split(array):
    high = array.astype(BF16)
    low = (array - high.astype(F32)).astype(BF16)
    return high, low


def dot(lhs, rhs):
    return lax.dot_general(lhs, rhs, (((1,), (0,)), ((), ())), preferred_element_type=F32)


def dot_t(lhs, rhs):
    return lax.dot_general(lhs, rhs, (((0,), (0,)), ((), ())), preferred_element_type=F32)


def weight_stack(weights):
    high, low = split(weights)
    return jnp.concatenate([high, high, low], axis=0)


def value_stack(values):
    high, low = split(values)
    return jnp.concatenate([high, low, high], axis=0)


def column(row):
    size = row.shape[1]
    eye = lax.broadcasted_iota(jnp.int32, (size, size), 0) == lax.broadcasted_iota(
        jnp.int32, (size, size), 1
    )
    return jnp.sum(jnp.where(eye, jnp.broadcast_to(row, (size, size)), 0.0), axis=1, keepdims=True)


def np_split(array):
    high = array.astype(np.float32).astype(ml_dtypes.bfloat16)
    low = (array - high.astype(np.float64)).astype(np.float32).astype(ml_dtypes.bfloat16)
    return high, low


def stacked(array):
    high, low = np_split(array)
    return np.concatenate([high, low], axis=1)


def transform_tables(side):
    total = side * side
    ids = np.arange(side)
    first = np.exp(-2j * np.pi * np.outer(ids - 0.25, ids) / side)
    twist = np.exp(-2j * np.pi * np.outer(ids - 0.25, ids) / total)
    second = np.exp(-2j * np.pi * (np.outer(ids, ids) % side) / side)
    left = np.concatenate([first.real, first.imag], axis=0)
    right = np.block([[second.real, second.imag], [-second.imag, second.real]])
    return (
        stacked(left),
        np.concatenate([stacked(left.T), np_split(left.T)[0]], axis=1),
        np_split(right)[0],
        np_split(np.ascontiguousarray(right.T))[0],
        twist.real.astype(np.float32),
        twist.imag.astype(np.float32),
    )


def short(current, taps):
    return (
        taps[0] * pltpu.roll(current, 2, 1)
        + taps[1] * pltpu.roll(current, 1, 1)
        + taps[2] * current
    )


def send_kernel(
    place, pos_hbm, phase_hbm, mix_hbm, mix_phase_hbm, out_hbm, decay_hbm, taps_hbm, query_hbm,
    key_hbm, value_hbm, sent, pos, phase, mix, mix_phase, out_cols, decay, taps, query_end, key,
    value, w_one, feats, spread, gate_spread, sems,
):
    bands = (pos.shape[0] - 1) // 2
    peers, slots, rows, half_side = sent.shape
    own = (slots - 1) // 4
    chans, tokens = key.shape
    total = peers * tokens
    pairs = [
        (pos_hbm, pos),
        (phase_hbm, phase),
        (mix_hbm, mix),
        (mix_phase_hbm, mix_phase),
        (out_hbm, out_cols),
        (decay_hbm, decay),
        (taps_hbm, taps),
        (query_hbm.at[:, tokens - half_side : tokens], query_end),
        (key_hbm, key),
        (value_hbm, value),
    ]
    copies = [
        pltpu.make_async_copy(source, target, sems.at[at])
        for at, (source, target) in enumerate(pairs)
    ]
    for copy in copies:
        copy.start()
    step = 2048
    for at in range(0, tokens, step):
        base = place[0] * tokens + at
        times = base + lax.broadcasted_iota(jnp.int32, (bands, step), 1)
        freqs = jnp.left_shift(
            jnp.ones((bands, step), jnp.int32), lax.broadcasted_iota(jnp.int32, (bands, step), 0)
        )
        turns = ((freqs * times) & (total - 1)).astype(F32) * (1.0 / total)
        row = lax.broadcasted_iota(jnp.int32, (bands, step), 0)
        extra = jnp.where(
            row == 0, times.astype(F32) * (1.0 / total), jnp.where(row == 1, 1.0, 0.0)
        )
        feats[:, at : at + step] = value_stack(
            jnp.concatenate([sin_turns(turns + 0.25), sin_turns(turns), extra], axis=0)
        )
    for copy in copies[:6]:
        copy.wait()
    inv_turn = 1.0 / (2.0 * math.pi)
    w_one[...] = jnp.zeros_like(w_one)
    w_one[0 : 2 * bands, :] = pos[1 : 2 * bands + 1, :] * inv_turn
    w_one[2 * bands : 2 * bands + 1, :] = pos[0:1, :] * inv_turn
    w_one[2 * bands + 1 : 2 * bands + 2, :] = phase[...] * inv_turn
    one_w = weight_stack(w_one[...])
    two_w = weight_stack(mix[...] * inv_turn)
    out_w = weight_stack(out_cols[...])
    two_bias = column(mix_phase[...] * inv_turn)
    decay_rate = -1.0 / column(decay[...])
    fine = jnp.exp(
        lax.broadcasted_iota(jnp.int32, (1, half_side), 1).astype(F32) * decay_rate
    )
    for at in range(0, tokens, step):
        base = place[0] * tokens + at
        hidden = sin_turns(dot_t(one_w, feats[:, at : at + step]))
        hidden = sin_turns(dot_t(two_w, value_stack(hidden)) + two_bias)
        raw = dot_t(out_w, value_stack(hidden))
        for sub in range(0, step, half_side):
            row_at, half = divmod((at + sub) // half_side, 2)
            coarse = jnp.exp((base + sub).astype(F32) * decay_rate)
            spread[half, pl.ds(row_at, chans, stride=rows), :] = raw[
                :, sub : sub + half_side
            ] * (coarse * fine + 0.1)
    for half in range(2):
        sent[:, (2 + half) * own : (3 + half) * own] = (
            spread[half].reshape(peers, own, rows, half_side).astype(BF16)
        )
    for copy in copies[6:]:
        copy.wait()
    columns = [[column(taps[which, i : i + 1, :]) for i in range(3)] for which in (1, 2)]
    group = 16
    for at in range(0, chans, group):
        pick = slice(at, at + group)
        gated = short(key[pick, :].astype(F32), [tap[pick, :] for tap in columns[0]]) * short(
            value[pick, :].astype(F32), [tap[pick, :] for tap in columns[1]]
        )
        for sub in range(0, tokens, half_side):
            row_at, half = divmod(sub // half_side, 2)
            gate_spread[half, pl.ds(at * rows + row_at, group, stride=rows), :] = gated[
                :, sub : sub + half_side
            ]
        for half in range(2):
            sent[at // own : (at + group) // own, half * own : (half + 1) * own] = (
                gate_spread[half, at * rows : (at + group) * rows, :]
                .reshape(group // own, own, rows, half_side)
                .astype(BF16)
            )
    lane = lax.broadcasted_iota(jnp.int32, (group, half_side), 1)
    ends = jnp.zeros((group, half_side), F32)
    for part in range(chans // group):
        moved = pltpu.roll(
            query_end[part * group : (part + 1) * group, :].astype(F32), 10 + 2 * part, 1
        )
        ends = jnp.where(lane // 2 == 4 + part, moved, ends)
    for part in range(chans // group):
        pick = slice(part * group, (part + 1) * group)
        edge = ends
        for at, (array, tap) in enumerate(((key, columns[0]), (value, columns[1]))):
            zero, one, two = (each[pick, :] for each in tap)
            head = array[pick, 0:half_side].astype(F32)
            last = array[pick, tokens - half_side : tokens].astype(F32)
            started = two * head + jnp.where(lane == 1, one * pltpu.roll(head, 1, 1), 0.0)
            ended = zero * last + jnp.where(
                lane == half_side - 2, one * pltpu.roll(last, half_side - 1, 1), 0.0
            )
            edge = jnp.where(lane // 2 == at, pltpu.roll(started, 2 * at, 1), edge)
            edge = jnp.where(lane // 2 == 2 + at, pltpu.roll(ended, 6 + 2 * at, 1), edge)
        edge = edge.astype(BF16)
        for peer in range(part * group // own, (part + 1) * group // own):
            sent[peer, slots - 1] = edge


def first_gated(edges, place, own):
    choices = edges.shape[1] // own
    here = jnp.zeros((edges.shape[0], own, edges.shape[2]), F32)
    for choice in range(choices):
        wanted = jnp.broadcast_to(lax.rem(place, choices), here.shape) == choice
        here = jnp.where(wanted, edges[:, choice * own : (choice + 1) * own, :], here)
    before = jnp.concatenate([jnp.zeros_like(here[:1]), here[:-1]], axis=0)
    lanes = here.shape[2]
    shorts = here + pltpu.roll(before, lanes - 4, 2)
    return shorts * pltpu.roll(shorts, lanes - 2, 2)


def conv_kernel(
    place, skip, got, left, back, right_hi, inv_hi,
    twist_re, twist_im, mixed,
):
    side = SIDE
    peers, slots, rows, half_side = got.shape
    own = (slots - 1) // 4
    firsts = first_gated(got[:, slots - 1].astype(F32), place[0], own)
    t_re = twist_re[...]
    t_im = twist_im[...]
    spot = (lax.broadcasted_iota(jnp.int32, (peers, rows, half_side), 1) == 0) & (
        lax.broadcasted_iota(jnp.int32, (peers, rows, half_side), 2) < 2
    )
    group = GROUP
    for at in range(0, own, group):
        data, filt = [], []
        for slot in range(at, at + group):
            head = jnp.where(spot, firsts[:, slot : slot + 1, :], got[:, slot].astype(F32))
            head = head.astype(BF16)
            data.append(
                jnp.concatenate(
                    [head.reshape(side, half_side), got[:, own + slot].reshape(side, half_side)],
                    axis=1,
                )
            )
            filt.append(
                jnp.concatenate(
                    [got[:, (2 + half) * own + slot].reshape(side, half_side) for half in range(2)],
                    axis=1,
                )
            )
        both = jnp.concatenate(data + filt, axis=1)
        first = dot(left[...], jnp.concatenate([both, both], axis=0))
        turned = []
        for at_col in range(0, 2 * group * side, side):
            re, im = first[:side, at_col : at_col + side], first[side:, at_col : at_col + side]
            turned.append(
                jnp.concatenate([re * t_re - im * t_im, re * t_im + im * t_re], axis=1).astype(BF16)
            )
        spec = dot(jnp.concatenate(turned, axis=0), right_hi[...])
        edge_row = group * side
        d_re, d_im = spec[:edge_row, :side], spec[:edge_row, side:]
        f_re, f_im = spec[edge_row:, :side], spec[edge_row:, side:]
        product = jnp.concatenate([d_re * f_re - d_im * f_im, d_re * f_im + d_im * f_re], axis=1)
        inner = dot(product.astype(BF16), inv_hi[...])
        turned = []
        for at_row in range(0, group * side, side):
            re, im = inner[at_row : at_row + side, :side], inner[at_row : at_row + side, side:]
            turned.append(jnp.concatenate([re * t_re + im * t_im, im * t_re - re * t_im], axis=0))
        high, low = split(jnp.concatenate(turned, axis=1))
        values = dot(back[...], jnp.concatenate([high, high, low], axis=0))
        for index in range(group):
            wide = filt[index].astype(F32)
            energy = jnp.sum(jnp.sum(wide * wide, axis=1, keepdims=True), axis=0, keepdims=True)
            unit = lax.rsqrt(energy + EPSILON) * (1.0 / (side * side))
            skipped = skip[place[0] * own + at + index] * data[index].astype(F32)
            result = values[:, index * side : (index + 1) * side] * unit + skipped
            mixed[:, at + index] = result.astype(BF16).reshape(peers, rows, side)


def query_kernel(place, query, taps, got, q_short):
    slots = got.shape[1]
    before = jnp.maximum(place[0] - 1, 0)
    tails = got[before, slots - 1].astype(F32)
    tails = jnp.where(jnp.broadcast_to(place[0], tails.shape) > 0, tails, 0.0)
    group = tails.shape[0]
    columns = [column(taps[0, i : i + 1, :]) for i in range(3)]
    for part in range(query.shape[0] // group):
        pick = slice(part * group, (part + 1) * group)
        tap = [each[pick, :] for each in columns]
        current = query[pick, :].astype(F32)
        q_short[pick, :] = short(current, tap)
        two, one = tails[:, 8 + 2 * part : 9 + 2 * part], tails[:, 9 + 2 * part : 10 + 2 * part]
        q_short[pick, 0:1] = tap[0] * two + tap[1] * one + tap[2] * current[:, 0:1]
        q_short[pick, 1:2] = (
            tap[0] * one + tap[1] * current[:, 0:1] + tap[2] * current[:, 1:2]
        )


def out_kernel(q_short, mixed, gain, gated_out, sums, spread, total):
    peers, own, rows, side = mixed.shape
    chans = peers * own
    half_side = side // 2
    gains = column(gain[...])
    for half in range(2):
        spread[half] = (
            mixed[:, :, :, half * half_side : (half + 1) * half_side]
            .astype(F32)
            .reshape(chans * rows, half_side)
        )
    for at in range(0, q_short.shape[1], half_side):
        row, half = divmod(at // half_side, 2)
        piece = q_short[:, at : at + half_side] * spread[half, pl.ds(row, chans, stride=rows), :]
        gated_out[:, at : at + half_side] = piece * gains
        sum_row, lane = divmod(at, sums.shape[2])
        total[sum_row : sum_row + 1, lane : lane + half_side] = jnp.sum(
            piece * piece, axis=0, keepdims=True
        )
    for peer in range(sums.shape[0]):
        sums[peer] = total[...].astype(BF16)


def scale_kernel(gated_out, sums, result):
    width = sums.shape[2]
    energy = jnp.sum(sums[...].astype(F32), axis=0)
    channels = gated_out.shape[0] * pl.num_programs(0) * sums.shape[0]
    scale = lax.rsqrt(energy / channels + EPSILON)
    for row in range(sums.shape[1]):
        at = row * width
        result[:, at : at + width] = (
            gated_out[:, at : at + width] * scale[row : row + 1, :]
        ).astype(BF16)


def whole(shape, memory_space=None):
    return pl.BlockSpec(shape, lambda *_: (0,) * len(shape), memory_space=memory_space)


SCALAR = pl.BlockSpec(memory_space=pltpu.SMEM)
VECTOR = pl.BlockSpec(memory_space=pltpu.VMEM)
OUTSIDE = pl.BlockSpec(memory_space=pltpu.HBM)


def in_hbm(array):
    return pltpu.with_memory_space_constraint(array, pltpu.HBM)


def params(**more):
    return pltpu.CompilerParams(vmem_limit_bytes=32 * 1024 * 1024, **more)


def shards(
    query_act,
    key_act,
    value_act,
    short_taps,
    pos_proj,
    pos_phase,
    mix_proj,
    mix_phase,
    filter_out,
    decay_len,
    skip_gain,
    out_gain,
):
    chans, tokens = query_act.shape
    peers = lax.axis_size("ctx")
    groups = lax.axis_size("ch")
    place = lax.axis_index("ctx").astype(jnp.int32).reshape(1)
    own = chans // peers
    rows = tokens // SIDE
    units = pos_proj.shape[1]
    half_side = SIDE // 2
    taps = jnp.transpose(short_taps, (0, 2, 1))
    spread = pltpu.VMEM((2, chans * rows, half_side), F32)
    sent = pl.pallas_call(
        send_kernel,
        out_shape=jax.ShapeDtypeStruct((peers, 4 * own + 1, rows, half_side), BF16),
        in_specs=[SCALAR] + [OUTSIDE] * 10,
        out_specs=VECTOR,
        scratch_shapes=[
            pltpu.VMEM(pos_proj.shape, F32),
            pltpu.VMEM((1, units), F32),
            pltpu.VMEM(mix_proj.shape, F32),
            pltpu.VMEM((1, units), F32),
            pltpu.VMEM(filter_out.shape, F32),
            pltpu.VMEM((1, chans), F32),
            pltpu.VMEM(taps.shape, F32),
            pltpu.VMEM((chans, half_side), BF16),
            pltpu.VMEM((chans, tokens), BF16),
            pltpu.VMEM((chans, tokens), BF16),
            pltpu.VMEM(((pos_proj.shape[0] - 1) // 2 * 3, units), F32),
            pltpu.VMEM(((pos_proj.shape[0] - 1) // 2 * 9, tokens), BF16),
            spread,
            spread,
            pltpu.SemaphoreType.DMA((10,)),
        ],
        compiler_params=params(),
        name="send",
    )(
        place,
        *map(
            in_hbm,
            (
                pos_proj,
                pos_phase[None],
                mix_proj,
                mix_phase[None],
                filter_out,
                decay_len[None],
                taps,
                query_act,
                key_act,
                value_act,
            ),
        ),
    )
    got = lax.all_to_all(sent, "ctx", split_axis=0, concat_axis=0, tiled=True)
    tables = [jnp.asarray(t) for t in transform_tables(SIDE)]
    mixed = pl.pallas_call(
        conv_kernel,
        out_shape=jax.ShapeDtypeStruct((peers, own, rows, SIDE), BF16),
        in_specs=[SCALAR, SCALAR] + [VECTOR] * (1 + len(tables)),
        out_specs=VECTOR,
        compiler_params=params(),
        name="long_conv",
    )(place, skip_gain, got, *tables)
    mixed = lax.all_to_all(mixed, "ctx", split_axis=0, concat_axis=0, tiled=True)
    q_short = pl.pallas_call(
        query_kernel,
        out_shape=jax.ShapeDtypeStruct((chans, tokens), F32),
        in_specs=[SCALAR] + [VECTOR] * 3,
        out_specs=VECTOR,
        compiler_params=params(),
        name="query_short",
    )(place, query_act, taps, got)
    width = SIDE
    gated_out, sums = pl.pallas_call(
        out_kernel,
        out_shape=(
            jax.ShapeDtypeStruct((chans, tokens), F32),
            jax.ShapeDtypeStruct((groups, tokens // width, width), BF16),
        ),
        in_specs=[VECTOR] * 3,
        out_specs=(VECTOR, VECTOR),
        scratch_shapes=[spread, pltpu.VMEM((tokens // width, width), F32)],
        compiler_params=params(),
        name="gate_out",
    )(q_short, mixed, out_gain[None])
    sums = lax.all_to_all(sums, "ch", split_axis=0, concat_axis=0, tiled=True)
    group = 16
    wide = pl.BlockSpec((group, tokens), lambda i: (i, 0))
    return pl.pallas_call(
        scale_kernel,
        out_shape=jax.ShapeDtypeStruct((chans, tokens), BF16),
        grid=(chans // group,),
        in_specs=[wide, whole((groups, tokens // width, width))],
        out_specs=wide,
        compiler_params=params(),
        name="norm_out",
    )(gated_out, sums)


def solution(mesh):
    return jax.shard_map(
        shards,
        mesh=mesh,
        in_specs=(
            P("ch", "ctx"),
            P("ch", "ctx"),
            P("ch", "ctx"),
            P(None, "ch", None),
            P(),
            P(),
            P(),
            P(),
            P(None, "ch"),
            P("ch"),
            P("ch"),
            P("ch"),
        ),
        out_specs=P("ch", "ctx"),
        check_vma=False,
    )
```

```python
import math

import ml_dtypes
import numpy as np

import jax
import jax.numpy as jnp
from jax import lax
from jax.experimental import pallas as pl
from jax.experimental.pallas import tpu as pltpu
from jax.sharding import PartitionSpec as P

EPSILON = 1e-06
F32 = jnp.float32
BF16 = jnp.bfloat16
SIDE = 256
GROUP = 2
FAR_STEP = 8192
FAR_SETS = 4
SIN_COEFS = (
    6.283182819148623,
    -41.341421436010776,
    81.59618459694858,
    -76.58010652932292,
    41.205417211473964,
    -12.271293082622988,
)


def sin_turns(turns):
    rest = turns - lax.round(turns, lax.RoundingMethod.TO_NEAREST_EVEN)
    square = rest * rest
    acc = jnp.full_like(rest, SIN_COEFS[-1])
    for coef in SIN_COEFS[-2::-1]:
        acc = acc * square + coef
    return acc * rest


def split(array):
    high = array.astype(BF16)
    low = (array - high.astype(F32)).astype(BF16)
    return high, low


def dot(lhs, rhs):
    return lax.dot_general(lhs, rhs, (((1,), (0,)), ((), ())), preferred_element_type=F32)


def dot_t(lhs, rhs):
    return lax.dot_general(lhs, rhs, (((0,), (0,)), ((), ())), preferred_element_type=F32)


def weight_stack(weights):
    high, low = split(weights)
    return jnp.concatenate([high, high, low], axis=0)


def value_stack(values):
    high, low = split(values)
    return jnp.concatenate([high, low, high], axis=0)


def column(row):
    size = row.shape[1]
    eye = lax.broadcasted_iota(jnp.int32, (size, size), 0) == lax.broadcasted_iota(
        jnp.int32, (size, size), 1
    )
    return jnp.sum(jnp.where(eye, jnp.broadcast_to(row, (size, size)), 0.0), axis=1, keepdims=True)


def np_split(array):
    high = array.astype(np.float32).astype(ml_dtypes.bfloat16)
    low = (array - high.astype(np.float64)).astype(np.float32).astype(ml_dtypes.bfloat16)
    return high, low


def stacked(array):
    high, low = np_split(array)
    return np.concatenate([high, low], axis=1)


def transform_tables(side):
    total = side * side
    ids = np.arange(side)
    first = np.exp(-2j * np.pi * np.outer(ids - 0.25, ids) / side)
    twist = np.exp(-2j * np.pi * np.outer(ids - 0.25, ids) / total)
    second = np.exp(-2j * np.pi * (np.outer(ids, ids) % side) / side)
    left = np.concatenate([first.real, first.imag], axis=0)
    return (
        stacked(left),
        stacked(left.T),
        np_split(np.concatenate([second.real, second.imag], axis=1))[0],
        twist.real.astype(np.float32),
        twist.imag.astype(np.float32),
    )


def feature_stack(base, bands, step, total):
    times = base + lax.broadcasted_iota(jnp.int32, (bands, step), 1)
    row = lax.broadcasted_iota(jnp.int32, (bands, step), 0)
    freqs = jnp.left_shift(jnp.ones((bands, step), jnp.int32), row)
    turns = ((freqs * times) & (total - 1)).astype(F32) * (1.0 / total)
    extra = jnp.where(row == 0, times.astype(F32) * (1.0 / total), jnp.where(row == 1, 1.0, 0.0))
    return value_stack(
        jnp.concatenate([sin_turns(turns + 0.25), sin_turns(turns), extra], axis=0)
    )


def network_weights(pos, phase, mix, mix_phase, w_one):
    bands = (pos.shape[0] - 1) // 2
    inv_turn = 1.0 / (2.0 * math.pi)
    w_one[...] = jnp.zeros_like(w_one)
    w_one[0 : 2 * bands, :] = pos[1 : 2 * bands + 1, :] * inv_turn
    w_one[2 * bands : 2 * bands + 1, :] = pos[0:1, :] * inv_turn
    w_one[2 * bands + 1 : 2 * bands + 2, :] = phase[...] * inv_turn
    row = lax.broadcasted_iota(jnp.int32, (bands, w_one.shape[1]), 0)
    high, low = split(mix_phase[...] * inv_turn)
    bias = jnp.where(row == 0, high.astype(F32), jnp.where(row == 1, low.astype(F32), 0.0))
    return jnp.concatenate([weight_stack(mix[...] * inv_turn), bias.astype(BF16)], axis=0)


def hidden_units(feats, one_w, two_w):
    hidden = value_stack(sin_turns(dot_t(one_w, feats)))
    ones = jnp.ones((two_w.shape[0] - hidden.shape[0], hidden.shape[1]), BF16)
    return sin_turns(dot_t(two_w, jnp.concatenate([hidden, ones], axis=0)))


def far_kernel(
    place, pos_hbm, phase_hbm, mix_hbm, mix_phase_hbm, out_hbm, decay_hbm, far, pos, phase, mix,
    mix_phase, out_cols, decay, w_one, feats, spread, sems,
):
    bands = (pos.shape[0] - 1) // 2
    own, _, rows, half_side = far.shape
    begin = rows * SIDE
    total = 2 * begin
    pairs = [
        (pos_hbm, pos),
        (phase_hbm, phase),
        (mix_hbm, mix),
        (mix_phase_hbm, mix_phase),
        (out_hbm, out_cols),
        (decay_hbm, decay),
    ]
    copies = [
        pltpu.make_async_copy(source, target, sems.at[at])
        for at, (source, target) in enumerate(pairs)
    ]
    for copy in copies:
        copy.start()
    step = FAR_STEP
    feats[...] = feature_stack(0, bands, step, total)
    for copy in copies:
        copy.wait()
    two_w = network_weights(pos, phase, mix, mix_phase, w_one)
    cos_w = w_one[0:bands, :]
    sin_w = w_one[bands : 2 * bands, :]
    slope = w_one[2 * bands : 2 * bands + 1, :]
    level = w_one[2 * bands + 1 : 2 * bands + 2, :]
    freqs = jnp.left_shift(
        jnp.ones((bands, 1), jnp.int32), lax.broadcasted_iota(jnp.int32, (bands, 1), 0)
    )
    lane = lax.broadcasted_iota(jnp.int32, out_cols.shape, 1)
    units = out_cols.shape[0]
    narrow = lax.broadcasted_iota(jnp.int32, (units, FAR_SETS * 16), 1)
    tall = lax.broadcasted_iota(jnp.int32, (8, 1), 0)
    cols = jnp.zeros(narrow.shape, F32)
    rate = jnp.zeros(tall.shape, F32)
    decay_rate = -1.0 / decay[...]
    for slot in range(own):
        here = lane == place[0] * own + slot
        col = jnp.sum(jnp.where(here, out_cols[...], 0.0), axis=1, keepdims=True)
        cols = jnp.where(lax.rem(narrow, 8) == slot, col, cols)
        one_rate = jnp.sum(jnp.where(here[0:1, :], decay_rate, 0.0), axis=1, keepdims=True)
        rate = jnp.where(tall == slot, one_rate, rate)
    high, low = split(cols)
    cols = jnp.where(lax.rem(narrow, 16) < 8, high.astype(F32), low.astype(F32))
    out_w = jnp.concatenate(
        [jnp.where(narrow // 16 == part, cols, 0.0) for part in range(FAR_SETS)], axis=0
    ).astype(BF16)
    fine = jnp.exp(lax.broadcasted_iota(jnp.int32, (1, half_side), 1).astype(F32) * rate)
    step = FAR_STEP

    def chunk(index, carry):
        base = begin + index * step
        turns = ((freqs * base) & (total - 1)).astype(F32) * (1.0 / total)
        cosine, sine = sin_turns(turns + 0.25), sin_turns(turns)
        w_one[0:bands, :] = cos_w * cosine + sin_w * sine
        w_one[bands : 2 * bands, :] = sin_w * cosine - cos_w * sine
        w_one[2 * bands + 1 : 2 * bands + 2, :] = level + slope * (base.astype(F32) * (1.0 / total))
        hidden = hidden_units(feats[...], weight_stack(w_one[...]), two_w).astype(BF16)
        width = step // FAR_SETS
        parts = [hidden[:, part * width : (part + 1) * width] for part in range(FAR_SETS)]
        both = dot_t(out_w, jnp.concatenate(parts, axis=0))
        for sub in range(0, step, half_side):
            row_at, half = divmod(sub // half_side, 2)
            coarse = jnp.exp((base + sub).astype(F32) * rate)
            row = index * (step // SIDE) + row_at
            part, lanes = divmod(sub, width)
            raw = (
                both[part * 16 : part * 16 + 8, lanes : lanes + half_side]
                + both[part * 16 + 8 : part * 16 + 16, lanes : lanes + half_side]
            )
            spread[half, pl.ds(row, 8, stride=rows), :] = raw * (coarse * fine + 0.1)
        return carry

    lax.fori_loop(0, begin // step, chunk, 0, unroll=2)
    for slot in range(own):
        for half in range(2):
            far[slot, half] = spread[half, slot * rows : (slot + 1) * rows, :].astype(BF16)


def short(current, taps):
    return (
        taps[0] * pltpu.roll(current, 2, 1)
        + taps[1] * pltpu.roll(current, 1, 1)
        + taps[2] * current
    )


def send_kernel(
    place, pos_hbm, phase_hbm, mix_hbm, mix_phase_hbm, out_hbm, decay_hbm, taps_hbm, query_hbm,
    key_hbm, value_hbm, sent, pos, phase, mix, mix_phase, out_cols, decay, w_one, taps, query_end,
    key, value, feats, spread, gate_spread, sems,
):
    bands = (pos.shape[0] - 1) // 2
    peers, slots, rows, half_side = sent.shape
    own = (slots - 1) // 3
    chans, tokens = key.shape
    total = peers * tokens
    pairs = [
        (pos_hbm, pos),
        (phase_hbm, phase),
        (mix_hbm, mix),
        (mix_phase_hbm, mix_phase),
        (out_hbm, out_cols),
        (decay_hbm, decay),
        (taps_hbm, taps),
        (query_hbm.at[:, tokens - half_side : tokens], query_end),
        (key_hbm, key),
        (value_hbm, value),
    ]
    copies = [
        pltpu.make_async_copy(source, target, sems.at[at])
        for at, (source, target) in enumerate(pairs)
    ]
    for copy in copies:
        copy.start()
    near = tokens // 2
    base = place[0] * near
    feats[...] = feature_stack(base, bands, near, total)
    for copy in copies[:6]:
        copy.wait()
    two_w = network_weights(pos, phase, mix, mix_phase, w_one)
    out_w = weight_stack(out_cols[...])
    decay_rate = -1.0 / column(decay[...])
    fine = jnp.exp(lax.broadcasted_iota(jnp.int32, (1, half_side), 1).astype(F32) * decay_rate)
    raw = dot_t(out_w, value_stack(hidden_units(feats[...], weight_stack(w_one[...]), two_w)))
    for sub in range(0, near, half_side):
        row_at, half = divmod(sub // half_side, 2)
        coarse = jnp.exp((base + sub).astype(F32) * decay_rate)
        spread[pl.ds(row_at + half * rows // 2, chans, stride=rows), :] = raw[
            :, sub : sub + half_side
        ] * (coarse * fine + 0.1)
    sent[:, 2 * own : 3 * own] = spread[...].reshape(peers, own, rows, half_side).astype(BF16)
    for copy in copies[6:]:
        copy.wait()
    columns = [[column(taps[which, i : i + 1, :]) for i in range(3)] for which in (1, 2)]
    group = 16
    for at in range(0, chans, group):
        pick = slice(at, at + group)
        gated = short(key[pick, :].astype(F32), [tap[pick, :] for tap in columns[0]]) * short(
            value[pick, :].astype(F32), [tap[pick, :] for tap in columns[1]]
        )
        for sub in range(0, tokens, half_side):
            row_at, half = divmod(sub // half_side, 2)
            gate_spread[half, pl.ds(at * rows + row_at, group, stride=rows), :] = gated[
                :, sub : sub + half_side
            ]
        for half in range(2):
            sent[at // own : (at + group) // own, half * own : (half + 1) * own] = (
                gate_spread[half, at * rows : (at + group) * rows, :]
                .reshape(group // own, own, rows, half_side)
                .astype(BF16)
            )
    lane = lax.broadcasted_iota(jnp.int32, (group, half_side), 1)
    ends = jnp.zeros((group, half_side), F32)
    for part in range(chans // group):
        moved = pltpu.roll(
            query_end[part * group : (part + 1) * group, :].astype(F32), 10 + 2 * part, 1
        )
        ends = jnp.where(lane // 2 == 4 + part, moved, ends)
    for part in range(chans // group):
        pick = slice(part * group, (part + 1) * group)
        edge = ends
        for at, (array, tap) in enumerate(((key, columns[0]), (value, columns[1]))):
            zero, one, two = (each[pick, :] for each in tap)
            head = array[pick, 0:half_side].astype(F32)
            last = array[pick, tokens - half_side : tokens].astype(F32)
            started = two * head + jnp.where(lane == 1, one * pltpu.roll(head, 1, 1), 0.0)
            ended = zero * last + jnp.where(
                lane == half_side - 2, one * pltpu.roll(last, half_side - 1, 1), 0.0
            )
            edge = jnp.where(lane // 2 == at, pltpu.roll(started, 2 * at, 1), edge)
            edge = jnp.where(lane // 2 == 2 + at, pltpu.roll(ended, 6 + 2 * at, 1), edge)
        edge = edge.astype(BF16)
        for peer in range(part * group // own, (part + 1) * group // own):
            sent[peer, slots - 1] = edge


def first_gated(edges, place, own):
    choices = edges.shape[1] // own
    here = jnp.zeros((edges.shape[0], own, edges.shape[2]), F32)
    for choice in range(choices):
        wanted = jnp.broadcast_to(lax.rem(place, choices), here.shape) == choice
        here = jnp.where(wanted, edges[:, choice * own : (choice + 1) * own, :], here)
    before = jnp.concatenate([jnp.zeros_like(here[:1]), here[:-1]], axis=0)
    lanes = here.shape[2]
    shorts = here + pltpu.roll(before, lanes - 4, 2)
    return shorts * pltpu.roll(shorts, lanes - 2, 2)


def conv_kernel(
    place, skip, got, far, left, back, ahead, twist_re, twist_im, mixed, right, inverse,
):
    side = SIDE
    peers, slots, rows, half_side = got.shape
    own = (slots - 1) // 3
    firsts = first_gated(got[:, slots - 1].astype(F32), place[0], own)
    ahead_re, ahead_im = ahead[:, :side], ahead[:, side:]
    right[0:side, 0:side] = ahead_re
    right[0:side, side:] = ahead_im
    right[side:, 0:side] = -ahead_im
    right[side:, side:] = ahead_re
    inverse[0:side, 0:side] = ahead_re
    inverse[0:side, side:] = -ahead_im
    inverse[side:, 0:side] = ahead_im
    inverse[side:, side:] = ahead_re
    t_re = twist_re[...]
    t_im = twist_im[...]
    spot = (lax.broadcasted_iota(jnp.int32, (peers, rows, half_side), 1) == 0) & (
        lax.broadcasted_iota(jnp.int32, (peers, rows, half_side), 2) < 2
    )
    group = GROUP
    for at in range(0, own, group):
        data, filt = [], []
        for slot in range(at, at + group):
            head = jnp.where(spot, firsts[:, slot : slot + 1, :], got[:, slot].astype(F32))
            head = head.astype(BF16)
            data.append(
                jnp.concatenate(
                    [head.reshape(side, half_side), got[:, own + slot].reshape(side, half_side)],
                    axis=1,
                )
            )
            near = got[:, 2 * own + slot].astype(F32)
            near = [
                near[:, half * rows // 2 : (half + 1) * rows // 2].reshape(side // 2, half_side)
                for half in range(2)
            ]
            filt.append(
                jnp.concatenate(
                    [
                        jnp.concatenate(near, axis=1).astype(BF16),
                        jnp.concatenate([far[slot, 0], far[slot, 1]], axis=1),
                    ],
                    axis=0,
                )
            )
        both = jnp.concatenate(data + filt, axis=1)
        first = dot(left[...], jnp.concatenate([both, both], axis=0))
        turned = []
        for at_col in range(0, 2 * group * side, side):
            re, im = first[:side, at_col : at_col + side], first[side:, at_col : at_col + side]
            turned.append(
                jnp.concatenate([re * t_re - im * t_im, re * t_im + im * t_re], axis=1).astype(BF16)
            )
        spec = dot(jnp.concatenate(turned, axis=0), right[...])
        edge_row = group * side
        d_re, d_im = spec[:edge_row, :side], spec[:edge_row, side:]
        f_re, f_im = spec[edge_row:, :side], spec[edge_row:, side:]
        product = jnp.concatenate([d_re * f_re - d_im * f_im, d_re * f_im + d_im * f_re], axis=1)
        inner = dot(product.astype(BF16), inverse[...])
        turned = []
        for at_row in range(0, group * side, side):
            re, im = inner[at_row : at_row + side, :side], inner[at_row : at_row + side, side:]
            turned.append(jnp.concatenate([re * t_re + im * t_im, im * t_re - re * t_im], axis=0))
        high, low = split(jnp.concatenate(turned, axis=1))
        values = dot(back[...], jnp.concatenate([high, high], axis=0))
        values = values + dot(back[:, : 2 * side], low)
        for index in range(group):
            wide = filt[index].astype(F32)
            energy = jnp.sum(jnp.sum(wide * wide, axis=1, keepdims=True), axis=0, keepdims=True)
            unit = lax.rsqrt(energy + EPSILON) * (1.0 / (side * side))
            skipped = skip[place[0] * own + at + index] * data[index].astype(F32)
            result = values[:, index * side : (index + 1) * side] * unit + skipped
            mixed[:, at + index] = result.astype(BF16).reshape(peers, rows, side)


def query_kernel(place, query_hbm, taps, got, q_short, query, sem):
    copy = pltpu.make_async_copy(query_hbm, query, sem)
    copy.start()
    slots = got.shape[1]
    before = jnp.maximum(place[0] - 1, 0)
    tails = got[before, slots - 1].astype(F32)
    tails = jnp.where(jnp.broadcast_to(place[0], tails.shape) > 0, tails, 0.0)
    group = tails.shape[0]
    columns = [column(taps[0, i : i + 1, :]) for i in range(3)]
    copy.wait()
    for part in range(query.shape[0] // group):
        pick = slice(part * group, (part + 1) * group)
        tap = [each[pick, :] for each in columns]
        current = query[pick, :].astype(F32)
        q_short[pick, :] = short(current, tap)
        two, one = tails[:, 8 + 2 * part : 9 + 2 * part], tails[:, 9 + 2 * part : 10 + 2 * part]
        q_short[pick, 0:1] = tap[0] * two + tap[1] * one + tap[2] * current[:, 0:1]
        q_short[pick, 1:2] = (
            tap[0] * one + tap[1] * current[:, 0:1] + tap[2] * current[:, 1:2]
        )


def out_kernel(q_short, mixed, gain, gated_out, sums, spread, total):
    peers, own, rows, side = mixed.shape
    chans = peers * own
    half_side = side // 2
    gains = column(gain[...])
    for half in range(2):
        spread[half] = (
            mixed[:, :, :, half * half_side : (half + 1) * half_side]
            .astype(F32)
            .reshape(chans * rows, half_side)
        )
    for at in range(0, q_short.shape[1], half_side):
        row, half = divmod(at // half_side, 2)
        piece = q_short[:, at : at + half_side] * spread[half, pl.ds(row, chans, stride=rows), :]
        gated_out[:, at : at + half_side] = piece * gains
        sum_row, lane = divmod(at, sums.shape[2])
        total[sum_row : sum_row + 1, lane : lane + half_side] = jnp.sum(
            piece * piece, axis=0, keepdims=True
        )
    for peer in range(sums.shape[0]):
        sums[peer] = total[...].astype(BF16)


def scale_kernel(gated_out, sums, result):
    width = sums.shape[2]
    energy = jnp.sum(sums[...].astype(F32), axis=0)
    channels = gated_out.shape[0] * pl.num_programs(0) * sums.shape[0]
    scale = lax.rsqrt(energy / channels + EPSILON)
    for row in range(sums.shape[1]):
        at = row * width
        result[:, at : at + width] = (
            gated_out[:, at : at + width] * scale[row : row + 1, :]
        ).astype(BF16)


def whole(shape, memory_space=None):
    return pl.BlockSpec(shape, lambda *_: (0,) * len(shape), memory_space=memory_space)


SCALAR = pl.BlockSpec(memory_space=pltpu.SMEM)
VECTOR = pl.BlockSpec(memory_space=pltpu.VMEM)
OUTSIDE = pl.BlockSpec(memory_space=pltpu.HBM)


def in_hbm(array):
    return pltpu.with_memory_space_constraint(array, pltpu.HBM)


def params(mebibytes):
    return pltpu.CompilerParams(vmem_limit_bytes=mebibytes * 1024 * 1024)


def shards(
    query_act,
    key_act,
    value_act,
    short_taps,
    pos_proj,
    pos_phase,
    mix_proj,
    mix_phase,
    filter_out,
    decay_len,
    skip_gain,
    out_gain,
):
    chans, tokens = query_act.shape
    peers = lax.axis_size("ctx")
    groups = lax.axis_size("ch")
    place = lax.axis_index("ctx").astype(jnp.int32).reshape(1)
    own = chans // peers
    rows = tokens // SIDE
    units = pos_proj.shape[1]
    half_side = SIDE // 2
    taps = jnp.transpose(short_taps, (0, 2, 1))
    spread = pltpu.VMEM((2, chans * rows, half_side), F32)
    bands = (pos_proj.shape[0] - 1) // 2
    network = [
        pltpu.VMEM(pos_proj.shape, F32),
        pltpu.VMEM((1, units), F32),
        pltpu.VMEM(mix_proj.shape, F32),
        pltpu.VMEM((1, units), F32),
        pltpu.VMEM(filter_out.shape, F32),
        pltpu.VMEM((1, chans), F32),
        pltpu.VMEM((bands * 3, units), F32),
    ]
    weights = [
        in_hbm(array)
        for array in (
            pos_proj, pos_phase[None], mix_proj, mix_phase[None], filter_out, decay_len[None]
        )
    ]
    sent = pl.pallas_call(
        send_kernel,
        out_shape=jax.ShapeDtypeStruct((peers, 3 * own + 1, rows, half_side), BF16),
        in_specs=[SCALAR] + [OUTSIDE] * 10,
        out_specs=VECTOR,
        scratch_shapes=network
        + [
            pltpu.VMEM(taps.shape, F32),
            pltpu.VMEM((chans, half_side), BF16),
            pltpu.VMEM((chans, tokens), BF16),
            pltpu.VMEM((chans, tokens), BF16),
            pltpu.VMEM((bands * 9, tokens // 2), BF16),
            pltpu.VMEM((chans * rows, half_side), F32),
            pltpu.VMEM((2, chans * rows, half_side), F32),
            pltpu.SemaphoreType.DMA((10,)),
        ],
        compiler_params=params(24),
        name="send",
    )(place, *weights, *map(in_hbm, (taps, query_act, key_act, value_act)))
    far_rows = SIDE // 2
    far = pl.pallas_call(
        far_kernel,
        out_shape=jax.ShapeDtypeStruct((own, 2, far_rows, half_side), BF16),
        in_specs=[SCALAR] + [OUTSIDE] * 6,
        out_specs=VECTOR,
        scratch_shapes=network
        + [
            pltpu.VMEM((bands * 9, FAR_STEP), BF16),
            pltpu.VMEM((2, 8 * far_rows, half_side), F32),
            pltpu.SemaphoreType.DMA((6,)),
        ],
        compiler_params=params(16),
        cost_estimate=pl.CostEstimate(
            flops=10_000_000_000, transcendentals=0, bytes_accessed=1_000_000
        ),
        name="far_taps",
    )(place, *weights)
    got = lax.all_to_all(sent, "ctx", split_axis=0, concat_axis=0, tiled=True)
    tables = [jnp.asarray(t) for t in transform_tables(SIDE)]
    mixed = pl.pallas_call(
        conv_kernel,
        out_shape=jax.ShapeDtypeStruct((peers, own, rows, SIDE), BF16),
        in_specs=[SCALAR, SCALAR] + [VECTOR] * (2 + len(tables)),
        out_specs=VECTOR,
        scratch_shapes=[pltpu.VMEM((2 * SIDE, 2 * SIDE), BF16)] * 2,
        compiler_params=params(24),
        name="long_conv",
    )(place, skip_gain, got, far, *tables)
    mixed = lax.all_to_all(mixed, "ctx", split_axis=0, concat_axis=0, tiled=True)
    q_short = pl.pallas_call(
        query_kernel,
        out_shape=jax.ShapeDtypeStruct((chans, tokens), F32),
        in_specs=[SCALAR, OUTSIDE, VECTOR, VECTOR],
        out_specs=VECTOR,
        scratch_shapes=[pltpu.VMEM((chans, tokens), BF16), pltpu.SemaphoreType.DMA],
        compiler_params=params(16),
        name="query_short",
    )(place, in_hbm(query_act), taps, got)
    width = SIDE
    gated_out, sums = pl.pallas_call(
        out_kernel,
        out_shape=(
            jax.ShapeDtypeStruct((chans, tokens), F32),
            jax.ShapeDtypeStruct((groups, tokens // width, width), BF16),
        ),
        in_specs=[VECTOR] * 3,
        out_specs=(VECTOR, VECTOR),
        scratch_shapes=[spread, pltpu.VMEM((tokens // width, width), F32)],
        compiler_params=params(16),
        name="gate_out",
    )(q_short, mixed, out_gain[None])
    sums = lax.all_to_all(sums, "ch", split_axis=0, concat_axis=0, tiled=True)
    group = 16
    wide = pl.BlockSpec((group, tokens), lambda i: (i, 0))
    return pl.pallas_call(
        scale_kernel,
        out_shape=jax.ShapeDtypeStruct((chans, tokens), BF16),
        grid=(chans // group,),
        in_specs=[wide, whole((groups, tokens // width, width))],
        out_specs=wide,
        compiler_params=params(16),
        name="norm_out",
    )(gated_out, sums)


def solution(mesh):
    return jax.shard_map(
        shards,
        mesh=mesh,
        in_specs=(
            P("ch", "ctx"),
            P("ch", "ctx"),
            P("ch", "ctx"),
            P(None, "ch", None),
            P(),
            P(),
            P(),
            P(),
            P(None, "ch"),
            P("ch"),
            P("ch"),
            P("ch"),
        ),
        out_specs=P("ch", "ctx"),
        check_vma=False,
    )
```

```python
import math

import ml_dtypes
import numpy as np

import jax
import jax.numpy as jnp
from jax import lax
from jax.experimental import pallas as pl
from jax.experimental.pallas import tpu as pltpu
from jax.sharding import PartitionSpec as P

EPSILON = 1e-06
F32 = jnp.float32
BF16 = jnp.bfloat16
SIDE = 256
GROUP = 2
FAR_STEP = 8192
FAR_SETS = 4
SIN_COEFS = (
    6.283182819148623,
    -41.341421436010776,
    81.59618459694858,
    -76.58010652932292,
    41.205417211473964,
    -12.271293082622988,
)


def sin_turns(turns):
    rest = turns - lax.round(turns, lax.RoundingMethod.TO_NEAREST_EVEN)
    square = rest * rest
    acc = jnp.full_like(rest, SIN_COEFS[-1])
    for coef in SIN_COEFS[-2::-1]:
        acc = acc * square + coef
    return acc * rest


def split(array):
    high = array.astype(BF16)
    low = (array - high.astype(F32)).astype(BF16)
    return high, low


def dot(lhs, rhs):
    return lax.dot_general(lhs, rhs, (((1,), (0,)), ((), ())), preferred_element_type=F32)


def dot_t(lhs, rhs):
    return lax.dot_general(lhs, rhs, (((0,), (0,)), ((), ())), preferred_element_type=F32)


def weight_stack(weights):
    high, low = split(weights)
    return jnp.concatenate([high, high, low], axis=0)


def value_stack(values):
    high, low = split(values)
    return jnp.concatenate([high, low, high], axis=0)


def column(row):
    size = row.shape[1]
    eye = lax.broadcasted_iota(jnp.int32, (size, size), 0) == lax.broadcasted_iota(
        jnp.int32, (size, size), 1
    )
    return jnp.sum(jnp.where(eye, jnp.broadcast_to(row, (size, size)), 0.0), axis=1, keepdims=True)


def np_split(array):
    high = array.astype(np.float32).astype(ml_dtypes.bfloat16)
    low = (array - high.astype(np.float64)).astype(np.float32).astype(ml_dtypes.bfloat16)
    return high, low


def stacked(array):
    high, low = np_split(array)
    return np.concatenate([high, low], axis=1)


def transform_tables(side):
    total = side * side
    ids = np.arange(side)
    first = np.exp(-2j * np.pi * np.outer(ids - 0.25, ids) / side)
    twist = np.exp(-2j * np.pi * np.outer(ids - 0.25, ids) / total)
    second = np.exp(-2j * np.pi * (np.outer(ids, ids) % side) / side)
    left = np.concatenate([first.real, first.imag], axis=0)
    right = np.block([[second.real, second.imag], [-second.imag, second.real]])
    return (
        stacked(left),
        stacked(left.T),
        np_split(right)[0],
        twist.real.astype(np.float32),
        twist.imag.astype(np.float32),
    )


def feature_stack(base, bands, step, total):
    times = base + lax.broadcasted_iota(jnp.int32, (bands, step), 1)
    row = lax.broadcasted_iota(jnp.int32, (bands, step), 0)
    freqs = jnp.left_shift(jnp.ones((bands, step), jnp.int32), row)
    turns = ((freqs * times) & (total - 1)).astype(F32) * (1.0 / total)
    extra = jnp.where(row == 0, times.astype(F32) * (1.0 / total), jnp.where(row == 1, 1.0, 0.0))
    return value_stack(
        jnp.concatenate([sin_turns(turns + 0.25), sin_turns(turns), extra], axis=0)
    )


def network_weights(pos, phase, mix, mix_phase, w_one):
    bands = (pos.shape[0] - 1) // 2
    inv_turn = 1.0 / (2.0 * math.pi)
    w_one[...] = jnp.zeros_like(w_one)
    w_one[0 : 2 * bands, :] = pos[1 : 2 * bands + 1, :] * inv_turn
    w_one[2 * bands : 2 * bands + 1, :] = pos[0:1, :] * inv_turn
    w_one[2 * bands + 1 : 2 * bands + 2, :] = phase[...] * inv_turn
    row = lax.broadcasted_iota(jnp.int32, (bands, w_one.shape[1]), 0)
    high, low = split(mix_phase[...] * inv_turn)
    bias = jnp.where(row == 0, high.astype(F32), jnp.where(row == 1, low.astype(F32), 0.0))
    return jnp.concatenate([weight_stack(mix[...] * inv_turn), bias.astype(BF16)], axis=0)


def hidden_units(feats, one_w, two_w):
    hidden = value_stack(sin_turns(dot_t(one_w, feats)))
    ones = jnp.ones((two_w.shape[0] - hidden.shape[0], hidden.shape[1]), BF16)
    return sin_turns(dot_t(two_w, jnp.concatenate([hidden, ones], axis=0)))


def far_kernel(
    place, pos_hbm, phase_hbm, mix_hbm, mix_phase_hbm, out_hbm, decay_hbm, gain_hbm, skip_hbm, far,
    gain, skip, pos, phase, mix, mix_phase, out_cols, decay, w_one, feats, spread, sems,
):
    bands = (pos.shape[0] - 1) // 2
    own, _, rows, half_side = far.shape
    begin = rows * SIDE
    total = 2 * begin
    pairs = [
        (pos_hbm, pos),
        (phase_hbm, phase),
        (mix_hbm, mix),
        (mix_phase_hbm, mix_phase),
        (out_hbm, out_cols),
        (decay_hbm, decay),
        (gain_hbm, gain),
        (skip_hbm, skip),
    ]
    copies = [
        pltpu.make_async_copy(source, target, sems.at[at])
        for at, (source, target) in enumerate(pairs)
    ]
    for copy in copies:
        copy.start()
    step = FAR_STEP
    feats[...] = feature_stack(0, bands, step, total)
    for copy in copies:
        copy.wait()
    two_w = network_weights(pos, phase, mix, mix_phase, w_one)
    cos_w = w_one[0:bands, :]
    sin_w = w_one[bands : 2 * bands, :]
    slope = w_one[2 * bands : 2 * bands + 1, :]
    level = w_one[2 * bands + 1 : 2 * bands + 2, :]
    freqs = jnp.left_shift(
        jnp.ones((bands, 1), jnp.int32), lax.broadcasted_iota(jnp.int32, (bands, 1), 0)
    )
    lane = lax.broadcasted_iota(jnp.int32, out_cols.shape, 1)
    units = out_cols.shape[0]
    narrow = lax.broadcasted_iota(jnp.int32, (units, FAR_SETS * 16), 1)
    tall = lax.broadcasted_iota(jnp.int32, (8, 1), 0)
    cols = jnp.zeros(narrow.shape, F32)
    rate = jnp.zeros(tall.shape, F32)
    decay_rate = -1.0 / decay[...]
    for slot in range(own):
        here = lane == place[0] * own + slot
        col = jnp.sum(jnp.where(here, out_cols[...], 0.0), axis=1, keepdims=True)
        cols = jnp.where(lax.rem(narrow, 8) == slot, col, cols)
        one_rate = jnp.sum(jnp.where(here[0:1, :], decay_rate, 0.0), axis=1, keepdims=True)
        rate = jnp.where(tall == slot, one_rate, rate)
    high, low = split(cols)
    cols = jnp.where(lax.rem(narrow, 16) < 8, high.astype(F32), low.astype(F32))
    out_w = jnp.concatenate(
        [jnp.where(narrow // 16 == part, cols, 0.0) for part in range(FAR_SETS)], axis=0
    ).astype(BF16)
    fine = jnp.exp(lax.broadcasted_iota(jnp.int32, (1, half_side), 1).astype(F32) * rate)
    step = FAR_STEP

    def chunk(index, carry):
        base = begin + index * step
        turns = ((freqs * base) & (total - 1)).astype(F32) * (1.0 / total)
        cosine, sine = sin_turns(turns + 0.25), sin_turns(turns)
        w_one[0:bands, :] = cos_w * cosine + sin_w * sine
        w_one[bands : 2 * bands, :] = sin_w * cosine - cos_w * sine
        w_one[2 * bands + 1 : 2 * bands + 2, :] = level + slope * (base.astype(F32) * (1.0 / total))
        hidden = hidden_units(feats[...], weight_stack(w_one[...]), two_w).astype(BF16)
        width = step // FAR_SETS
        parts = [hidden[:, part * width : (part + 1) * width] for part in range(FAR_SETS)]
        both = dot_t(out_w, jnp.concatenate(parts, axis=0))
        for sub in range(0, step, half_side):
            row_at, half = divmod(sub // half_side, 2)
            coarse = jnp.exp((base + sub).astype(F32) * rate)
            row = index * (step // SIDE) + row_at
            part, lanes = divmod(sub, width)
            raw = (
                both[part * 16 : part * 16 + 8, lanes : lanes + half_side]
                + both[part * 16 + 8 : part * 16 + 16, lanes : lanes + half_side]
            )
            spread[half, pl.ds(row, 8, stride=rows), :] = raw * (coarse * fine + 0.1)
        return carry

    lax.fori_loop(0, begin // step, chunk, 0, unroll=2)
    for slot in range(own):
        for half in range(2):
            far[slot, half] = spread[half, slot * rows : (slot + 1) * rows, :].astype(BF16)


def short(current, taps):
    return (
        taps[0] * pltpu.roll(current, 2, 1)
        + taps[1] * pltpu.roll(current, 1, 1)
        + taps[2] * current
    )


def send_kernel(
    place, pos_hbm, phase_hbm, mix_hbm, mix_phase_hbm, out_hbm, decay_hbm, taps_hbm, query_hbm,
    key_hbm, value_hbm, sent_hbm, pos, phase, mix, mix_phase, out_cols, decay, w_one, taps, query_end,
    key, value, feats, spread, gate_spread, sent, sems,
):
    bands = (pos.shape[0] - 1) // 2
    peers, slots, rows, half_side = sent.shape
    own = (slots - 1) // 3
    chans, tokens = key.shape
    total = peers * tokens
    pairs = [
        (pos_hbm, pos),
        (phase_hbm, phase),
        (mix_hbm, mix),
        (mix_phase_hbm, mix_phase),
        (out_hbm, out_cols),
        (decay_hbm, decay),
        (taps_hbm, taps),
        (query_hbm.at[:, tokens - half_side : tokens], query_end),
        (key_hbm, key),
        (value_hbm, value),
    ]
    copies = [
        pltpu.make_async_copy(source, target, sems.at[at])
        for at, (source, target) in enumerate(pairs)
    ]
    for copy in copies:
        copy.start()
    near = tokens // 2
    base = place[0] * near
    feats[...] = feature_stack(base, bands, near, total)
    for copy in copies[:6]:
        copy.wait()
    two_w = network_weights(pos, phase, mix, mix_phase, w_one)
    out_w = weight_stack(out_cols[...])
    decay_rate = -1.0 / column(decay[...])
    fine = jnp.exp(lax.broadcasted_iota(jnp.int32, (1, half_side), 1).astype(F32) * decay_rate)
    raw = dot_t(out_w, value_stack(hidden_units(feats[...], weight_stack(w_one[...]), two_w)))
    for sub in range(0, near, half_side):
        row_at, half = divmod(sub // half_side, 2)
        coarse = jnp.exp((base + sub).astype(F32) * decay_rate)
        spread[pl.ds(row_at + half * rows // 2, chans, stride=rows), :] = raw[
            :, sub : sub + half_side
        ] * (coarse * fine + 0.1)
    sent[:, 2 * own : 3 * own] = spread[...].reshape(peers, own, rows, half_side).astype(BF16)
    leaving = [
        pltpu.make_async_copy(
            sent.at[:, 2 * own : 3 * own], sent_hbm.at[:, 2 * own : 3 * own], sems.at[len(pairs)]
        )
    ]
    leaving[0].start()
    for copy in copies[6:]:
        copy.wait()
    columns = [[column(taps[which, i : i + 1, :]) for i in range(3)] for which in (1, 2)]
    group = 16
    lane = lax.broadcasted_iota(jnp.int32, (group, half_side), 1)
    ends = jnp.zeros((group, half_side), F32)
    for part in range(chans // group):
        moved = pltpu.roll(
            query_end[part * group : (part + 1) * group, :].astype(F32), 10 + 2 * part, 1
        )
        ends = jnp.where(lane // 2 == 4 + part, moved, ends)
    for part in range(chans // group):
        pick = slice(part * group, (part + 1) * group)
        edge = ends
        for at, (array, tap) in enumerate(((key, columns[0]), (value, columns[1]))):
            zero, one, two = (each[pick, :] for each in tap)
            head = array[pick, 0:half_side].astype(F32)
            last = array[pick, tokens - half_side : tokens].astype(F32)
            started = two * head + jnp.where(lane == 1, one * pltpu.roll(head, 1, 1), 0.0)
            ended = zero * last + jnp.where(
                lane == half_side - 2, one * pltpu.roll(last, half_side - 1, 1), 0.0
            )
            edge = jnp.where(lane // 2 == at, pltpu.roll(started, 2 * at, 1), edge)
            edge = jnp.where(lane // 2 == 2 + at, pltpu.roll(ended, 6 + 2 * at, 1), edge)
        edge = edge.astype(BF16)
        for peer in range(part * group // own, (part + 1) * group // own):
            sent[peer, slots - 1] = edge
    for at in range(0, chans, group):
        pick = slice(at, at + group)
        gated = short(key[pick, :].astype(F32), [tap[pick, :] for tap in columns[0]]) * short(
            value[pick, :].astype(F32), [tap[pick, :] for tap in columns[1]]
        )
        for sub in range(0, tokens, half_side):
            row_at, half = divmod(sub // half_side, 2)
            gate_spread[half, pl.ds(at * rows + row_at, group, stride=rows), :] = gated[
                :, sub : sub + half_side
            ]
        for half in range(2):
            sent[at // own : (at + group) // own, half * own : (half + 1) * own] = (
                gate_spread[half, at * rows : (at + group) * rows, :]
                .reshape(group // own, own, rows, half_side)
                .astype(BF16)
            )
        to = slice(at // own, (at + group) // own)
        leaving.append(
            pltpu.make_async_copy(
                sent.at[to, 0 : 2 * own],
                sent_hbm.at[to, 0 : 2 * own],
                sems.at[len(pairs) + 1 + at // group],
            )
        )
        leaving[-1].start()
    leaving.append(
        pltpu.make_async_copy(
            sent.at[:, slots - 1 : slots], sent_hbm.at[:, slots - 1 : slots], sems.at[len(pairs) + 5]
        )
    )
    leaving[-1].start()
    for copy in leaving:
        copy.wait()


def first_gated(edges, place, own):
    choices = edges.shape[1] // own
    here = jnp.zeros((edges.shape[0], own, edges.shape[2]), F32)
    for choice in range(choices):
        wanted = jnp.broadcast_to(lax.rem(place, choices), here.shape) == choice
        here = jnp.where(wanted, edges[:, choice * own : (choice + 1) * own, :], here)
    before = jnp.concatenate([jnp.zeros_like(here[:1]), here[:-1]], axis=0)
    lanes = here.shape[2]
    shorts = here + pltpu.roll(before, lanes - 4, 2)
    return shorts * pltpu.roll(shorts, lanes - 2, 2)


def conv_kernel(
    place, skip, got, far, left, back, right, twist_re, twist_im, mixed,
):
    side = SIDE
    peers, slots, rows, half_side = got.shape
    own = (slots - 1) // 3
    firsts = first_gated(got[:, slots - 1].astype(F32), place[0], own)
    t_re = twist_re[...]
    t_im = twist_im[...]
    spot = (lax.broadcasted_iota(jnp.int32, (peers, rows, half_side), 1) == 0) & (
        lax.broadcasted_iota(jnp.int32, (peers, rows, half_side), 2) < 2
    )
    group = GROUP
    for at in range(0, own, group):
        data, filt = [], []
        for slot in range(at, at + group):
            head = jnp.where(spot, firsts[:, slot : slot + 1, :], got[:, slot].astype(F32))
            head = head.astype(BF16)
            data.append(
                jnp.concatenate(
                    [head.reshape(side, half_side), got[:, own + slot].reshape(side, half_side)],
                    axis=1,
                )
            )
            near = got[:, 2 * own + slot].astype(F32)
            near = [
                near[:, half * rows // 2 : (half + 1) * rows // 2].reshape(side // 2, half_side)
                for half in range(2)
            ]
            filt.append(
                jnp.concatenate(
                    [
                        jnp.concatenate(near, axis=1).astype(BF16),
                        jnp.concatenate([far[slot, 0], far[slot, 1]], axis=1),
                    ],
                    axis=0,
                )
            )
        both = jnp.concatenate(data + filt, axis=1)
        first = dot(left[...], jnp.concatenate([both, both], axis=0))
        turned = []
        for at_col in range(0, 2 * group * side, side):
            re, im = first[:side, at_col : at_col + side], first[side:, at_col : at_col + side]
            turned.append(
                jnp.concatenate([re * t_re - im * t_im, re * t_im + im * t_re], axis=1).astype(BF16)
            )
        spec = dot(jnp.concatenate(turned, axis=0), right[...])
        edge_row = group * side
        d_re, d_im = spec[:edge_row, :side], spec[:edge_row, side:]
        f_re, f_im = spec[edge_row:, :side], spec[edge_row:, side:]
        product = jnp.concatenate([d_re * f_im + d_im * f_re, d_re * f_re - d_im * f_im], axis=1)
        inner = dot(product.astype(BF16), right[...])
        turned = []
        for at_row in range(0, group * side, side):
            im, re = inner[at_row : at_row + side, :side], inner[at_row : at_row + side, side:]
            turned.append(jnp.concatenate([re * t_re + im * t_im, im * t_re - re * t_im], axis=0))
        high, low = split(jnp.concatenate(turned, axis=1))
        values = dot(back[...], jnp.concatenate([high, high], axis=0))
        values = values + dot(back[:, : 2 * side], low)
        for index in range(group):
            wide = filt[index].astype(F32)
            energy = jnp.sum(jnp.sum(wide * wide, axis=1, keepdims=True), axis=0, keepdims=True)
            unit = lax.rsqrt(energy + EPSILON) * (1.0 / (side * side))
            lane = lax.broadcasted_iota(jnp.int32, skip.shape, 1)
            here = lane == place[0] * own + at + index
            direct = jnp.sum(jnp.where(here, skip[...], 0.0), axis=1, keepdims=True)
            skipped = direct * data[index].astype(F32)
            result = values[:, index * side : (index + 1) * side] * unit + skipped
            mixed[:, at + index] = result.astype(BF16).reshape(peers, rows, side)


def out_kernel(place, query, taps, got, mixed, gain, gated_out, sums, q_short, spread, total):
    peers, own, rows, side = mixed.shape
    chans = peers * own
    half_side = side // 2
    before = jnp.maximum(place[0] - 1, 0)
    tails = got[before, got.shape[1] - 1].astype(F32)
    tails = jnp.where(jnp.broadcast_to(place[0], tails.shape) > 0, tails, 0.0)
    group = tails.shape[0]
    columns = [column(taps[0, i : i + 1, :]) for i in range(3)]
    for part in range(chans // group):
        pick = slice(part * group, (part + 1) * group)
        tap = [each[pick, :] for each in columns]
        current = query[pick, :].astype(F32)
        q_short[pick, :] = short(current, tap)
        two, one = tails[:, 8 + 2 * part : 9 + 2 * part], tails[:, 9 + 2 * part : 10 + 2 * part]
        q_short[pick, 0:1] = tap[0] * two + tap[1] * one + tap[2] * current[:, 0:1]
        q_short[pick, 1:2] = tap[0] * one + tap[1] * current[:, 0:1] + tap[2] * current[:, 1:2]
    gains = column(gain[...])
    for half in range(2):
        spread[half] = (
            mixed[:, :, :, half * half_side : (half + 1) * half_side]
            .astype(F32)
            .reshape(chans * rows, half_side)
        )
    for at in range(0, q_short.shape[1], half_side):
        row, half = divmod(at // half_side, 2)
        piece = q_short[:, at : at + half_side] * spread[half, pl.ds(row, chans, stride=rows), :]
        gated_out[:, at : at + half_side] = piece * gains
        sum_row, lane = divmod(at, sums.shape[2])
        total[sum_row : sum_row + 1, lane : lane + half_side] = jnp.sum(
            piece * piece, axis=0, keepdims=True
        )
    for peer in range(sums.shape[0]):
        sums[peer] = total[...].astype(BF16)


def scale_kernel(gated_out, sums, result):
    group = result.shape[0]
    width = sums.shape[2]
    energy = jnp.sum(sums[...].astype(F32), axis=0)
    channels = gated_out.shape[0] * sums.shape[0]
    scale = lax.rsqrt(energy / channels + EPSILON)
    begin = pl.multiple_of(pl.program_id(0) * group, group)
    for row in range(sums.shape[1]):
        at = row * width
        piece = gated_out[pl.ds(begin, group), at : at + width]
        result[:, at : at + width] = (piece * scale[row : row + 1, :]).astype(BF16)


def whole(shape, memory_space=None):
    return pl.BlockSpec(shape, lambda *_: (0,) * len(shape), memory_space=memory_space)


SCALAR = pl.BlockSpec(memory_space=pltpu.SMEM)
VECTOR = pl.BlockSpec(memory_space=pltpu.VMEM)
OUTSIDE = pl.BlockSpec(memory_space=pltpu.HBM)


def in_hbm(array):
    return pltpu.with_memory_space_constraint(array, pltpu.HBM)


def params(mebibytes):
    return pltpu.CompilerParams(vmem_limit_bytes=mebibytes * 1024 * 1024)


def shards(
    query_act,
    key_act,
    value_act,
    short_taps,
    pos_proj,
    pos_phase,
    mix_proj,
    mix_phase,
    filter_out,
    decay_len,
    skip_gain,
    out_gain,
):
    chans, tokens = query_act.shape
    peers = lax.axis_size("ctx")
    groups = lax.axis_size("ch")
    place = lax.axis_index("ctx").astype(jnp.int32).reshape(1)
    own = chans // peers
    rows = tokens // SIDE
    units = pos_proj.shape[1]
    half_side = SIDE // 2
    taps = jnp.transpose(short_taps, (0, 2, 1))
    bands = (pos_proj.shape[0] - 1) // 2
    network = [
        pltpu.VMEM(pos_proj.shape, F32),
        pltpu.VMEM((1, units), F32),
        pltpu.VMEM(mix_proj.shape, F32),
        pltpu.VMEM((1, units), F32),
        pltpu.VMEM(filter_out.shape, F32),
        pltpu.VMEM((1, chans), F32),
        pltpu.VMEM((bands * 3, units), F32),
    ]
    weights = [
        in_hbm(array)
        for array in (
            pos_proj, pos_phase[None], mix_proj, mix_phase[None], filter_out, decay_len[None]
        )
    ]
    sent_shape = (peers, 3 * own + 1, rows, half_side)
    sent = pl.pallas_call(
        send_kernel,
        out_shape=jax.ShapeDtypeStruct(sent_shape, BF16),
        in_specs=[SCALAR] + [OUTSIDE] * 10,
        out_specs=OUTSIDE,
        scratch_shapes=network
        + [
            pltpu.VMEM(taps.shape, F32),
            pltpu.VMEM((chans, half_side), BF16),
            pltpu.VMEM((chans, tokens), BF16),
            pltpu.VMEM((chans, tokens), BF16),
            pltpu.VMEM((bands * 9, tokens // 2), BF16),
            pltpu.VMEM((chans * rows, half_side), F32),
            pltpu.VMEM((2, chans * rows, half_side), F32),
            pltpu.VMEM(sent_shape, BF16),
            pltpu.SemaphoreType.DMA((16,)),
        ],
        compiler_params=params(24),
        name="send",
    )(place, *weights, *map(in_hbm, (taps, query_act, key_act, value_act)))
    far_rows = SIDE // 2
    far, gain, skip = pl.pallas_call(
        far_kernel,
        out_shape=(
            jax.ShapeDtypeStruct((own, 2, far_rows, half_side), BF16),
            jax.ShapeDtypeStruct((1, chans), F32),
            jax.ShapeDtypeStruct((1, chans), F32),
        ),
        in_specs=[SCALAR] + [OUTSIDE] * 8,
        out_specs=(VECTOR,) * 3,
        scratch_shapes=network
        + [
            pltpu.VMEM((bands * 9, FAR_STEP), BF16),
            pltpu.VMEM((2, 8 * far_rows, half_side), F32),
            pltpu.SemaphoreType.DMA((8,)),
        ],
        compiler_params=params(16),
        cost_estimate=pl.CostEstimate(
            flops=10_000_000_000, transcendentals=0, bytes_accessed=1_000_000
        ),
        name="far_taps",
    )(place, *weights, in_hbm(out_gain[None]), in_hbm(skip_gain[None]))
    got = lax.all_to_all(sent, "ctx", split_axis=0, concat_axis=0, tiled=True)
    tables = [jnp.asarray(t) for t in transform_tables(SIDE)]
    mixed = pl.pallas_call(
        conv_kernel,
        out_shape=jax.ShapeDtypeStruct((peers, own, rows, SIDE), BF16),
        in_specs=[SCALAR] + [VECTOR] * (3 + len(tables)),
        out_specs=VECTOR,
        compiler_params=params(24),
        name="long_conv",
    )(place, skip, got, far, *tables)
    mixed = lax.all_to_all(mixed, "ctx", split_axis=0, concat_axis=0, tiled=True)
    width = SIDE
    gated_out, sums = pl.pallas_call(
        out_kernel,
        out_shape=(
            jax.ShapeDtypeStruct((chans, tokens), F32),
            jax.ShapeDtypeStruct((groups, tokens // width, width), BF16),
        ),
        in_specs=[SCALAR] + [VECTOR] * 5,
        out_specs=(VECTOR, VECTOR),
        scratch_shapes=[
            pltpu.VMEM((chans, tokens), F32),
            pltpu.VMEM((2, chans * rows, half_side), F32),
            pltpu.VMEM((tokens // width, width), F32),
        ],
        compiler_params=params(16),
        name="gate_out",
    )(place, query_act, taps, got, mixed, gain)
    sums = lax.all_to_all(sums, "ch", split_axis=0, concat_axis=0, tiled=True)
    group = chans // 2
    wide = pl.BlockSpec((group, tokens), lambda i: (i, 0))
    return pl.pallas_call(
        scale_kernel,
        out_shape=jax.ShapeDtypeStruct((chans, tokens), BF16),
        grid=(chans // group,),
        in_specs=[VECTOR, VECTOR],
        out_specs=wide,
        compiler_params=params(16),
        name="norm_out",
    )(gated_out, sums)


def solution(mesh):
    return jax.shard_map(
        shards,
        mesh=mesh,
        in_specs=(
            P("ch", "ctx"),
            P("ch", "ctx"),
            P("ch", "ctx"),
            P(None, "ch", None),
            P(),
            P(),
            P(),
            P(),
            P(None, "ch"),
            P("ch"),
            P("ch"),
            P("ch"),
        ),
        out_specs=P("ch", "ctx"),
        check_vma=False,
    )
```

```python
import math

import ml_dtypes
import numpy as np

import jax
import jax.numpy as jnp
from jax import lax
from jax.experimental import pallas as pl
from jax.experimental.pallas import tpu as pltpu
from jax.sharding import PartitionSpec as P

EPSILON = 1e-06
F32 = jnp.float32
BF16 = jnp.bfloat16
SIDE = 256
GROUP = 2
FAR_STEP = 8192
FAR_SETS = 4
COS_COEFS = (
    -6.283164044920963,
    41.337142429298574,
    -81.34077038150495,
    70.99344453177132,
)


def cos_turns(turns):
    rest = turns - lax.round(turns, lax.RoundingMethod.TO_NEAREST_EVEN)
    quarter = jnp.abs(rest) - 0.25
    square = quarter * quarter
    acc = jnp.full_like(quarter, COS_COEFS[-1])
    for coef in COS_COEFS[-2::-1]:
        acc = acc * square + coef
    return acc * quarter


def split(array):
    high = array.astype(BF16)
    low = (array - high.astype(F32)).astype(BF16)
    return high, low


def dot(lhs, rhs):
    return lax.dot_general(lhs, rhs, (((1,), (0,)), ((), ())), preferred_element_type=F32)


def dot_t(lhs, rhs):
    return lax.dot_general(lhs, rhs, (((0,), (0,)), ((), ())), preferred_element_type=F32)


def weight_stack(weights):
    high, low = split(weights)
    return jnp.concatenate([high, high, low], axis=0)


def value_stack(values):
    high, low = split(values)
    return jnp.concatenate([high, low, high], axis=0)


def column(row):
    size = row.shape[1]
    eye = lax.broadcasted_iota(jnp.int32, (size, size), 0) == lax.broadcasted_iota(
        jnp.int32, (size, size), 1
    )
    return jnp.sum(jnp.where(eye, jnp.broadcast_to(row, (size, size)), 0.0), axis=1, keepdims=True)


def np_split(array):
    high = array.astype(np.float32).astype(ml_dtypes.bfloat16)
    low = (array - high.astype(np.float64)).astype(np.float32).astype(ml_dtypes.bfloat16)
    return high, low


def stacked(array):
    high, low = np_split(array)
    return np.concatenate([high, low], axis=1)


def transform_tables(side):
    total = side * side
    ids = np.arange(side)
    first = np.exp(-2j * np.pi * np.outer(ids - 0.25, ids) / side)
    twist = np.exp(-2j * np.pi * np.outer(ids - 0.25, ids) / total)
    second = np.exp(-2j * np.pi * (np.outer(ids, ids) % side) / side)
    left = np.concatenate([first.real, first.imag], axis=0)
    right = np.block([[second.real, second.imag], [-second.imag, second.real]])
    return (
        stacked(left),
        np.concatenate([np_split(left.T)[0], stacked(left.T)], axis=1),
        np_split(right)[0],
        twist.real.astype(np.float32),
        twist.imag.astype(np.float32),
    )


def feature_stack(base, bands, step, total):
    times = base + lax.broadcasted_iota(jnp.int32, (bands, step), 1)
    row = lax.broadcasted_iota(jnp.int32, (bands, step), 0)
    freqs = jnp.left_shift(jnp.ones((bands, step), jnp.int32), row)
    turns = ((freqs * times) & (total - 1)).astype(F32) * (1.0 / total)
    extra = jnp.where(row == 0, times.astype(F32) * (1.0 / total), jnp.where(row == 1, 1.0, 0.0))
    return value_stack(
        jnp.concatenate([cos_turns(turns), cos_turns(turns - 0.25), extra], axis=0)
    )


def network_weights(pos, phase, mix, mix_phase, w_one):
    bands = (pos.shape[0] - 1) // 2
    inv_turn = 1.0 / (2.0 * math.pi)
    w_one[...] = jnp.zeros_like(w_one)
    w_one[0 : 2 * bands, :] = pos[1 : 2 * bands + 1, :] * inv_turn
    w_one[2 * bands : 2 * bands + 1, :] = pos[0:1, :] * inv_turn
    w_one[2 * bands + 1 : 2 * bands + 2, :] = phase[...] * inv_turn - 0.25
    row = lax.broadcasted_iota(jnp.int32, (bands, w_one.shape[1]), 0)
    high, low = split(mix_phase[...] * inv_turn - 0.25)
    bias = jnp.where(row == 0, high.astype(F32), jnp.where(row == 1, low.astype(F32), 0.0))
    return jnp.concatenate([weight_stack(mix[...] * inv_turn), bias.astype(BF16)], axis=0)


def hidden_units(feats, one_w, two_w):
    hidden = value_stack(cos_turns(dot_t(one_w, feats)))
    ones = jnp.ones((two_w.shape[0] - hidden.shape[0], hidden.shape[1]), BF16)
    return cos_turns(dot_t(two_w, jnp.concatenate([hidden, ones], axis=0)))


def far_kernel(
    place, pos_hbm, phase_hbm, mix_hbm, mix_phase_hbm, out_hbm, decay_hbm, gain_hbm, skip_hbm, far,
    gain, skip, pos, phase, mix, mix_phase, out_cols, decay, w_one, feats, spread, sems,
):
    bands = (pos.shape[0] - 1) // 2
    own, _, rows, half_side = far.shape
    begin = rows * SIDE
    total = 2 * begin
    pairs = [
        (pos_hbm, pos),
        (phase_hbm, phase),
        (mix_hbm, mix),
        (mix_phase_hbm, mix_phase),
        (out_hbm, out_cols),
        (decay_hbm, decay),
        (gain_hbm, gain),
        (skip_hbm, skip),
    ]
    copies = [
        pltpu.make_async_copy(source, target, sems.at[at])
        for at, (source, target) in enumerate(pairs)
    ]
    for copy in copies:
        copy.start()
    step = FAR_STEP
    feats[...] = feature_stack(0, bands, step, total)
    for copy in copies:
        copy.wait()
    two_w = network_weights(pos, phase, mix, mix_phase, w_one)
    cos_w = w_one[0:bands, :]
    sin_w = w_one[bands : 2 * bands, :]
    slope = w_one[2 * bands : 2 * bands + 1, :]
    level = w_one[2 * bands + 1 : 2 * bands + 2, :]
    freqs = jnp.left_shift(
        jnp.ones((bands, 1), jnp.int32), lax.broadcasted_iota(jnp.int32, (bands, 1), 0)
    )
    lane = lax.broadcasted_iota(jnp.int32, out_cols.shape, 1)
    units = out_cols.shape[0]
    narrow = lax.broadcasted_iota(jnp.int32, (units, FAR_SETS * 16), 1)
    tall = lax.broadcasted_iota(jnp.int32, (8, 1), 0)
    cols = jnp.zeros(narrow.shape, F32)
    rate = jnp.zeros(tall.shape, F32)
    decay_rate = -1.0 / decay[...]
    for slot in range(own):
        here = lane == place[0] * own + slot
        col = jnp.sum(jnp.where(here, out_cols[...], 0.0), axis=1, keepdims=True)
        cols = jnp.where(lax.rem(narrow, 8) == slot, col, cols)
        one_rate = jnp.sum(jnp.where(here[0:1, :], decay_rate, 0.0), axis=1, keepdims=True)
        rate = jnp.where(tall == slot, one_rate, rate)
    high, low = split(cols)
    cols = jnp.where(lax.rem(narrow, 16) < 8, high.astype(F32), low.astype(F32))
    out_w = jnp.concatenate(
        [jnp.where(narrow // 16 == part, cols, 0.0) for part in range(FAR_SETS)], axis=0
    ).astype(BF16)
    fine = jnp.exp(lax.broadcasted_iota(jnp.int32, (1, half_side), 1).astype(F32) * rate)
    step = FAR_STEP

    def chunk(index, carry):
        base = begin + index * step
        turns = ((freqs * base) & (total - 1)).astype(F32) * (1.0 / total)
        cosine, sine = cos_turns(turns), cos_turns(turns - 0.25)
        w_one[0:bands, :] = cos_w * cosine + sin_w * sine
        w_one[bands : 2 * bands, :] = sin_w * cosine - cos_w * sine
        w_one[2 * bands + 1 : 2 * bands + 2, :] = level + slope * (base.astype(F32) * (1.0 / total))
        hidden = hidden_units(feats[...], weight_stack(w_one[...]), two_w).astype(BF16)
        width = step // FAR_SETS
        parts = [hidden[:, part * width : (part + 1) * width] for part in range(FAR_SETS)]
        both = dot_t(out_w, jnp.concatenate(parts, axis=0))
        for sub in range(0, step, half_side):
            row_at, half = divmod(sub // half_side, 2)
            coarse = jnp.exp((base + sub).astype(F32) * rate)
            row = index * (step // SIDE) + row_at
            part, lanes = divmod(sub, width)
            raw = (
                both[part * 16 : part * 16 + 8, lanes : lanes + half_side]
                + both[part * 16 + 8 : part * 16 + 16, lanes : lanes + half_side]
            )
            spread[half, pl.ds(row, 8, stride=rows), :] = raw * (coarse * fine + 0.1)
        return carry

    lax.fori_loop(0, begin // step, chunk, 0, unroll=2)
    for slot in range(own):
        for half in range(2):
            far[slot, half] = spread[half, slot * rows : (slot + 1) * rows, :].astype(BF16)


def short(current, taps):
    return (
        taps[0] * pltpu.roll(current, 2, 1)
        + taps[1] * pltpu.roll(current, 1, 1)
        + taps[2] * current
    )


def send_kernel(
    place, pos_hbm, phase_hbm, mix_hbm, mix_phase_hbm, out_hbm, decay_hbm, taps_hbm, query_hbm,
    key_hbm, value_hbm, sent_hbm, pos, phase, mix, mix_phase, out_cols, decay, w_one, taps, query_end,
    key, value, feats, spread, gate_spread, sent, sems,
):
    bands = (pos.shape[0] - 1) // 2
    peers, slots, rows, half_side = sent.shape
    own = (slots - 1) // 3
    chans, tokens = key.shape
    total = peers * tokens
    pairs = [
        (pos_hbm, pos),
        (phase_hbm, phase),
        (mix_hbm, mix),
        (mix_phase_hbm, mix_phase),
        (out_hbm, out_cols),
        (decay_hbm, decay),
        (taps_hbm, taps),
        (query_hbm.at[:, tokens - half_side : tokens], query_end),
        (key_hbm, key),
        (value_hbm, value),
    ]
    copies = [
        pltpu.make_async_copy(source, target, sems.at[at])
        for at, (source, target) in enumerate(pairs)
    ]
    for copy in copies:
        copy.start()
    near = tokens // 2
    base = place[0] * near
    feats[...] = feature_stack(base, bands, near, total)
    for copy in copies[:6]:
        copy.wait()
    two_w = network_weights(pos, phase, mix, mix_phase, w_one)
    out_w = weight_stack(out_cols[...])
    decay_rate = -1.0 / column(decay[...])
    fine = jnp.exp(lax.broadcasted_iota(jnp.int32, (1, half_side), 1).astype(F32) * decay_rate)
    raw = dot_t(out_w, value_stack(hidden_units(feats[...], weight_stack(w_one[...]), two_w)))
    for sub in range(0, near, half_side):
        row_at, half = divmod(sub // half_side, 2)
        coarse = jnp.exp((base + sub).astype(F32) * decay_rate)
        spread[pl.ds(row_at + half * rows // 2, chans, stride=rows), :] = raw[
            :, sub : sub + half_side
        ] * (coarse * fine + 0.1)
    sent[:, 2 * own : 3 * own] = spread[...].reshape(peers, own, rows, half_side).astype(BF16)
    leaving = [
        pltpu.make_async_copy(
            sent.at[:, 2 * own : 3 * own], sent_hbm.at[:, 2 * own : 3 * own], sems.at[len(pairs)]
        )
    ]
    leaving[0].start()
    for copy in copies[6:]:
        copy.wait()
    columns = [[column(taps[which, i : i + 1, :]) for i in range(3)] for which in (1, 2)]
    group = 16
    lane = lax.broadcasted_iota(jnp.int32, (group, half_side), 1)
    ends = jnp.zeros((group, half_side), F32)
    for part in range(chans // group):
        moved = pltpu.roll(
            query_end[part * group : (part + 1) * group, :].astype(F32), 10 + 2 * part, 1
        )
        ends = jnp.where(lane // 2 == 4 + part, moved, ends)
    for part in range(chans // group):
        pick = slice(part * group, (part + 1) * group)
        edge = ends
        for at, (array, tap) in enumerate(((key, columns[0]), (value, columns[1]))):
            zero, one, two = (each[pick, :] for each in tap)
            head = array[pick, 0:half_side].astype(F32)
            last = array[pick, tokens - half_side : tokens].astype(F32)
            started = two * head + jnp.where(lane == 1, one * pltpu.roll(head, 1, 1), 0.0)
            ended = zero * last + jnp.where(
                lane == half_side - 2, one * pltpu.roll(last, half_side - 1, 1), 0.0
            )
            edge = jnp.where(lane // 2 == at, pltpu.roll(started, 2 * at, 1), edge)
            edge = jnp.where(lane // 2 == 2 + at, pltpu.roll(ended, 6 + 2 * at, 1), edge)
        edge = edge.astype(BF16)
        for peer in range(part * group // own, (part + 1) * group // own):
            sent[peer, slots - 1] = edge
    for at in range(0, chans, group):
        pick = slice(at, at + group)
        gated = short(key[pick, :].astype(F32), [tap[pick, :] for tap in columns[0]]) * short(
            value[pick, :].astype(F32), [tap[pick, :] for tap in columns[1]]
        )
        for sub in range(0, tokens, half_side):
            row_at, half = divmod(sub // half_side, 2)
            gate_spread[half, pl.ds(at * rows + row_at, group, stride=rows), :] = gated[
                :, sub : sub + half_side
            ]
        for half in range(2):
            sent[at // own : (at + group) // own, half * own : (half + 1) * own] = (
                gate_spread[half, at * rows : (at + group) * rows, :]
                .reshape(group // own, own, rows, half_side)
                .astype(BF16)
            )
        to = slice(at // own, (at + group) // own)
        leaving.append(
            pltpu.make_async_copy(
                sent.at[to, 0 : 2 * own],
                sent_hbm.at[to, 0 : 2 * own],
                sems.at[len(pairs) + 1 + at // group],
            )
        )
        leaving[-1].start()
    leaving.append(
        pltpu.make_async_copy(
            sent.at[:, slots - 1 : slots], sent_hbm.at[:, slots - 1 : slots], sems.at[len(pairs) + 5]
        )
    )
    leaving[-1].start()
    for copy in leaving:
        copy.wait()


def first_gated(edges, place, own):
    choices = edges.shape[1] // own
    here = jnp.zeros((edges.shape[0], own, edges.shape[2]), F32)
    for choice in range(choices):
        wanted = jnp.broadcast_to(lax.rem(place, choices), here.shape) == choice
        here = jnp.where(wanted, edges[:, choice * own : (choice + 1) * own, :], here)
    before = jnp.concatenate([jnp.zeros_like(here[:1]), here[:-1]], axis=0)
    lanes = here.shape[2]
    shorts = here + pltpu.roll(before, lanes - 4, 2)
    return shorts * pltpu.roll(shorts, lanes - 2, 2)


def conv_kernel(
    place, skip, got, far, left, back, right, twist_re, twist_im, mixed,
):
    side = SIDE
    peers, slots, rows, half_side = got.shape
    own = (slots - 1) // 3
    firsts = first_gated(got[:, slots - 1].astype(F32), place[0], own)
    t_re = twist_re[...]
    t_im = twist_im[...]
    spot = (lax.broadcasted_iota(jnp.int32, (peers, rows, half_side), 1) == 0) & (
        lax.broadcasted_iota(jnp.int32, (peers, rows, half_side), 2) < 2
    )
    group = GROUP
    for at in range(0, own, group):
        data, filt = [], []
        for slot in range(at, at + group):
            head = jnp.where(spot, firsts[:, slot : slot + 1, :], got[:, slot].astype(F32))
            head = head.astype(BF16)
            data.append(
                jnp.concatenate(
                    [head.reshape(side, half_side), got[:, own + slot].reshape(side, half_side)],
                    axis=1,
                )
            )
            near = got[:, 2 * own + slot].astype(F32)
            near = [
                near[:, half * rows // 2 : (half + 1) * rows // 2].reshape(side // 2, half_side)
                for half in range(2)
            ]
            filt.append(
                jnp.concatenate(
                    [
                        jnp.concatenate(near, axis=1).astype(BF16),
                        jnp.concatenate([far[slot, 0], far[slot, 1]], axis=1),
                    ],
                    axis=0,
                )
            )
        both = jnp.concatenate(data + filt, axis=1)
        first = dot(left[...], jnp.concatenate([both, both], axis=0))
        turned = []
        for at_col in range(0, 2 * group * side, side):
            re, im = first[:side, at_col : at_col + side], first[side:, at_col : at_col + side]
            turned.append(
                jnp.concatenate([re * t_re - im * t_im, re * t_im + im * t_re], axis=1).astype(BF16)
            )
        spec = dot(jnp.concatenate(turned, axis=0), right[...])
        edge_row = group * side
        d_re, d_im = spec[:edge_row, :side], spec[:edge_row, side:]
        f_re, f_im = spec[edge_row:, :side], spec[edge_row:, side:]
        product = jnp.concatenate([d_re * f_im + d_im * f_re, d_re * f_re - d_im * f_im], axis=1)
        inner = dot(product.astype(BF16), right[...])
        turned = []
        for at_row in range(0, group * side, side):
            im, re = inner[at_row : at_row + side, :side], inner[at_row : at_row + side, side:]
            turned.append(jnp.concatenate([re * t_re + im * t_im, im * t_re - re * t_im], axis=0))
        high, low = split(jnp.concatenate(turned, axis=1))
        values = dot(back[...], jnp.concatenate([high, low, high], axis=0))
        for index in range(group):
            wide = filt[index].astype(F32)
            energy = jnp.sum(jnp.sum(wide * wide, axis=1, keepdims=True), axis=0, keepdims=True)
            unit = lax.rsqrt(energy + EPSILON) * (1.0 / (side * side))
            lane = lax.broadcasted_iota(jnp.int32, skip.shape, 1)
            here = lane == place[0] * own + at + index
            direct = jnp.sum(jnp.where(here, skip[...], 0.0), axis=1, keepdims=True)
            skipped = direct * data[index].astype(F32)
            result = values[:, index * side : (index + 1) * side] * unit + skipped
            mixed[:, at + index] = result.astype(BF16).reshape(peers, rows, side)


def out_kernel(place, query, taps, got, mixed, gain, gated_out, sums, q_short, spread, total):
    peers, own, rows, side = mixed.shape
    chans = peers * own
    half_side = side // 2
    before = jnp.maximum(place[0] - 1, 0)
    tails = got[before, got.shape[1] - 1].astype(F32)
    tails = jnp.where(jnp.broadcast_to(place[0], tails.shape) > 0, tails, 0.0)
    group = tails.shape[0]
    columns = [column(taps[0, i : i + 1, :]) for i in range(3)]
    for part in range(chans // group):
        pick = slice(part * group, (part + 1) * group)
        tap = [each[pick, :] for each in columns]
        current = query[pick, :].astype(F32)
        q_short[pick, :] = short(current, tap)
        two, one = tails[:, 8 + 2 * part : 9 + 2 * part], tails[:, 9 + 2 * part : 10 + 2 * part]
        q_short[pick, 0:1] = tap[0] * two + tap[1] * one + tap[2] * current[:, 0:1]
        q_short[pick, 1:2] = tap[0] * one + tap[1] * current[:, 0:1] + tap[2] * current[:, 1:2]
    gains = column(gain[...])
    for half in range(2):
        spread[half] = (
            mixed[:, :, :, half * half_side : (half + 1) * half_side]
            .astype(F32)
            .reshape(chans * rows, half_side)
        )
    for at in range(0, q_short.shape[1], half_side):
        row, half = divmod(at // half_side, 2)
        piece = q_short[:, at : at + half_side] * spread[half, pl.ds(row, chans, stride=rows), :]
        gated_out[:, at : at + half_side] = piece * gains
        sum_row, lane = divmod(at, sums.shape[2])
        total[sum_row : sum_row + 1, lane : lane + half_side] = jnp.sum(
            piece * piece, axis=0, keepdims=True
        )
    for peer in range(sums.shape[0]):
        sums[peer] = total[...].astype(BF16)


def scale_kernel(gated_out, sums, result):
    group = result.shape[0]
    width = sums.shape[2]
    energy = jnp.sum(sums[...].astype(F32), axis=0)
    channels = gated_out.shape[0] * sums.shape[0]
    scale = lax.rsqrt(energy / channels + EPSILON)
    begin = pl.multiple_of(pl.program_id(0) * group, group)
    for row in range(sums.shape[1]):
        at = row * width
        piece = gated_out[pl.ds(begin, group), at : at + width]
        result[:, at : at + width] = (piece * scale[row : row + 1, :]).astype(BF16)


def whole(shape, memory_space=None):
    return pl.BlockSpec(shape, lambda *_: (0,) * len(shape), memory_space=memory_space)


SCALAR = pl.BlockSpec(memory_space=pltpu.SMEM)
VECTOR = pl.BlockSpec(memory_space=pltpu.VMEM)
OUTSIDE = pl.BlockSpec(memory_space=pltpu.HBM)


def in_hbm(array):
    return pltpu.with_memory_space_constraint(array, pltpu.HBM)


def params(mebibytes):
    return pltpu.CompilerParams(vmem_limit_bytes=mebibytes * 1024 * 1024)


def shards(
    query_act,
    key_act,
    value_act,
    short_taps,
    pos_proj,
    pos_phase,
    mix_proj,
    mix_phase,
    filter_out,
    decay_len,
    skip_gain,
    out_gain,
):
    chans, tokens = query_act.shape
    peers = lax.axis_size("ctx")
    groups = lax.axis_size("ch")
    place = lax.axis_index("ctx").astype(jnp.int32).reshape(1)
    own = chans // peers
    rows = tokens // SIDE
    units = pos_proj.shape[1]
    half_side = SIDE // 2
    taps = jnp.transpose(short_taps, (0, 2, 1))
    bands = (pos_proj.shape[0] - 1) // 2
    network = [
        pltpu.VMEM(pos_proj.shape, F32),
        pltpu.VMEM((1, units), F32),
        pltpu.VMEM(mix_proj.shape, F32),
        pltpu.VMEM((1, units), F32),
        pltpu.VMEM(filter_out.shape, F32),
        pltpu.VMEM((1, chans), F32),
        pltpu.VMEM((bands * 3, units), F32),
    ]
    weights = [
        in_hbm(array)
        for array in (
            pos_proj, pos_phase[None], mix_proj, mix_phase[None], filter_out, decay_len[None]
        )
    ]
    sent_shape = (peers, 3 * own + 1, rows, half_side)
    sent = pl.pallas_call(
        send_kernel,
        out_shape=jax.ShapeDtypeStruct(sent_shape, BF16),
        in_specs=[SCALAR] + [OUTSIDE] * 10,
        out_specs=OUTSIDE,
        scratch_shapes=network
        + [
            pltpu.VMEM(taps.shape, F32),
            pltpu.VMEM((chans, half_side), BF16),
            pltpu.VMEM((chans, tokens), BF16),
            pltpu.VMEM((chans, tokens), BF16),
            pltpu.VMEM((bands * 9, tokens // 2), BF16),
            pltpu.VMEM((chans * rows, half_side), F32),
            pltpu.VMEM((2, chans * rows, half_side), F32),
            pltpu.VMEM(sent_shape, BF16),
            pltpu.SemaphoreType.DMA((16,)),
        ],
        compiler_params=params(24),
        name="send",
    )(place, *weights, *map(in_hbm, (taps, query_act, key_act, value_act)))
    far_rows = SIDE // 2
    far, gain, skip = pl.pallas_call(
        far_kernel,
        out_shape=(
            jax.ShapeDtypeStruct((own, 2, far_rows, half_side), BF16),
            jax.ShapeDtypeStruct((1, chans), F32),
            jax.ShapeDtypeStruct((1, chans), F32),
        ),
        in_specs=[SCALAR] + [OUTSIDE] * 8,
        out_specs=(VECTOR,) * 3,
        scratch_shapes=network
        + [
            pltpu.VMEM((bands * 9, FAR_STEP), BF16),
            pltpu.VMEM((2, 8 * far_rows, half_side), F32),
            pltpu.SemaphoreType.DMA((8,)),
        ],
        compiler_params=params(16),
        cost_estimate=pl.CostEstimate(
            flops=10_000_000_000, transcendentals=0, bytes_accessed=1_000_000
        ),
        name="far_taps",
    )(place, *weights, in_hbm(out_gain[None]), in_hbm(skip_gain[None]))
    got = lax.all_to_all(sent, "ctx", split_axis=0, concat_axis=0, tiled=True)
    tables = [jnp.asarray(t) for t in transform_tables(SIDE)]
    mixed = pl.pallas_call(
        conv_kernel,
        out_shape=jax.ShapeDtypeStruct((peers, own, rows, SIDE), BF16),
        in_specs=[SCALAR] + [VECTOR] * (3 + len(tables)),
        out_specs=VECTOR,
        compiler_params=params(24),
        name="long_conv",
    )(place, skip, got, far, *tables)
    mixed = lax.all_to_all(mixed, "ctx", split_axis=0, concat_axis=0, tiled=True)
    width = SIDE
    gated_out, sums = pl.pallas_call(
        out_kernel,
        out_shape=(
            jax.ShapeDtypeStruct((chans, tokens), F32),
            jax.ShapeDtypeStruct((groups, tokens // width, width), BF16),
        ),
        in_specs=[SCALAR] + [VECTOR] * 5,
        out_specs=(VECTOR, VECTOR),
        scratch_shapes=[
            pltpu.VMEM((chans, tokens), F32),
            pltpu.VMEM((2, chans * rows, half_side), F32),
            pltpu.VMEM((tokens // width, width), F32),
        ],
        compiler_params=params(16),
        name="gate_out",
    )(place, query_act, taps, got, mixed, gain)
    sums = lax.all_to_all(sums, "ch", split_axis=0, concat_axis=0, tiled=True)
    group = chans // 2
    wide = pl.BlockSpec((group, tokens), lambda i: (i, 0))
    return pl.pallas_call(
        scale_kernel,
        out_shape=jax.ShapeDtypeStruct((chans, tokens), BF16),
        grid=(chans // group,),
        in_specs=[VECTOR, VECTOR],
        out_specs=wide,
        compiler_params=params(16),
        name="norm_out",
    )(gated_out, sums)


def solution(mesh):
    return jax.shard_map(
        shards,
        mesh=mesh,
        in_specs=(
            P("ch", "ctx"),
            P("ch", "ctx"),
            P("ch", "ctx"),
            P(None, "ch", None),
            P(),
            P(),
            P(),
            P(),
            P(None, "ch"),
            P("ch"),
            P("ch"),
            P("ch"),
        ),
        out_specs=P("ch", "ctx"),
        check_vma=False,
    )
```

```python
import math

import ml_dtypes
import numpy as np

import jax
import jax.numpy as jnp
from jax import lax
from jax.experimental import pallas as pl
from jax.experimental.pallas import tpu as pltpu
from jax.sharding import PartitionSpec as P

EPSILON = 1e-06
F32 = jnp.float32
BF16 = jnp.bfloat16
SIDE = 256
GROUP = 2
FAR_STEP = 8192
FAR_SETS = 4
COS_COEFS = (
    -6.283164044920963,
    41.337142429298574,
    -81.34077038150495,
    70.99344453177132,
)


def cos_turns(turns):
    rest = turns - lax.round(turns, lax.RoundingMethod.TO_NEAREST_EVEN)
    quarter = jnp.abs(rest) - 0.25
    square = quarter * quarter
    acc = jnp.full_like(quarter, COS_COEFS[-1])
    for coef in COS_COEFS[-2::-1]:
        acc = acc * square + coef
    return acc * quarter


def split(array):
    high = array.astype(BF16)
    low = (array - high.astype(F32)).astype(BF16)
    return high, low


def dot(lhs, rhs):
    return lax.dot_general(lhs, rhs, (((1,), (0,)), ((), ())), preferred_element_type=F32)


def dot_t(lhs, rhs):
    return lax.dot_general(lhs, rhs, (((0,), (0,)), ((), ())), preferred_element_type=F32)


def weight_stack(weights):
    high, low = split(weights)
    return jnp.concatenate([high, high, low], axis=0)


def value_stack(values):
    high, low = split(values)
    return jnp.concatenate([high, low, high], axis=0)


def column(row):
    size = row.shape[1]
    eye = lax.broadcasted_iota(jnp.int32, (size, size), 0) == lax.broadcasted_iota(
        jnp.int32, (size, size), 1
    )
    return jnp.sum(jnp.where(eye, jnp.broadcast_to(row, (size, size)), 0.0), axis=1, keepdims=True)


def np_split(array):
    high = array.astype(np.float32).astype(ml_dtypes.bfloat16)
    low = (array - high.astype(np.float64)).astype(np.float32).astype(ml_dtypes.bfloat16)
    return high, low


def stacked(array):
    high, low = np_split(array)
    return np.concatenate([high, low], axis=1)


def transform_tables(side):
    total = side * side
    ids = np.arange(side)
    first = np.exp(-2j * np.pi * np.outer(ids - 0.25, ids) / side)
    twist = np.exp(-2j * np.pi * np.outer(ids - 0.25, ids) / total)
    second = np.exp(-2j * np.pi * (np.outer(ids, ids) % side) / side)
    left = np.concatenate([first.real, first.imag], axis=0)
    right = np.block([[second.real, second.imag], [-second.imag, second.real]])
    return (
        stacked(left),
        np.concatenate([np_split(left.T)[0], stacked(left.T)], axis=1),
        np_split(right)[0],
        twist.real.astype(np.float32),
        twist.imag.astype(np.float32),
    )


def feature_stack(base, bands, step, total):
    times = base + lax.broadcasted_iota(jnp.int32, (bands, step), 1)
    row = lax.broadcasted_iota(jnp.int32, (bands, step), 0)
    freqs = jnp.left_shift(jnp.ones((bands, step), jnp.int32), row)
    turns = ((freqs * times) & (total - 1)).astype(F32) * (1.0 / total)
    extra = jnp.where(row == 0, times.astype(F32) * (1.0 / total), jnp.where(row == 1, 1.0, 0.0))
    return value_stack(
        jnp.concatenate([cos_turns(turns), cos_turns(turns - 0.25), extra], axis=0)
    )


def network_weights(pos, phase, mix, mix_phase, w_one):
    bands = (pos.shape[0] - 1) // 2
    inv_turn = 1.0 / (2.0 * math.pi)
    w_one[...] = jnp.zeros_like(w_one)
    w_one[0 : 2 * bands, :] = pos[1 : 2 * bands + 1, :] * inv_turn
    w_one[2 * bands : 2 * bands + 1, :] = pos[0:1, :] * inv_turn
    w_one[2 * bands + 1 : 2 * bands + 2, :] = phase[...] * inv_turn - 0.25
    row = lax.broadcasted_iota(jnp.int32, (bands, w_one.shape[1]), 0)
    high, low = split(mix_phase[...] * inv_turn - 0.25)
    bias = jnp.where(row == 0, high.astype(F32), jnp.where(row == 1, low.astype(F32), 0.0))
    return jnp.concatenate([weight_stack(mix[...] * inv_turn), bias.astype(BF16)], axis=0)


def hidden_units(feats, one_w, two_w):
    hidden = value_stack(cos_turns(dot_t(one_w, feats)))
    ones = jnp.ones((two_w.shape[0] - hidden.shape[0], hidden.shape[1]), BF16)
    return cos_turns(dot_t(two_w, jnp.concatenate([hidden, ones], axis=0)))


def far_kernel(
    place, pos_hbm, phase_hbm, mix_hbm, mix_phase_hbm, out_hbm, decay_hbm, gain_hbm, skip_hbm, far,
    gain, skip, pos, phase, mix, mix_phase, out_cols, decay, w_one, feats, spread, sems,
):
    bands = (pos.shape[0] - 1) // 2
    own, _, rows, half_side = far.shape
    begin = rows * SIDE
    total = 2 * begin
    pairs = [
        (pos_hbm, pos),
        (phase_hbm, phase),
        (mix_hbm, mix),
        (mix_phase_hbm, mix_phase),
        (out_hbm, out_cols),
        (decay_hbm, decay),
        (gain_hbm, gain),
        (skip_hbm, skip),
    ]
    copies = [
        pltpu.make_async_copy(source, target, sems.at[at])
        for at, (source, target) in enumerate(pairs)
    ]
    for copy in copies:
        copy.start()
    step = FAR_STEP
    feats[...] = feature_stack(0, bands, step, total)
    for copy in copies:
        copy.wait()
    two_w = network_weights(pos, phase, mix, mix_phase, w_one)
    cos_w = w_one[0:bands, :]
    sin_w = w_one[bands : 2 * bands, :]
    slope = w_one[2 * bands : 2 * bands + 1, :]
    level = w_one[2 * bands + 1 : 2 * bands + 2, :]
    freqs = jnp.left_shift(
        jnp.ones((bands, 1), jnp.int32), lax.broadcasted_iota(jnp.int32, (bands, 1), 0)
    )
    lane = lax.broadcasted_iota(jnp.int32, out_cols.shape, 1)
    units = out_cols.shape[0]
    narrow = lax.broadcasted_iota(jnp.int32, (units, FAR_SETS * 16), 1)
    tall = lax.broadcasted_iota(jnp.int32, (8, 1), 0)
    cols = jnp.zeros(narrow.shape, F32)
    rate = jnp.zeros(tall.shape, F32)
    decay_rate = -1.0 / decay[...]
    for slot in range(own):
        here = lane == place[0] * own + slot
        col = jnp.sum(jnp.where(here, out_cols[...], 0.0), axis=1, keepdims=True)
        cols = jnp.where(lax.rem(narrow, 8) == slot, col, cols)
        one_rate = jnp.sum(jnp.where(here[0:1, :], decay_rate, 0.0), axis=1, keepdims=True)
        rate = jnp.where(tall == slot, one_rate, rate)
    high, low = split(cols)
    cols = jnp.where(lax.rem(narrow, 16) < 8, high.astype(F32), low.astype(F32))
    out_w = jnp.concatenate(
        [jnp.where(narrow // 16 == part, cols, 0.0) for part in range(FAR_SETS)], axis=0
    ).astype(BF16)
    fine = jnp.exp(lax.broadcasted_iota(jnp.int32, (1, half_side), 1).astype(F32) * rate)
    step = FAR_STEP

    def chunk(index, carry):
        base = begin + index * step
        turns = ((freqs * base) & (total - 1)).astype(F32) * (1.0 / total)
        cosine, sine = cos_turns(turns), cos_turns(turns - 0.25)
        w_one[0:bands, :] = cos_w * cosine + sin_w * sine
        w_one[bands : 2 * bands, :] = sin_w * cosine - cos_w * sine
        w_one[2 * bands + 1 : 2 * bands + 2, :] = level + slope * (base.astype(F32) * (1.0 / total))
        hidden = hidden_units(feats[...], weight_stack(w_one[...]), two_w).astype(BF16)
        width = step // FAR_SETS
        parts = [hidden[:, part * width : (part + 1) * width] for part in range(FAR_SETS)]
        both = dot_t(out_w, jnp.concatenate(parts, axis=0))
        for sub in range(0, step, half_side):
            row_at, half = divmod(sub // half_side, 2)
            coarse = jnp.exp((base + sub).astype(F32) * rate)
            row = index * (step // SIDE) + row_at
            part, lanes = divmod(sub, width)
            raw = (
                both[part * 16 : part * 16 + 8, lanes : lanes + half_side]
                + both[part * 16 + 8 : part * 16 + 16, lanes : lanes + half_side]
            )
            spread[half, pl.ds(row, 8, stride=rows), :] = raw * (coarse * fine + 0.1)
        return carry

    lax.fori_loop(0, begin // step, chunk, 0, unroll=4)
    for slot in range(own):
        for half in range(2):
            far[slot, half] = spread[half, slot * rows : (slot + 1) * rows, :].astype(BF16)


def short(current, taps):
    return (
        taps[0] * pltpu.roll(current, 2, 1)
        + taps[1] * pltpu.roll(current, 1, 1)
        + taps[2] * current
    )


def send_kernel(
    place, pos_hbm, phase_hbm, mix_hbm, mix_phase_hbm, out_hbm, decay_hbm, taps_hbm, query_hbm,
    key_hbm, value_hbm, sent_hbm, pos, phase, mix, mix_phase, out_cols, decay, w_one, taps, query_end,
    key, value, feats, spread, gate_spread, sent, sems,
):
    bands = (pos.shape[0] - 1) // 2
    peers, slots, rows, half_side = sent.shape
    own = (slots - 1) // 3
    chans, tokens = key.shape
    total = peers * tokens
    pairs = [
        (pos_hbm, pos),
        (phase_hbm, phase),
        (mix_hbm, mix),
        (mix_phase_hbm, mix_phase),
        (out_hbm, out_cols),
        (decay_hbm, decay),
        (taps_hbm, taps),
        (query_hbm.at[:, tokens - half_side : tokens], query_end),
        (key_hbm, key),
        (value_hbm, value),
    ]
    copies = [
        pltpu.make_async_copy(source, target, sems.at[at])
        for at, (source, target) in enumerate(pairs)
    ]
    for copy in copies:
        copy.start()
    near = tokens // 2
    base = place[0] * near
    feats[...] = feature_stack(base, bands, near, total)
    for copy in copies[:6]:
        copy.wait()
    two_w = network_weights(pos, phase, mix, mix_phase, w_one)
    out_w = weight_stack(out_cols[...])
    decay_rate = -1.0 / column(decay[...])
    fine = jnp.exp(lax.broadcasted_iota(jnp.int32, (1, half_side), 1).astype(F32) * decay_rate)
    raw = dot_t(out_w, value_stack(hidden_units(feats[...], weight_stack(w_one[...]), two_w)))
    for sub in range(0, near, half_side):
        row_at, half = divmod(sub // half_side, 2)
        coarse = jnp.exp((base + sub).astype(F32) * decay_rate)
        spread[pl.ds(row_at + half * rows // 2, chans, stride=rows), :] = raw[
            :, sub : sub + half_side
        ] * (coarse * fine + 0.1)
    sent[:, 2 * own : 3 * own] = spread[...].reshape(peers, own, rows, half_side).astype(BF16)
    leaving = [
        pltpu.make_async_copy(
            sent.at[:, 2 * own : 3 * own], sent_hbm.at[:, 2 * own : 3 * own], sems.at[len(pairs)]
        )
    ]
    leaving[0].start()
    for copy in copies[6:]:
        copy.wait()
    columns = [[column(taps[which, i : i + 1, :]) for i in range(3)] for which in (1, 2)]
    group = 16
    lane = lax.broadcasted_iota(jnp.int32, (group, half_side), 1)
    ends = jnp.zeros((group, half_side), F32)
    for part in range(chans // group):
        moved = pltpu.roll(
            query_end[part * group : (part + 1) * group, :].astype(F32), 10 + 2 * part, 1
        )
        ends = jnp.where(lane // 2 == 4 + part, moved, ends)
    for part in range(chans // group):
        pick = slice(part * group, (part + 1) * group)
        edge = ends
        for at, (array, tap) in enumerate(((key, columns[0]), (value, columns[1]))):
            zero, one, two = (each[pick, :] for each in tap)
            head = array[pick, 0:half_side].astype(F32)
            last = array[pick, tokens - half_side : tokens].astype(F32)
            started = two * head + jnp.where(lane == 1, one * pltpu.roll(head, 1, 1), 0.0)
            ended = zero * last + jnp.where(
                lane == half_side - 2, one * pltpu.roll(last, half_side - 1, 1), 0.0
            )
            edge = jnp.where(lane // 2 == at, pltpu.roll(started, 2 * at, 1), edge)
            edge = jnp.where(lane // 2 == 2 + at, pltpu.roll(ended, 6 + 2 * at, 1), edge)
        edge = edge.astype(BF16)
        for peer in range(part * group // own, (part + 1) * group // own):
            sent[peer, slots - 1] = edge
    for at in range(0, chans, group):
        pick = slice(at, at + group)
        gated = short(key[pick, :].astype(F32), [tap[pick, :] for tap in columns[0]]) * short(
            value[pick, :].astype(F32), [tap[pick, :] for tap in columns[1]]
        )
        for sub in range(0, tokens, half_side):
            row_at, half = divmod(sub // half_side, 2)
            gate_spread[half, pl.ds(at * rows + row_at, group, stride=rows), :] = gated[
                :, sub : sub + half_side
            ]
        for half in range(2):
            sent[at // own : (at + group) // own, half * own : (half + 1) * own] = (
                gate_spread[half, at * rows : (at + group) * rows, :]
                .reshape(group // own, own, rows, half_side)
                .astype(BF16)
            )
        to = slice(at // own, (at + group) // own)
        leaving.append(
            pltpu.make_async_copy(
                sent.at[to, 0 : 2 * own],
                sent_hbm.at[to, 0 : 2 * own],
                sems.at[len(pairs) + 1 + at // group],
            )
        )
        leaving[-1].start()
    leaving.append(
        pltpu.make_async_copy(
            sent.at[:, slots - 1 : slots], sent_hbm.at[:, slots - 1 : slots], sems.at[len(pairs) + 5]
        )
    )
    leaving[-1].start()
    for copy in leaving:
        copy.wait()


def first_gated(edges, place, own):
    choices = edges.shape[1] // own
    here = jnp.zeros((edges.shape[0], own, edges.shape[2]), F32)
    for choice in range(choices):
        wanted = jnp.broadcast_to(lax.rem(place, choices), here.shape) == choice
        here = jnp.where(wanted, edges[:, choice * own : (choice + 1) * own, :], here)
    before = jnp.concatenate([jnp.zeros_like(here[:1]), here[:-1]], axis=0)
    lanes = here.shape[2]
    shorts = here + pltpu.roll(before, lanes - 4, 2)
    return shorts * pltpu.roll(shorts, lanes - 2, 2)


def conv_kernel(
    place, skip, got, far, left, back, right, twist_re, twist_im, mixed,
):
    side = SIDE
    peers, slots, rows, half_side = got.shape
    own = (slots - 1) // 3
    firsts = first_gated(got[:, slots - 1].astype(F32), place[0], own)
    t_re = twist_re[...]
    t_im = twist_im[...]
    spot = (lax.broadcasted_iota(jnp.int32, (peers, rows, half_side), 1) == 0) & (
        lax.broadcasted_iota(jnp.int32, (peers, rows, half_side), 2) < 2
    )
    group = GROUP
    for at in range(0, own, group):
        data, filt = [], []
        for slot in range(at, at + group):
            head = jnp.where(spot, firsts[:, slot : slot + 1, :], got[:, slot].astype(F32))
            head = head.astype(BF16)
            data.append(
                jnp.concatenate(
                    [head.reshape(side, half_side), got[:, own + slot].reshape(side, half_side)],
                    axis=1,
                )
            )
            near = got[:, 2 * own + slot].astype(F32)
            near = [
                near[:, half * rows // 2 : (half + 1) * rows // 2].reshape(side // 2, half_side)
                for half in range(2)
            ]
            filt.append(
                jnp.concatenate(
                    [
                        jnp.concatenate(near, axis=1).astype(BF16),
                        jnp.concatenate([far[slot, 0], far[slot, 1]], axis=1),
                    ],
                    axis=0,
                )
            )
        both = jnp.concatenate(data + filt, axis=1)
        first = dot(left[...], jnp.concatenate([both, both], axis=0))
        turned = []
        for at_col in range(0, 2 * group * side, side):
            re, im = first[:side, at_col : at_col + side], first[side:, at_col : at_col + side]
            turned.append(
                jnp.concatenate([re * t_re - im * t_im, re * t_im + im * t_re], axis=1).astype(BF16)
            )
        spec = dot(jnp.concatenate(turned, axis=0), right[...])
        edge_row = group * side
        d_re, d_im = spec[:edge_row, :side], spec[:edge_row, side:]
        f_re, f_im = spec[edge_row:, :side], spec[edge_row:, side:]
        product = jnp.concatenate([d_re * f_im + d_im * f_re, d_re * f_re - d_im * f_im], axis=1)
        inner = dot(product.astype(BF16), right[...])
        turned = []
        for at_row in range(0, group * side, side):
            im, re = inner[at_row : at_row + side, :side], inner[at_row : at_row + side, side:]
            turned.append(jnp.concatenate([re * t_re + im * t_im, im * t_re - re * t_im], axis=0))
        high, low = split(jnp.concatenate(turned, axis=1))
        values = dot(back[...], jnp.concatenate([high, low, high], axis=0))
        for index in range(group):
            wide = filt[index].astype(F32)
            energy = jnp.sum(jnp.sum(wide * wide, axis=1, keepdims=True), axis=0, keepdims=True)
            unit = lax.rsqrt(energy + EPSILON) * (1.0 / (side * side))
            lane = lax.broadcasted_iota(jnp.int32, skip.shape, 1)
            here = lane == place[0] * own + at + index
            direct = jnp.sum(jnp.where(here, skip[...], 0.0), axis=1, keepdims=True)
            skipped = direct * data[index].astype(F32)
            result = values[:, index * side : (index + 1) * side] * unit + skipped
            mixed[:, at + index] = result.astype(BF16).reshape(peers, rows, side)


def out_kernel(place, query, taps, got, mixed, gain, gated_out, sums, q_short, spread, total):
    peers, own, rows, side = mixed.shape
    chans = peers * own
    half_side = side // 2
    before = jnp.maximum(place[0] - 1, 0)
    tails = got[before, got.shape[1] - 1].astype(F32)
    tails = jnp.where(jnp.broadcast_to(place[0], tails.shape) > 0, tails, 0.0)
    group = tails.shape[0]
    columns = [column(taps[0, i : i + 1, :]) for i in range(3)]
    for part in range(chans // group):
        pick = slice(part * group, (part + 1) * group)
        tap = [each[pick, :] for each in columns]
        current = query[pick, :].astype(F32)
        q_short[pick, :] = short(current, tap)
        two, one = tails[:, 8 + 2 * part : 9 + 2 * part], tails[:, 9 + 2 * part : 10 + 2 * part]
        q_short[pick, 0:1] = tap[0] * two + tap[1] * one + tap[2] * current[:, 0:1]
        q_short[pick, 1:2] = tap[0] * one + tap[1] * current[:, 0:1] + tap[2] * current[:, 1:2]
    gains = column(gain[...])
    for half in range(2):
        spread[half] = (
            mixed[:, :, :, half * half_side : (half + 1) * half_side]
            .astype(F32)
            .reshape(chans * rows, half_side)
        )
    for at in range(0, q_short.shape[1], half_side):
        row, half = divmod(at // half_side, 2)
        piece = q_short[:, at : at + half_side] * spread[half, pl.ds(row, chans, stride=rows), :]
        gated_out[:, at : at + half_side] = piece * gains
        sum_row, lane = divmod(at, sums.shape[2])
        total[sum_row : sum_row + 1, lane : lane + half_side] = jnp.sum(
            piece * piece, axis=0, keepdims=True
        )
    for peer in range(sums.shape[0]):
        sums[peer] = total[...].astype(BF16)


def scale_kernel(gated_out, sums, result):
    group = result.shape[0]
    width = sums.shape[2]
    energy = jnp.sum(sums[...].astype(F32), axis=0)
    channels = gated_out.shape[0] * sums.shape[0]
    scale = lax.rsqrt(energy / channels + EPSILON)
    begin = pl.multiple_of(pl.program_id(0) * group, group)
    for row in range(sums.shape[1]):
        at = row * width
        piece = gated_out[pl.ds(begin, group), at : at + width]
        result[:, at : at + width] = (piece * scale[row : row + 1, :]).astype(BF16)


def whole(shape, memory_space=None):
    return pl.BlockSpec(shape, lambda *_: (0,) * len(shape), memory_space=memory_space)


SCALAR = pl.BlockSpec(memory_space=pltpu.SMEM)
VECTOR = pl.BlockSpec(memory_space=pltpu.VMEM)
OUTSIDE = pl.BlockSpec(memory_space=pltpu.HBM)


def in_hbm(array):
    return pltpu.with_memory_space_constraint(array, pltpu.HBM)


def params(mebibytes):
    return pltpu.CompilerParams(vmem_limit_bytes=mebibytes * 1024 * 1024)


def shards(
    query_act,
    key_act,
    value_act,
    short_taps,
    pos_proj,
    pos_phase,
    mix_proj,
    mix_phase,
    filter_out,
    decay_len,
    skip_gain,
    out_gain,
):
    chans, tokens = query_act.shape
    peers = lax.axis_size("ctx")
    groups = lax.axis_size("ch")
    place = lax.axis_index("ctx").astype(jnp.int32).reshape(1)
    own = chans // peers
    rows = tokens // SIDE
    units = pos_proj.shape[1]
    half_side = SIDE // 2
    taps = jnp.transpose(short_taps, (0, 2, 1))
    bands = (pos_proj.shape[0] - 1) // 2
    network = [
        pltpu.VMEM(pos_proj.shape, F32),
        pltpu.VMEM((1, units), F32),
        pltpu.VMEM(mix_proj.shape, F32),
        pltpu.VMEM((1, units), F32),
        pltpu.VMEM(filter_out.shape, F32),
        pltpu.VMEM((1, chans), F32),
        pltpu.VMEM((bands * 3, units), F32),
    ]
    weights = [
        in_hbm(array)
        for array in (
            pos_proj, pos_phase[None], mix_proj, mix_phase[None], filter_out, decay_len[None]
        )
    ]
    sent_shape = (peers, 3 * own + 1, rows, half_side)
    sent = pl.pallas_call(
        send_kernel,
        out_shape=jax.ShapeDtypeStruct(sent_shape, BF16),
        in_specs=[SCALAR] + [OUTSIDE] * 10,
        out_specs=OUTSIDE,
        scratch_shapes=network
        + [
            pltpu.VMEM(taps.shape, F32),
            pltpu.VMEM((chans, half_side), BF16),
            pltpu.VMEM((chans, tokens), BF16),
            pltpu.VMEM((chans, tokens), BF16),
            pltpu.VMEM((bands * 9, tokens // 2), BF16),
            pltpu.VMEM((chans * rows, half_side), F32),
            pltpu.VMEM((2, chans * rows, half_side), F32),
            pltpu.VMEM(sent_shape, BF16),
            pltpu.SemaphoreType.DMA((16,)),
        ],
        compiler_params=params(24),
        name="send",
    )(place, *weights, *map(in_hbm, (taps, query_act, key_act, value_act)))
    far_rows = SIDE // 2
    far, gain, skip = pl.pallas_call(
        far_kernel,
        out_shape=(
            jax.ShapeDtypeStruct((own, 2, far_rows, half_side), BF16),
            jax.ShapeDtypeStruct((1, chans), F32),
            jax.ShapeDtypeStruct((1, chans), F32),
        ),
        in_specs=[SCALAR] + [OUTSIDE] * 8,
        out_specs=(VECTOR,) * 3,
        scratch_shapes=network
        + [
            pltpu.VMEM((bands * 9, FAR_STEP), BF16),
            pltpu.VMEM((2, 8 * far_rows, half_side), F32),
            pltpu.SemaphoreType.DMA((8,)),
        ],
        compiler_params=params(16),
        cost_estimate=pl.CostEstimate(
            flops=10_000_000_000, transcendentals=0, bytes_accessed=1_000_000
        ),
        name="far_taps",
    )(place, *weights, in_hbm(out_gain[None]), in_hbm(skip_gain[None]))
    got = lax.all_to_all(sent, "ctx", split_axis=0, concat_axis=0, tiled=True)
    tables = [jnp.asarray(t) for t in transform_tables(SIDE)]
    mixed = pl.pallas_call(
        conv_kernel,
        out_shape=jax.ShapeDtypeStruct((peers, own, rows, SIDE), BF16),
        in_specs=[SCALAR] + [VECTOR] * (3 + len(tables)),
        out_specs=VECTOR,
        compiler_params=params(24),
        name="long_conv",
    )(place, skip, got, far, *tables)
    mixed = lax.all_to_all(mixed, "ctx", split_axis=0, concat_axis=0, tiled=True)
    width = SIDE
    gated_out, sums = pl.pallas_call(
        out_kernel,
        out_shape=(
            jax.ShapeDtypeStruct((chans, tokens), F32),
            jax.ShapeDtypeStruct((groups, tokens // width, width), BF16),
        ),
        in_specs=[SCALAR] + [VECTOR] * 5,
        out_specs=(VECTOR, VECTOR),
        scratch_shapes=[
            pltpu.VMEM((chans, tokens), F32),
            pltpu.VMEM((2, chans * rows, half_side), F32),
            pltpu.VMEM((tokens // width, width), F32),
        ],
        compiler_params=params(16),
        name="gate_out",
    )(place, query_act, taps, got, mixed, gain)
    sums = lax.all_to_all(sums, "ch", split_axis=0, concat_axis=0, tiled=True)
    group = chans // 2
    wide = pl.BlockSpec((group, tokens), lambda i: (i, 0))
    return pl.pallas_call(
        scale_kernel,
        out_shape=jax.ShapeDtypeStruct((chans, tokens), BF16),
        grid=(chans // group,),
        in_specs=[VECTOR, VECTOR],
        out_specs=wide,
        compiler_params=params(16),
        name="norm_out",
    )(gated_out, sums)


def solution(mesh):
    return jax.shard_map(
        shards,
        mesh=mesh,
        in_specs=(
            P("ch", "ctx"),
            P("ch", "ctx"),
            P("ch", "ctx"),
            P(None, "ch", None),
            P(),
            P(),
            P(),
            P(),
            P(None, "ch"),
            P("ch"),
            P("ch"),
            P("ch"),
        ),
        out_specs=P("ch", "ctx"),
        check_vma=False,
    )
```

```python
import math

import ml_dtypes
import numpy as np

import jax
import jax.numpy as jnp
from jax import lax
from jax.experimental import pallas as pl
from jax.experimental.pallas import tpu as pltpu
from jax.sharding import PartitionSpec as P

EPSILON = 1e-06
F32 = jnp.float32
BF16 = jnp.bfloat16
SIDE = 256
GROUP = 2
FAR_STEP = 8192
FAR_SETS = 4
COS_COEFS = (
    -6.283164044920963,
    41.337142429298574,
    -81.34077038150495,
    70.99344453177132,
)


def cos_turns(turns):
    rest = turns - lax.round(turns, lax.RoundingMethod.TO_NEAREST_EVEN)
    quarter = jnp.abs(rest) - 0.25
    square = quarter * quarter
    acc = jnp.full_like(quarter, COS_COEFS[-1])
    for coef in COS_COEFS[-2::-1]:
        acc = acc * square + coef
    return acc * quarter


def split(array):
    high = array.astype(BF16)
    low = (array - high.astype(F32)).astype(BF16)
    return high, low


def dot(lhs, rhs):
    return lax.dot_general(lhs, rhs, (((1,), (0,)), ((), ())), preferred_element_type=F32)


def dot_t(lhs, rhs):
    return lax.dot_general(lhs, rhs, (((0,), (0,)), ((), ())), preferred_element_type=F32)


def weight_stack(weights):
    high, low = split(weights)
    return jnp.concatenate([high, high, low], axis=0)


def value_stack(values):
    high, low = split(values)
    return jnp.concatenate([high, low, high], axis=0)


def column(row):
    size = row.shape[1]
    eye = lax.broadcasted_iota(jnp.int32, (size, size), 0) == lax.broadcasted_iota(
        jnp.int32, (size, size), 1
    )
    return jnp.sum(jnp.where(eye, jnp.broadcast_to(row, (size, size)), 0.0), axis=1, keepdims=True)


def np_split(array):
    high = array.astype(np.float32).astype(ml_dtypes.bfloat16)
    low = (array - high.astype(np.float64)).astype(np.float32).astype(ml_dtypes.bfloat16)
    return high, low


def stacked(array):
    high, low = np_split(array)
    return np.concatenate([high, low], axis=1)


def transform_tables(side):
    total = side * side
    ids = np.arange(side)
    first = np.exp(-2j * np.pi * np.outer(ids - 0.25, ids) / side)
    twist = np.exp(-2j * np.pi * np.outer(ids - 0.25, ids) / total)
    second = np.exp(-2j * np.pi * (np.outer(ids, ids) % side) / side)
    left = np.concatenate([first.real, first.imag], axis=0)
    right = np.block([[second.real, second.imag], [-second.imag, second.real]])
    return (
        stacked(left),
        np.concatenate([np_split(left.T)[0], stacked(left.T)], axis=1),
        np_split(right)[0],
        twist.real.astype(np.float32),
        twist.imag.astype(np.float32),
    )


def feature_stack(base, bands, step, total):
    times = base + lax.broadcasted_iota(jnp.int32, (bands, step), 1)
    row = lax.broadcasted_iota(jnp.int32, (bands, step), 0)
    freqs = jnp.left_shift(jnp.ones((bands, step), jnp.int32), row)
    turns = ((freqs * times) & (total - 1)).astype(F32) * (1.0 / total)
    extra = jnp.where(row == 0, times.astype(F32) * (1.0 / total), jnp.where(row == 1, 1.0, 0.0))
    return value_stack(
        jnp.concatenate([cos_turns(turns), cos_turns(turns - 0.25), extra], axis=0)
    )


def network_weights(pos, phase, mix, mix_phase, w_one):
    bands = (pos.shape[0] - 1) // 2
    inv_turn = 1.0 / (2.0 * math.pi)
    w_one[...] = jnp.zeros_like(w_one)
    w_one[0 : 2 * bands, :] = pos[1 : 2 * bands + 1, :] * inv_turn
    w_one[2 * bands : 2 * bands + 1, :] = pos[0:1, :] * inv_turn
    w_one[2 * bands + 1 : 2 * bands + 2, :] = phase[...] * inv_turn - 0.25
    row = lax.broadcasted_iota(jnp.int32, (bands, w_one.shape[1]), 0)
    high, low = split(mix_phase[...] * inv_turn - 0.25)
    bias = jnp.where(row == 0, high.astype(F32), jnp.where(row == 1, low.astype(F32), 0.0))
    return jnp.concatenate([weight_stack(mix[...] * inv_turn), bias.astype(BF16)], axis=0)


def hidden_units(feats, one_w, two_w):
    hidden = value_stack(cos_turns(dot_t(one_w, feats)))
    ones = jnp.ones((two_w.shape[0] - hidden.shape[0], hidden.shape[1]), BF16)
    return cos_turns(dot_t(two_w, jnp.concatenate([hidden, ones], axis=0)))


def far_kernel(
    place, pos_hbm, phase_hbm, mix_hbm, mix_phase_hbm, out_hbm, decay_hbm, gain_hbm, skip_hbm, far,
    gain, skip, pos, phase, mix, mix_phase, out_cols, decay, w_one, feats, spread, sems,
):
    bands = (pos.shape[0] - 1) // 2
    own, _, rows, half_side = far.shape
    begin = rows * SIDE
    total = 2 * begin
    pairs = [
        (pos_hbm, pos),
        (phase_hbm, phase),
        (mix_hbm, mix),
        (mix_phase_hbm, mix_phase),
        (out_hbm, out_cols),
        (decay_hbm, decay),
        (gain_hbm, gain),
        (skip_hbm, skip),
    ]
    copies = [
        pltpu.make_async_copy(source, target, sems.at[at])
        for at, (source, target) in enumerate(pairs)
    ]
    for copy in copies:
        copy.start()
    step = FAR_STEP
    feats[...] = feature_stack(0, bands, step, total)
    for copy in copies:
        copy.wait()
    two_w = network_weights(pos, phase, mix, mix_phase, w_one)
    cos_w = w_one[0:bands, :]
    sin_w = w_one[bands : 2 * bands, :]
    slope = w_one[2 * bands : 2 * bands + 1, :]
    level = w_one[2 * bands + 1 : 2 * bands + 2, :]
    freqs = jnp.left_shift(
        jnp.ones((bands, 1), jnp.int32), lax.broadcasted_iota(jnp.int32, (bands, 1), 0)
    )
    lane = lax.broadcasted_iota(jnp.int32, out_cols.shape, 1)
    units = out_cols.shape[0]
    narrow = lax.broadcasted_iota(jnp.int32, (units, FAR_SETS * 16), 1)
    tall = lax.broadcasted_iota(jnp.int32, (8, 1), 0)
    cols = jnp.zeros(narrow.shape, F32)
    rate = jnp.zeros(tall.shape, F32)
    decay_rate = -1.0 / decay[...]
    for slot in range(own):
        here = lane == place[0] * own + slot
        col = jnp.sum(jnp.where(here, out_cols[...], 0.0), axis=1, keepdims=True)
        cols = jnp.where(lax.rem(narrow, 8) == slot, col, cols)
        one_rate = jnp.sum(jnp.where(here[0:1, :], decay_rate, 0.0), axis=1, keepdims=True)
        rate = jnp.where(tall == slot, one_rate, rate)
    high, low = split(cols)
    cols = jnp.where(lax.rem(narrow, 16) < 8, high.astype(F32), low.astype(F32))
    out_w = jnp.concatenate(
        [jnp.where(narrow // 16 == part, cols, 0.0) for part in range(FAR_SETS)], axis=0
    ).astype(BF16)
    fine = jnp.exp(lax.broadcasted_iota(jnp.int32, (1, half_side), 1).astype(F32) * rate)
    step = FAR_STEP

    def chunk(index, carry):
        base = begin + index * step
        turns = ((freqs * base) & (total - 1)).astype(F32) * (1.0 / total)
        cosine, sine = cos_turns(turns), cos_turns(turns - 0.25)
        w_one[0:bands, :] = cos_w * cosine + sin_w * sine
        w_one[bands : 2 * bands, :] = sin_w * cosine - cos_w * sine
        w_one[2 * bands + 1 : 2 * bands + 2, :] = level + slope * (base.astype(F32) * (1.0 / total))
        hidden = hidden_units(feats[...], weight_stack(w_one[...]), two_w).astype(BF16)
        width = step // FAR_SETS
        parts = [hidden[:, part * width : (part + 1) * width] for part in range(FAR_SETS)]
        both = dot_t(out_w, jnp.concatenate(parts, axis=0))
        for sub in range(0, step, half_side):
            row_at, half = divmod(sub // half_side, 2)
            coarse = jnp.exp((base + sub).astype(F32) * rate)
            row = index * (step // SIDE) + row_at
            part, lanes = divmod(sub, width)
            raw = (
                both[part * 16 : part * 16 + 8, lanes : lanes + half_side]
                + both[part * 16 + 8 : part * 16 + 16, lanes : lanes + half_side]
            )
            spread[half, pl.ds(row, 8, stride=rows), :] = raw * (coarse * fine + 0.1)
        return carry

    lax.fori_loop(0, begin // step, chunk, 0, unroll=2)
    for slot in range(own):
        for half in range(2):
            far[slot, half] = spread[half, slot * rows : (slot + 1) * rows, :].astype(BF16)


def short(current, taps):
    return (
        taps[0] * pltpu.roll(current, 2, 1)
        + taps[1] * pltpu.roll(current, 1, 1)
        + taps[2] * current
    )


def send_kernel(
    place, pos_hbm, phase_hbm, mix_hbm, mix_phase_hbm, out_hbm, decay_hbm, taps_hbm, query_hbm,
    key_hbm, value_hbm, sent_hbm, pos, phase, mix, mix_phase, out_cols, decay, w_one, taps, query_end,
    key, value, feats, spread, gate_spread, sent, sems,
):
    bands = (pos.shape[0] - 1) // 2
    peers, slots, rows, half_side = sent.shape
    own = (slots - 1) // 3
    chans, tokens = key.shape
    total = peers * tokens
    pairs = [
        (pos_hbm, pos),
        (phase_hbm, phase),
        (mix_hbm, mix),
        (mix_phase_hbm, mix_phase),
        (out_hbm, out_cols),
        (decay_hbm, decay),
        (taps_hbm, taps),
        (query_hbm.at[:, tokens - half_side : tokens], query_end),
        (key_hbm, key),
        (value_hbm, value),
    ]
    copies = [
        pltpu.make_async_copy(source, target, sems.at[at])
        for at, (source, target) in enumerate(pairs)
    ]
    for copy in copies:
        copy.start()
    near = tokens // 2
    base = place[0] * near
    feats[...] = feature_stack(base, bands, near, total)
    for copy in copies[:6]:
        copy.wait()
    two_w = network_weights(pos, phase, mix, mix_phase, w_one)
    out_w = weight_stack(out_cols[...])
    decay_rate = -1.0 / column(decay[...])
    fine = jnp.exp(lax.broadcasted_iota(jnp.int32, (1, half_side), 1).astype(F32) * decay_rate)
    starts = base + half_side * lax.broadcasted_iota(jnp.int32, (1, half_side), 1)
    coarse = jnp.exp(starts.astype(F32) * decay_rate)
    raw = dot_t(out_w, value_stack(hidden_units(feats[...], weight_stack(w_one[...]), two_w)))
    for sub in range(0, near, half_side):
        row_at, half = divmod(sub // half_side, 2)
        at = sub // half_side
        spread[pl.ds(row_at + half * rows // 2, chans, stride=rows), :] = raw[
            :, sub : sub + half_side
        ] * (coarse[:, at : at + 1] * fine + 0.1)
    sent[:, 2 * own : 3 * own] = spread[...].reshape(peers, own, rows, half_side).astype(BF16)
    leaving = [
        pltpu.make_async_copy(
            sent.at[:, 2 * own : 3 * own], sent_hbm.at[:, 2 * own : 3 * own], sems.at[len(pairs)]
        )
    ]
    leaving[0].start()
    for copy in copies[6:]:
        copy.wait()
    columns = [[column(taps[which, i : i + 1, :]) for i in range(3)] for which in (1, 2)]
    group = 16
    lane = lax.broadcasted_iota(jnp.int32, (group, half_side), 1)
    ends = jnp.zeros((group, half_side), F32)
    for part in range(chans // group):
        moved = pltpu.roll(
            query_end[part * group : (part + 1) * group, :].astype(F32), 10 + 2 * part, 1
        )
        ends = jnp.where(lane // 2 == 4 + part, moved, ends)
    for part in range(chans // group):
        pick = slice(part * group, (part + 1) * group)
        edge = ends
        for at, (array, tap) in enumerate(((key, columns[0]), (value, columns[1]))):
            zero, one, two = (each[pick, :] for each in tap)
            head = array[pick, 0:half_side].astype(F32)
            last = array[pick, tokens - half_side : tokens].astype(F32)
            started = two * head + jnp.where(lane == 1, one * pltpu.roll(head, 1, 1), 0.0)
            ended = zero * last + jnp.where(
                lane == half_side - 2, one * pltpu.roll(last, half_side - 1, 1), 0.0
            )
            edge = jnp.where(lane // 2 == at, pltpu.roll(started, 2 * at, 1), edge)
            edge = jnp.where(lane // 2 == 2 + at, pltpu.roll(ended, 6 + 2 * at, 1), edge)
        edge = edge.astype(BF16)
        for peer in range(part * group // own, (part + 1) * group // own):
            sent[peer, slots - 1] = edge
    for at in range(0, chans, group):
        pick = slice(at, at + group)
        gated = short(key[pick, :].astype(F32), [tap[pick, :] for tap in columns[0]]) * short(
            value[pick, :].astype(F32), [tap[pick, :] for tap in columns[1]]
        )
        for sub in range(0, tokens, half_side):
            row_at, half = divmod(sub // half_side, 2)
            gate_spread[half, pl.ds(at * rows + row_at, group, stride=rows), :] = gated[
                :, sub : sub + half_side
            ]
        for half in range(2):
            sent[at // own : (at + group) // own, half * own : (half + 1) * own] = (
                gate_spread[half, at * rows : (at + group) * rows, :]
                .reshape(group // own, own, rows, half_side)
                .astype(BF16)
            )
        to = slice(at // own, (at + group) // own)
        leaving.append(
            pltpu.make_async_copy(
                sent.at[to, 0 : 2 * own],
                sent_hbm.at[to, 0 : 2 * own],
                sems.at[len(pairs) + 1 + at // group],
            )
        )
        leaving[-1].start()
    leaving.append(
        pltpu.make_async_copy(
            sent.at[:, slots - 1 : slots], sent_hbm.at[:, slots - 1 : slots], sems.at[len(pairs) + 5]
        )
    )
    leaving[-1].start()
    for copy in leaving:
        copy.wait()


def first_gated(edges, place, own):
    choices = edges.shape[1] // own
    here = jnp.zeros((edges.shape[0], own, edges.shape[2]), F32)
    for choice in range(choices):
        wanted = jnp.broadcast_to(lax.rem(place, choices), here.shape) == choice
        here = jnp.where(wanted, edges[:, choice * own : (choice + 1) * own, :], here)
    before = jnp.concatenate([jnp.zeros_like(here[:1]), here[:-1]], axis=0)
    lanes = here.shape[2]
    shorts = here + pltpu.roll(before, lanes - 4, 2)
    return shorts * pltpu.roll(shorts, lanes - 2, 2)


def conv_kernel(
    place, skip, got, far, left, back, right, twist_re, twist_im, mixed,
):
    side = SIDE
    peers, slots, rows, half_side = got.shape
    own = (slots - 1) // 3
    firsts = first_gated(got[:, slots - 1].astype(F32), place[0], own)
    t_re = twist_re[...]
    t_im = twist_im[...]
    spot = (lax.broadcasted_iota(jnp.int32, (peers, rows, half_side), 1) == 0) & (
        lax.broadcasted_iota(jnp.int32, (peers, rows, half_side), 2) < 2
    )
    group = GROUP
    for at in range(0, own, group):
        data, filt = [], []
        for slot in range(at, at + group):
            head = jnp.where(spot, firsts[:, slot : slot + 1, :], got[:, slot].astype(F32))
            head = head.astype(BF16)
            data.append(
                jnp.concatenate(
                    [head.reshape(side, half_side), got[:, own + slot].reshape(side, half_side)],
                    axis=1,
                )
            )
            near = got[:, 2 * own + slot].astype(F32)
            near = [
                near[:, half * rows // 2 : (half + 1) * rows // 2].reshape(side // 2, half_side)
                for half in range(2)
            ]
            filt.append(
                jnp.concatenate(
                    [
                        jnp.concatenate(near, axis=1).astype(BF16),
                        jnp.concatenate([far[slot, 0], far[slot, 1]], axis=1),
                    ],
                    axis=0,
                )
            )
        both = jnp.concatenate(data + filt, axis=1)
        first = dot(left[...], jnp.concatenate([both, both], axis=0))
        turned = []
        for at_col in range(0, 2 * group * side, side):
            re, im = first[:side, at_col : at_col + side], first[side:, at_col : at_col + side]
            turned.append(
                jnp.concatenate([re * t_re - im * t_im, re * t_im + im * t_re], axis=1).astype(BF16)
            )
        spec = dot(jnp.concatenate(turned, axis=0), right[...])
        edge_row = group * side
        d_re, d_im = spec[:edge_row, :side], spec[:edge_row, side:]
        f_re, f_im = spec[edge_row:, :side], spec[edge_row:, side:]
        product = jnp.concatenate([d_re * f_im + d_im * f_re, d_re * f_re - d_im * f_im], axis=1)
        inner = dot(product.astype(BF16), right[...])
        turned = []
        for at_row in range(0, group * side, side):
            im, re = inner[at_row : at_row + side, :side], inner[at_row : at_row + side, side:]
            turned.append(jnp.concatenate([re * t_re + im * t_im, im * t_re - re * t_im], axis=0))
        high, low = split(jnp.concatenate(turned, axis=1))
        values = dot(back[...], jnp.concatenate([high, low, high], axis=0))
        for index in range(group):
            wide = filt[index].astype(F32)
            energy = jnp.sum(jnp.sum(wide * wide, axis=1, keepdims=True), axis=0, keepdims=True)
            unit = lax.rsqrt(energy + EPSILON) * (1.0 / (side * side))
            lane = lax.broadcasted_iota(jnp.int32, skip.shape, 1)
            here = lane == place[0] * own + at + index
            direct = jnp.sum(jnp.where(here, skip[...], 0.0), axis=1, keepdims=True)
            skipped = direct * data[index].astype(F32)
            result = values[:, index * side : (index + 1) * side] * unit + skipped
            mixed[:, at + index] = result.astype(BF16).reshape(peers, rows, side)


def out_kernel(place, query, taps, got, mixed, gain, gated_out, sums, q_short, spread, total):
    peers, own, rows, side = mixed.shape
    chans = peers * own
    half_side = side // 2
    before = jnp.maximum(place[0] - 1, 0)
    tails = got[before, got.shape[1] - 1].astype(F32)
    tails = jnp.where(jnp.broadcast_to(place[0], tails.shape) > 0, tails, 0.0)
    group = tails.shape[0]
    columns = [column(taps[0, i : i + 1, :]) for i in range(3)]
    for part in range(chans // group):
        pick = slice(part * group, (part + 1) * group)
        tap = [each[pick, :] for each in columns]
        current = query[pick, :].astype(F32)
        q_short[pick, :] = short(current, tap)
        two, one = tails[:, 8 + 2 * part : 9 + 2 * part], tails[:, 9 + 2 * part : 10 + 2 * part]
        q_short[pick, 0:1] = tap[0] * two + tap[1] * one + tap[2] * current[:, 0:1]
        q_short[pick, 1:2] = tap[0] * one + tap[1] * current[:, 0:1] + tap[2] * current[:, 1:2]
    gains = column(gain[...])
    for half in range(2):
        spread[half] = (
            mixed[:, :, :, half * half_side : (half + 1) * half_side]
            .astype(F32)
            .reshape(chans * rows, half_side)
        )
    for at in range(0, q_short.shape[1], half_side):
        row, half = divmod(at // half_side, 2)
        piece = q_short[:, at : at + half_side] * spread[half, pl.ds(row, chans, stride=rows), :]
        gated_out[:, at : at + half_side] = piece * gains
        sum_row, lane = divmod(at, sums.shape[2])
        total[sum_row : sum_row + 1, lane : lane + half_side] = jnp.sum(
            piece * piece, axis=0, keepdims=True
        )
    for peer in range(sums.shape[0]):
        sums[peer] = total[...].astype(BF16)


def scale_kernel(gated_out, sums, result):
    group = result.shape[0]
    width = sums.shape[2]
    energy = jnp.sum(sums[...].astype(F32), axis=0)
    channels = gated_out.shape[0] * sums.shape[0]
    scale = lax.rsqrt(energy / channels + EPSILON)
    begin = pl.multiple_of(pl.program_id(0) * group, group)
    for row in range(sums.shape[1]):
        at = row * width
        piece = gated_out[pl.ds(begin, group), at : at + width]
        result[:, at : at + width] = (piece * scale[row : row + 1, :]).astype(BF16)


def whole(shape, memory_space=None):
    return pl.BlockSpec(shape, lambda *_: (0,) * len(shape), memory_space=memory_space)


SCALAR = pl.BlockSpec(memory_space=pltpu.SMEM)
VECTOR = pl.BlockSpec(memory_space=pltpu.VMEM)
OUTSIDE = pl.BlockSpec(memory_space=pltpu.HBM)


def in_hbm(array):
    return pltpu.with_memory_space_constraint(array, pltpu.HBM)


def params(mebibytes):
    return pltpu.CompilerParams(vmem_limit_bytes=mebibytes * 1024 * 1024)


def shards(
    query_act,
    key_act,
    value_act,
    short_taps,
    pos_proj,
    pos_phase,
    mix_proj,
    mix_phase,
    filter_out,
    decay_len,
    skip_gain,
    out_gain,
):
    chans, tokens = query_act.shape
    peers = lax.axis_size("ctx")
    groups = lax.axis_size("ch")
    place = lax.axis_index("ctx").astype(jnp.int32).reshape(1)
    own = chans // peers
    rows = tokens // SIDE
    units = pos_proj.shape[1]
    half_side = SIDE // 2
    taps = jnp.transpose(short_taps, (0, 2, 1))
    bands = (pos_proj.shape[0] - 1) // 2
    network = [
        pltpu.VMEM(pos_proj.shape, F32),
        pltpu.VMEM((1, units), F32),
        pltpu.VMEM(mix_proj.shape, F32),
        pltpu.VMEM((1, units), F32),
        pltpu.VMEM(filter_out.shape, F32),
        pltpu.VMEM((1, chans), F32),
        pltpu.VMEM((bands * 3, units), F32),
    ]
    weights = [
        in_hbm(array)
        for array in (
            pos_proj, pos_phase[None], mix_proj, mix_phase[None], filter_out, decay_len[None]
        )
    ]
    sent_shape = (peers, 3 * own + 1, rows, half_side)
    sent = pl.pallas_call(
        send_kernel,
        out_shape=jax.ShapeDtypeStruct(sent_shape, BF16),
        in_specs=[SCALAR] + [OUTSIDE] * 10,
        out_specs=OUTSIDE,
        scratch_shapes=network
        + [
            pltpu.VMEM(taps.shape, F32),
            pltpu.VMEM((chans, half_side), BF16),
            pltpu.VMEM((chans, tokens), BF16),
            pltpu.VMEM((chans, tokens), BF16),
            pltpu.VMEM((bands * 9, tokens // 2), BF16),
            pltpu.VMEM((chans * rows, half_side), F32),
            pltpu.VMEM((2, chans * rows, half_side), F32),
            pltpu.VMEM(sent_shape, BF16),
            pltpu.SemaphoreType.DMA((16,)),
        ],
        compiler_params=params(24),
        name="send",
    )(place, *weights, *map(in_hbm, (taps, query_act, key_act, value_act)))
    far_rows = SIDE // 2
    far, gain, skip = pl.pallas_call(
        far_kernel,
        out_shape=(
            jax.ShapeDtypeStruct((own, 2, far_rows, half_side), BF16),
            jax.ShapeDtypeStruct((1, chans), F32),
            jax.ShapeDtypeStruct((1, chans), F32),
        ),
        in_specs=[SCALAR] + [OUTSIDE] * 8,
        out_specs=(VECTOR,) * 3,
        scratch_shapes=network
        + [
            pltpu.VMEM((bands * 9, FAR_STEP), BF16),
            pltpu.VMEM((2, 8 * far_rows, half_side), F32),
            pltpu.SemaphoreType.DMA((8,)),
        ],
        compiler_params=params(16),
        cost_estimate=pl.CostEstimate(
            flops=10_000_000_000, transcendentals=0, bytes_accessed=1_000_000
        ),
        name="far_taps",
    )(place, *weights, in_hbm(out_gain[None]), in_hbm(skip_gain[None]))
    got = lax.all_to_all(sent, "ctx", split_axis=0, concat_axis=0, tiled=True)
    tables = [jnp.asarray(t) for t in transform_tables(SIDE)]
    mixed = pl.pallas_call(
        conv_kernel,
        out_shape=jax.ShapeDtypeStruct((peers, own, rows, SIDE), BF16),
        in_specs=[SCALAR] + [VECTOR] * (3 + len(tables)),
        out_specs=VECTOR,
        compiler_params=params(24),
        name="long_conv",
    )(place, skip, got, far, *tables)
    mixed = lax.all_to_all(mixed, "ctx", split_axis=0, concat_axis=0, tiled=True)
    width = SIDE
    gated_out, sums = pl.pallas_call(
        out_kernel,
        out_shape=(
            jax.ShapeDtypeStruct((chans, tokens), F32),
            jax.ShapeDtypeStruct((groups, tokens // width, width), BF16),
        ),
        in_specs=[SCALAR] + [VECTOR] * 5,
        out_specs=(VECTOR, VECTOR),
        scratch_shapes=[
            pltpu.VMEM((chans, tokens), F32),
            pltpu.VMEM((2, chans * rows, half_side), F32),
            pltpu.VMEM((tokens // width, width), F32),
        ],
        compiler_params=params(16),
        name="gate_out",
    )(place, query_act, taps, got, mixed, gain)
    sums = lax.all_to_all(sums, "ch", split_axis=0, concat_axis=0, tiled=True)
    group = chans // 2
    wide = pl.BlockSpec((group, tokens), lambda i: (i, 0))
    return pl.pallas_call(
        scale_kernel,
        out_shape=jax.ShapeDtypeStruct((chans, tokens), BF16),
        grid=(chans // group,),
        in_specs=[VECTOR, VECTOR],
        out_specs=wide,
        compiler_params=params(16),
        name="norm_out",
    )(gated_out, sums)


def solution(mesh):
    return jax.shard_map(
        shards,
        mesh=mesh,
        in_specs=(
            P("ch", "ctx"),
            P("ch", "ctx"),
            P("ch", "ctx"),
            P(None, "ch", None),
            P(),
            P(),
            P(),
            P(),
            P(None, "ch"),
            P("ch"),
            P("ch"),
            P("ch"),
        ),
        out_specs=P("ch", "ctx"),
        check_vma=False,
    )
```

```python
import math

import ml_dtypes
import numpy as np

import jax
import jax.numpy as jnp
from jax import lax
from jax.experimental import pallas as pl
from jax.experimental.pallas import tpu as pltpu
from jax.sharding import PartitionSpec as P

EPSILON = 1e-06
F32 = jnp.float32
BF16 = jnp.bfloat16
SIDE = 256
GROUP = 2
FAR_STEP = 8192
FAR_SETS = 4
COS_COEFS = (
    -6.283164044920963,
    41.337142429298574,
    -81.34077038150495,
    70.99344453177132,
)


def cos_turns(turns):
    rest = turns - lax.round(turns, lax.RoundingMethod.TO_NEAREST_EVEN)
    quarter = jnp.abs(rest) - 0.25
    square = quarter * quarter
    acc = jnp.full_like(quarter, COS_COEFS[-1])
    for coef in COS_COEFS[-2::-1]:
        acc = acc * square + coef
    return acc * quarter


def split(array):
    high = array.astype(BF16)
    low = (array - high.astype(F32)).astype(BF16)
    return high, low


def dot(lhs, rhs):
    return lax.dot_general(lhs, rhs, (((1,), (0,)), ((), ())), preferred_element_type=F32)


def dot_t(lhs, rhs):
    return lax.dot_general(lhs, rhs, (((0,), (0,)), ((), ())), preferred_element_type=F32)


def weight_stack(weights):
    high, low = split(weights)
    return jnp.concatenate([high, high, low], axis=0)


def value_stack(values):
    high, low = split(values)
    return jnp.concatenate([high, low, high], axis=0)


def column(row):
    size = row.shape[1]
    eye = lax.broadcasted_iota(jnp.int32, (size, size), 0) == lax.broadcasted_iota(
        jnp.int32, (size, size), 1
    )
    return jnp.sum(jnp.where(eye, jnp.broadcast_to(row, (size, size)), 0.0), axis=1, keepdims=True)


def np_split(array):
    high = array.astype(np.float32).astype(ml_dtypes.bfloat16)
    low = (array - high.astype(np.float64)).astype(np.float32).astype(ml_dtypes.bfloat16)
    return high, low


def stacked(array):
    high, low = np_split(array)
    return np.concatenate([high, low], axis=1)


def transform_tables(side):
    total = side * side
    ids = np.arange(side)
    first = np.exp(-2j * np.pi * np.outer(ids - 0.25, ids) / side)
    twist = np.exp(-2j * np.pi * np.outer(ids - 0.25, ids) / total)
    second = np.exp(-2j * np.pi * (np.outer(ids, ids) % side) / side)
    left = np.concatenate([first.real, first.imag], axis=0)
    right = np.block([[second.real, second.imag], [-second.imag, second.real]])
    return (
        stacked(left),
        np.concatenate([np_split(left.T)[0], stacked(left.T)], axis=1),
        np_split(right)[0],
        twist.real.astype(np.float32),
        twist.imag.astype(np.float32),
    )


def feature_stack(base, bands, step, total):
    times = base + lax.broadcasted_iota(jnp.int32, (bands, step), 1)
    row = lax.broadcasted_iota(jnp.int32, (bands, step), 0)
    freqs = jnp.left_shift(jnp.ones((bands, step), jnp.int32), row)
    turns = ((freqs * times) & (total - 1)).astype(F32) * (1.0 / total)
    extra = jnp.where(row == 0, times.astype(F32) * (1.0 / total), jnp.where(row == 1, 1.0, 0.0))
    return value_stack(
        jnp.concatenate([cos_turns(turns), cos_turns(turns - 0.25), extra], axis=0)
    )


def network_weights(pos, phase, mix, mix_phase, w_one):
    bands = (pos.shape[0] - 1) // 2
    inv_turn = 1.0 / (2.0 * math.pi)
    w_one[...] = jnp.zeros_like(w_one)
    w_one[0 : 2 * bands, :] = pos[1 : 2 * bands + 1, :] * inv_turn
    w_one[2 * bands : 2 * bands + 1, :] = pos[0:1, :] * inv_turn
    w_one[2 * bands + 1 : 2 * bands + 2, :] = phase[...] * inv_turn - 0.25
    row = lax.broadcasted_iota(jnp.int32, (bands, w_one.shape[1]), 0)
    high, low = split(mix_phase[...] * inv_turn - 0.25)
    bias = jnp.where(row == 0, high.astype(F32), jnp.where(row == 1, low.astype(F32), 0.0))
    return jnp.concatenate([weight_stack(mix[...] * inv_turn), bias.astype(BF16)], axis=0)


def hidden_units(feats, one_w, two_w):
    hidden = value_stack(cos_turns(dot_t(one_w, feats)))
    ones = jnp.ones((two_w.shape[0] - hidden.shape[0], hidden.shape[1]), BF16)
    return cos_turns(dot_t(two_w, jnp.concatenate([hidden, ones], axis=0)))


def far_kernel(
    place, pos_hbm, phase_hbm, mix_hbm, mix_phase_hbm, out_hbm, decay_hbm, gain_hbm, skip_hbm, far,
    gain, skip, pos, phase, mix, mix_phase, out_cols, decay, w_one, feats, spread, sems,
):
    bands = (pos.shape[0] - 1) // 2
    own, _, rows, half_side = far.shape
    begin = rows * SIDE
    total = 2 * begin
    pairs = [
        (pos_hbm, pos),
        (phase_hbm, phase),
        (mix_hbm, mix),
        (mix_phase_hbm, mix_phase),
        (out_hbm, out_cols),
        (decay_hbm, decay),
        (gain_hbm, gain),
        (skip_hbm, skip),
    ]
    copies = [
        pltpu.make_async_copy(source, target, sems.at[at])
        for at, (source, target) in enumerate(pairs)
    ]
    for copy in copies:
        copy.start()
    step = FAR_STEP
    feats[...] = feature_stack(0, bands, step, total)
    for copy in copies:
        copy.wait()
    two_w = network_weights(pos, phase, mix, mix_phase, w_one)
    cos_w = w_one[0:bands, :]
    sin_w = w_one[bands : 2 * bands, :]
    slope = w_one[2 * bands : 2 * bands + 1, :]
    level = w_one[2 * bands + 1 : 2 * bands + 2, :]
    freqs = jnp.left_shift(
        jnp.ones((bands, 1), jnp.int32), lax.broadcasted_iota(jnp.int32, (bands, 1), 0)
    )
    lane = lax.broadcasted_iota(jnp.int32, out_cols.shape, 1)
    units = out_cols.shape[0]
    narrow = lax.broadcasted_iota(jnp.int32, (units, FAR_SETS * 16), 1)
    tall = lax.broadcasted_iota(jnp.int32, (8, 1), 0)
    cols = jnp.zeros(narrow.shape, F32)
    rate = jnp.zeros(tall.shape, F32)
    decay_rate = -1.0 / decay[...]
    for slot in range(own):
        here = lane == place[0] * own + slot
        col = jnp.sum(jnp.where(here, out_cols[...], 0.0), axis=1, keepdims=True)
        cols = jnp.where(lax.rem(narrow, 8) == slot, col, cols)
        one_rate = jnp.sum(jnp.where(here[0:1, :], decay_rate, 0.0), axis=1, keepdims=True)
        rate = jnp.where(tall == slot, one_rate, rate)
    high, low = split(cols)
    cols = jnp.where(lax.rem(narrow, 16) < 8, high.astype(F32), low.astype(F32))
    out_w = jnp.concatenate(
        [jnp.where(narrow // 16 == part, cols, 0.0) for part in range(FAR_SETS)], axis=0
    ).astype(BF16)
    fine = jnp.exp(lax.broadcasted_iota(jnp.int32, (1, half_side), 1).astype(F32) * rate)
    step = FAR_STEP

    def chunk(index, carry):
        base = begin + index * step
        turns = ((freqs * base) & (total - 1)).astype(F32) * (1.0 / total)
        cosine, sine = cos_turns(turns), cos_turns(turns - 0.25)
        w_one[0:bands, :] = cos_w * cosine + sin_w * sine
        w_one[bands : 2 * bands, :] = sin_w * cosine - cos_w * sine
        w_one[2 * bands + 1 : 2 * bands + 2, :] = level + slope * (base.astype(F32) * (1.0 / total))
        hidden = hidden_units(feats[...], weight_stack(w_one[...]), two_w).astype(BF16)
        width = step // FAR_SETS
        parts = [hidden[:, part * width : (part + 1) * width] for part in range(FAR_SETS)]
        both = dot_t(out_w, jnp.concatenate(parts, axis=0))
        starts = base + half_side * lax.broadcasted_iota(jnp.int32, (1, half_side), 1)
        coarse = jnp.exp(starts.astype(F32) * rate)
        for sub in range(0, step, half_side):
            row_at, half = divmod(sub // half_side, 2)
            at = sub // half_side
            row = index * (step // SIDE) + row_at
            part, lanes = divmod(sub, width)
            raw = (
                both[part * 16 : part * 16 + 8, lanes : lanes + half_side]
                + both[part * 16 + 8 : part * 16 + 16, lanes : lanes + half_side]
            )
            spread[half, pl.ds(row, 8, stride=rows), :] = raw * (coarse[:, at : at + 1] * fine + 0.1)
        return carry

    lax.fori_loop(0, begin // step, chunk, 0, unroll=2)
    for slot in range(own):
        for half in range(2):
            far[slot, half] = spread[half, slot * rows : (slot + 1) * rows, :].astype(BF16)


def short(current, taps):
    return (
        taps[0] * pltpu.roll(current, 2, 1)
        + taps[1] * pltpu.roll(current, 1, 1)
        + taps[2] * current
    )


def send_kernel(
    place, pos_hbm, phase_hbm, mix_hbm, mix_phase_hbm, out_hbm, decay_hbm, taps_hbm, query_hbm,
    key_hbm, value_hbm, sent_hbm, pos, phase, mix, mix_phase, out_cols, decay, w_one, taps, query_end,
    key, value, feats, spread, gate_spread, sent, sems,
):
    bands = (pos.shape[0] - 1) // 2
    peers, slots, rows, half_side = sent.shape
    own = (slots - 1) // 3
    chans, tokens = key.shape
    total = peers * tokens
    pairs = [
        (pos_hbm, pos),
        (phase_hbm, phase),
        (mix_hbm, mix),
        (mix_phase_hbm, mix_phase),
        (out_hbm, out_cols),
        (decay_hbm, decay),
        (taps_hbm, taps),
        (query_hbm.at[:, tokens - half_side : tokens], query_end),
        (key_hbm, key),
        (value_hbm, value),
    ]
    copies = [
        pltpu.make_async_copy(source, target, sems.at[at])
        for at, (source, target) in enumerate(pairs)
    ]
    for copy in copies:
        copy.start()
    near = tokens // 2
    base = place[0] * near
    feats[...] = feature_stack(base, bands, near, total)
    for copy in copies[:6]:
        copy.wait()
    two_w = network_weights(pos, phase, mix, mix_phase, w_one)
    out_w = weight_stack(out_cols[...])
    decay_rate = -1.0 / column(decay[...])
    fine = jnp.exp(lax.broadcasted_iota(jnp.int32, (1, half_side), 1).astype(F32) * decay_rate)
    starts = base + half_side * lax.broadcasted_iota(jnp.int32, (1, half_side), 1)
    coarse = jnp.exp(starts.astype(F32) * decay_rate)
    raw = dot_t(out_w, value_stack(hidden_units(feats[...], weight_stack(w_one[...]), two_w)))
    for sub in range(0, near, half_side):
        row_at, half = divmod(sub // half_side, 2)
        at = sub // half_side
        spread[pl.ds(row_at + half * rows // 2, chans, stride=rows), :] = raw[
            :, sub : sub + half_side
        ] * (coarse[:, at : at + 1] * fine + 0.1)
    sent[:, 2 * own : 3 * own] = spread[...].reshape(peers, own, rows, half_side).astype(BF16)
    leaving = [
        pltpu.make_async_copy(
            sent.at[:, 2 * own : 3 * own], sent_hbm.at[:, 2 * own : 3 * own], sems.at[len(pairs)]
        )
    ]
    leaving[0].start()
    for copy in copies[6:]:
        copy.wait()
    columns = [[column(taps[which, i : i + 1, :]) for i in range(3)] for which in (1, 2)]
    group = 16
    lane = lax.broadcasted_iota(jnp.int32, (group, half_side), 1)
    ends = jnp.zeros((group, half_side), F32)
    for part in range(chans // group):
        moved = pltpu.roll(
            query_end[part * group : (part + 1) * group, :].astype(F32), 10 + 2 * part, 1
        )
        ends = jnp.where(lane // 2 == 4 + part, moved, ends)
    for part in range(chans // group):
        pick = slice(part * group, (part + 1) * group)
        edge = ends
        for at, (array, tap) in enumerate(((key, columns[0]), (value, columns[1]))):
            zero, one, two = (each[pick, :] for each in tap)
            head = array[pick, 0:half_side].astype(F32)
            last = array[pick, tokens - half_side : tokens].astype(F32)
            started = two * head + jnp.where(lane == 1, one * pltpu.roll(head, 1, 1), 0.0)
            ended = zero * last + jnp.where(
                lane == half_side - 2, one * pltpu.roll(last, half_side - 1, 1), 0.0
            )
            edge = jnp.where(lane // 2 == at, pltpu.roll(started, 2 * at, 1), edge)
            edge = jnp.where(lane // 2 == 2 + at, pltpu.roll(ended, 6 + 2 * at, 1), edge)
        edge = edge.astype(BF16)
        for peer in range(part * group // own, (part + 1) * group // own):
            sent[peer, slots - 1] = edge
    for at in range(0, chans, group):
        pick = slice(at, at + group)
        gated = short(key[pick, :].astype(F32), [tap[pick, :] for tap in columns[0]]) * short(
            value[pick, :].astype(F32), [tap[pick, :] for tap in columns[1]]
        )
        for sub in range(0, tokens, half_side):
            row_at, half = divmod(sub // half_side, 2)
            gate_spread[half, pl.ds(at * rows + row_at, group, stride=rows), :] = gated[
                :, sub : sub + half_side
            ]
        for half in range(2):
            sent[at // own : (at + group) // own, half * own : (half + 1) * own] = (
                gate_spread[half, at * rows : (at + group) * rows, :]
                .reshape(group // own, own, rows, half_side)
                .astype(BF16)
            )
        to = slice(at // own, (at + group) // own)
        leaving.append(
            pltpu.make_async_copy(
                sent.at[to, 0 : 2 * own],
                sent_hbm.at[to, 0 : 2 * own],
                sems.at[len(pairs) + 1 + at // group],
            )
        )
        leaving[-1].start()
    leaving.append(
        pltpu.make_async_copy(
            sent.at[:, slots - 1 : slots], sent_hbm.at[:, slots - 1 : slots], sems.at[len(pairs) + 5]
        )
    )
    leaving[-1].start()
    for copy in leaving:
        copy.wait()


def first_gated(edges, place, own):
    choices = edges.shape[1] // own
    here = jnp.zeros((edges.shape[0], own, edges.shape[2]), F32)
    for choice in range(choices):
        wanted = jnp.broadcast_to(lax.rem(place, choices), here.shape) == choice
        here = jnp.where(wanted, edges[:, choice * own : (choice + 1) * own, :], here)
    before = jnp.concatenate([jnp.zeros_like(here[:1]), here[:-1]], axis=0)
    lanes = here.shape[2]
    shorts = here + pltpu.roll(before, lanes - 4, 2)
    return shorts * pltpu.roll(shorts, lanes - 2, 2)


def conv_kernel(
    place, skip, got, far, left, back, right, twist_re, twist_im, mixed,
):
    side = SIDE
    peers, slots, rows, half_side = got.shape
    own = (slots - 1) // 3
    firsts = first_gated(got[:, slots - 1].astype(F32), place[0], own)
    t_re = twist_re[...]
    t_im = twist_im[...]
    spot = (lax.broadcasted_iota(jnp.int32, (peers, rows, half_side), 1) == 0) & (
        lax.broadcasted_iota(jnp.int32, (peers, rows, half_side), 2) < 2
    )
    group = GROUP
    for at in range(0, own, group):
        data, filt = [], []
        for slot in range(at, at + group):
            head = jnp.where(spot, firsts[:, slot : slot + 1, :], got[:, slot].astype(F32))
            head = head.astype(BF16)
            data.append(
                jnp.concatenate(
                    [head.reshape(side, half_side), got[:, own + slot].reshape(side, half_side)],
                    axis=1,
                )
            )
            near = got[:, 2 * own + slot].astype(F32)
            near = [
                near[:, half * rows // 2 : (half + 1) * rows // 2].reshape(side // 2, half_side)
                for half in range(2)
            ]
            filt.append(
                jnp.concatenate(
                    [
                        jnp.concatenate(near, axis=1).astype(BF16),
                        jnp.concatenate([far[slot, 0], far[slot, 1]], axis=1),
                    ],
                    axis=0,
                )
            )
        both = jnp.concatenate(data + filt, axis=1)
        first = dot(left[...], jnp.concatenate([both, both], axis=0))
        turned = []
        for at_col in range(0, 2 * group * side, side):
            re, im = first[:side, at_col : at_col + side], first[side:, at_col : at_col + side]
            turned.append(
                jnp.concatenate([re * t_re - im * t_im, re * t_im + im * t_re], axis=1).astype(BF16)
            )
        spec = dot(jnp.concatenate(turned, axis=0), right[...])
        edge_row = group * side
        d_re, d_im = spec[:edge_row, :side], spec[:edge_row, side:]
        f_re, f_im = spec[edge_row:, :side], spec[edge_row:, side:]
        product = jnp.concatenate([d_re * f_im + d_im * f_re, d_re * f_re - d_im * f_im], axis=1)
        inner = dot(product.astype(BF16), right[...])
        turned = []
        for at_row in range(0, group * side, side):
            im, re = inner[at_row : at_row + side, :side], inner[at_row : at_row + side, side:]
            turned.append(jnp.concatenate([re * t_re + im * t_im, im * t_re - re * t_im], axis=0))
        high, low = split(jnp.concatenate(turned, axis=1))
        values = dot(back[...], jnp.concatenate([high, low, high], axis=0))
        for index in range(group):
            wide = filt[index].astype(F32)
            energy = jnp.sum(jnp.sum(wide * wide, axis=1, keepdims=True), axis=0, keepdims=True)
            unit = lax.rsqrt(energy + EPSILON) * (1.0 / (side * side))
            lane = lax.broadcasted_iota(jnp.int32, skip.shape, 1)
            here = lane == place[0] * own + at + index
            direct = jnp.sum(jnp.where(here, skip[...], 0.0), axis=1, keepdims=True)
            skipped = direct * data[index].astype(F32)
            result = values[:, index * side : (index + 1) * side] * unit + skipped
            mixed[:, at + index] = result.astype(BF16).reshape(peers, rows, side)


def out_kernel(place, query, taps, got, mixed, gain, gated_out, sums, q_short, spread, total):
    peers, own, rows, side = mixed.shape
    chans = peers * own
    half_side = side // 2
    before = jnp.maximum(place[0] - 1, 0)
    tails = got[before, got.shape[1] - 1].astype(F32)
    tails = jnp.where(jnp.broadcast_to(place[0], tails.shape) > 0, tails, 0.0)
    group = tails.shape[0]
    columns = [column(taps[0, i : i + 1, :]) for i in range(3)]
    for part in range(chans // group):
        pick = slice(part * group, (part + 1) * group)
        tap = [each[pick, :] for each in columns]
        current = query[pick, :].astype(F32)
        q_short[pick, :] = short(current, tap)
        two, one = tails[:, 8 + 2 * part : 9 + 2 * part], tails[:, 9 + 2 * part : 10 + 2 * part]
        q_short[pick, 0:1] = tap[0] * two + tap[1] * one + tap[2] * current[:, 0:1]
        q_short[pick, 1:2] = tap[0] * one + tap[1] * current[:, 0:1] + tap[2] * current[:, 1:2]
    gains = column(gain[...])
    for half in range(2):
        spread[half] = (
            mixed[:, :, :, half * half_side : (half + 1) * half_side]
            .astype(F32)
            .reshape(chans * rows, half_side)
        )
    for at in range(0, q_short.shape[1], half_side):
        row, half = divmod(at // half_side, 2)
        piece = q_short[:, at : at + half_side] * spread[half, pl.ds(row, chans, stride=rows), :]
        gated_out[:, at : at + half_side] = piece * gains
        sum_row, lane = divmod(at, sums.shape[2])
        total[sum_row : sum_row + 1, lane : lane + half_side] = jnp.sum(
            piece * piece, axis=0, keepdims=True
        )
    for peer in range(sums.shape[0]):
        sums[peer] = total[...].astype(BF16)


def scale_kernel(gated_out, sums, result):
    group = result.shape[0]
    width = sums.shape[2]
    energy = jnp.sum(sums[...].astype(F32), axis=0)
    channels = gated_out.shape[0] * sums.shape[0]
    scale = lax.rsqrt(energy / channels + EPSILON)
    begin = pl.multiple_of(pl.program_id(0) * group, group)
    for row in range(sums.shape[1]):
        at = row * width
        piece = gated_out[pl.ds(begin, group), at : at + width]
        result[:, at : at + width] = (piece * scale[row : row + 1, :]).astype(BF16)


def whole(shape, memory_space=None):
    return pl.BlockSpec(shape, lambda *_: (0,) * len(shape), memory_space=memory_space)


SCALAR = pl.BlockSpec(memory_space=pltpu.SMEM)
VECTOR = pl.BlockSpec(memory_space=pltpu.VMEM)
OUTSIDE = pl.BlockSpec(memory_space=pltpu.HBM)


def in_hbm(array):
    return pltpu.with_memory_space_constraint(array, pltpu.HBM)


def params(mebibytes):
    return pltpu.CompilerParams(vmem_limit_bytes=mebibytes * 1024 * 1024)


def shards(
    query_act,
    key_act,
    value_act,
    short_taps,
    pos_proj,
    pos_phase,
    mix_proj,
    mix_phase,
    filter_out,
    decay_len,
    skip_gain,
    out_gain,
):
    chans, tokens = query_act.shape
    peers = lax.axis_size("ctx")
    groups = lax.axis_size("ch")
    place = lax.axis_index("ctx").astype(jnp.int32).reshape(1)
    own = chans // peers
    rows = tokens // SIDE
    units = pos_proj.shape[1]
    half_side = SIDE // 2
    taps = jnp.transpose(short_taps, (0, 2, 1))
    bands = (pos_proj.shape[0] - 1) // 2
    network = [
        pltpu.VMEM(pos_proj.shape, F32),
        pltpu.VMEM((1, units), F32),
        pltpu.VMEM(mix_proj.shape, F32),
        pltpu.VMEM((1, units), F32),
        pltpu.VMEM(filter_out.shape, F32),
        pltpu.VMEM((1, chans), F32),
        pltpu.VMEM((bands * 3, units), F32),
    ]
    weights = [
        in_hbm(array)
        for array in (
            pos_proj, pos_phase[None], mix_proj, mix_phase[None], filter_out, decay_len[None]
        )
    ]
    sent_shape = (peers, 3 * own + 1, rows, half_side)
    sent = pl.pallas_call(
        send_kernel,
        out_shape=jax.ShapeDtypeStruct(sent_shape, BF16),
        in_specs=[SCALAR] + [OUTSIDE] * 10,
        out_specs=OUTSIDE,
        scratch_shapes=network
        + [
            pltpu.VMEM(taps.shape, F32),
            pltpu.VMEM((chans, half_side), BF16),
            pltpu.VMEM((chans, tokens), BF16),
            pltpu.VMEM((chans, tokens), BF16),
            pltpu.VMEM((bands * 9, tokens // 2), BF16),
            pltpu.VMEM((chans * rows, half_side), F32),
            pltpu.VMEM((2, chans * rows, half_side), F32),
            pltpu.VMEM(sent_shape, BF16),
            pltpu.SemaphoreType.DMA((16,)),
        ],
        compiler_params=params(24),
        name="send",
    )(place, *weights, *map(in_hbm, (taps, query_act, key_act, value_act)))
    far_rows = SIDE // 2
    far, gain, skip = pl.pallas_call(
        far_kernel,
        out_shape=(
            jax.ShapeDtypeStruct((own, 2, far_rows, half_side), BF16),
            jax.ShapeDtypeStruct((1, chans), F32),
            jax.ShapeDtypeStruct((1, chans), F32),
        ),
        in_specs=[SCALAR] + [OUTSIDE] * 8,
        out_specs=(VECTOR,) * 3,
        scratch_shapes=network
        + [
            pltpu.VMEM((bands * 9, FAR_STEP), BF16),
            pltpu.VMEM((2, 8 * far_rows, half_side), F32),
            pltpu.SemaphoreType.DMA((8,)),
        ],
        compiler_params=params(16),
        cost_estimate=pl.CostEstimate(
            flops=10_000_000_000, transcendentals=0, bytes_accessed=1_000_000
        ),
        name="far_taps",
    )(place, *weights, in_hbm(out_gain[None]), in_hbm(skip_gain[None]))
    got = lax.all_to_all(sent, "ctx", split_axis=0, concat_axis=0, tiled=True)
    tables = [jnp.asarray(t) for t in transform_tables(SIDE)]
    mixed = pl.pallas_call(
        conv_kernel,
        out_shape=jax.ShapeDtypeStruct((peers, own, rows, SIDE), BF16),
        in_specs=[SCALAR] + [VECTOR] * (3 + len(tables)),
        out_specs=VECTOR,
        compiler_params=params(24),
        name="long_conv",
    )(place, skip, got, far, *tables)
    mixed = lax.all_to_all(mixed, "ctx", split_axis=0, concat_axis=0, tiled=True)
    width = SIDE
    gated_out, sums = pl.pallas_call(
        out_kernel,
        out_shape=(
            jax.ShapeDtypeStruct((chans, tokens), F32),
            jax.ShapeDtypeStruct((groups, tokens // width, width), BF16),
        ),
        in_specs=[SCALAR] + [VECTOR] * 5,
        out_specs=(VECTOR, VECTOR),
        scratch_shapes=[
            pltpu.VMEM((chans, tokens), F32),
            pltpu.VMEM((2, chans * rows, half_side), F32),
            pltpu.VMEM((tokens // width, width), F32),
        ],
        compiler_params=params(16),
        name="gate_out",
    )(place, query_act, taps, got, mixed, gain)
    sums = lax.all_to_all(sums, "ch", split_axis=0, concat_axis=0, tiled=True)
    group = chans // 2
    wide = pl.BlockSpec((group, tokens), lambda i: (i, 0))
    return pl.pallas_call(
        scale_kernel,
        out_shape=jax.ShapeDtypeStruct((chans, tokens), BF16),
        grid=(chans // group,),
        in_specs=[VECTOR, VECTOR],
        out_specs=wide,
        compiler_params=params(16),
        name="norm_out",
    )(gated_out, sums)


def solution(mesh):
    return jax.shard_map(
        shards,
        mesh=mesh,
        in_specs=(
            P("ch", "ctx"),
            P("ch", "ctx"),
            P("ch", "ctx"),
            P(None, "ch", None),
            P(),
            P(),
            P(),
            P(),
            P(None, "ch"),
            P("ch"),
            P("ch"),
            P("ch"),
        ),
        out_specs=P("ch", "ctx"),
        check_vma=False,
    )
```
